32 devices in a mesh: gx: 4 (over z), gy: 2 (over y), gz: 4 (over x, core).
Axes of the slice: x: 2, y: 2, z: 4, core: 2. Of those that a mesh axis runs over, the one named last changes fastest.
Arguments:
- positions: float32 [3, 131072], P(None, ('gx', 'gy', 'gz'))
- velocities: float32 [3, 131072], P(None, ('gx', 'gy', 'gz')), may hold values from -6 to 6
- forces_old: float32 [3, 131072], P(None, ('gx', 'gy', 'gz')), may hold values from -6 to 6
- inv_mass: float32 [131072], P(('gx', 'gy', 'gz')), may hold values from 0.25 to 4
- charges: float32 [131072], P(('gx', 'gy', 'gz')), may hold values from -3 to 3
- block_species: int32 [1024], P(('gx', 'gy', 'gz')), may hold values from 0 to 3
- sigma_table: float32 [4], replicated, may hold values from 0.25 to 0.5
- epsilon_table: float32 [4], replicated, may hold values from 0.02 to 0.2
- tower_index: int32 [32, 64], P(('gx', 'gy', 'gz')), may hold values from 0 to 127
- plate_index: int32 [32, 64], P(('gx', 'gy', 'gz')), may hold values from 0 to 287
- tile_counts: int32 [32], P(('gx', 'gy', 'gz')), may hold values from 1 to 64, as said below
- exclusions: int32 [32, 64, 16, 128], P(('gx', 'gy', 'gz')), may hold values from 0 to 255, as said below
- mig_block: int32 [32, 4], P(('gx', 'gy', 'gz')), may hold values from 0 to 31, as said below
- mig_dest: int32 [32, 4], P(('gx', 'gy', 'gz')), may hold values from 0 to 8, as said below
Outputs:
- positions_new: float32 [3, 131072], P(None, ('gx', 'gy', 'gz'))
- velocities_new: float32 [3, 131072], P(None, ('gx', 'gy', 'gz'))
- forces_new: float32 [3, 131072], P(None, ('gx', 'gy', 'gz'))
- arrivals: float32 [6, 32, 8, 512], P(None, ('gx', 'gy', 'gz'))
The draws below stay inside these ranges and needn't reach their ends.
Inputs may be any that keep to these rules, and one draw needn't show every extreme that they name: `tile_counts`: at most 64 for every box, and exactly 64 for some box; slots at or after a box's count carry no weight. `exclusions`: each of the low eight bits marks one excluded atom pair. `mig_block`: the 4 entries of one box are distinct. `mig_dest`: never 4.
All inputs are finite; a program needn't handle non-finite values.
Results may differ from the reference program's by a relative error of at most 0.0003.
Values sent between devices are 32-bit elements; how exact they have to be, the bound alone decides.
A program may use at most 64 MiB of HBM per device.

```python
import math
import jax
import jax.numpy as jnp
from jax import lax

TILE = 128
WORDS = 16
BLOCKS = 32
PAIRS = 64
MIG = 4
KINDS = 4
ATOMS = 131072
N_GX = 4
N_GY = 2
N_GZ = 4
DEVICES = 32


def draw_positions(key, part):
    atoms_box = BLOCKS * TILE
    atom_ids = jnp.arange(atoms_box * DEVICES, dtype=jnp.int32)
    box_ids = atom_ids // atoms_box
    coord_x = (box_ids // (N_GY * N_GZ)).astype(jnp.float32)
    coord_y = (box_ids // N_GZ % N_GY).astype(jnp.float32)
    coord_z = (box_ids % N_GZ).astype(jnp.float32)
    spread = jax.random.uniform(key, (3, atoms_box * DEVICES), jnp.float32)
    layer_height = 1.0 / N_GZ
    return jnp.stack([coord_x + spread[0], coord_y + spread[1], (coord_z + spread[2]) * layer_height], axis=0).astype(jnp.float32)


def draw_tile_counts(key, part):
    first_key, second_key, third_key = jax.random.split(jax.random.fold_in(key, 11), 3)
    left = jax.random.randint(first_key, (DEVICES,), 1, PAIRS + 1)
    right = jax.random.randint(second_key, (DEVICES,), 1, PAIRS + 1)
    counted = jnp.maximum(left * right // PAIRS, 1)
    busiest = jax.random.randint(third_key, (), 0, DEVICES)
    counted = jnp.where(jnp.arange(DEVICES) == busiest, PAIRS, counted)
    return counted.astype(jnp.int32)


def draw_exclusions(key, part):
    first_key, second_key = jax.random.split(jax.random.fold_in(key, 23), 2)
    shape_full = (DEVICES, PAIRS, WORDS, TILE)
    first_bits = jax.random.randint(first_key, shape_full, 0, 256, dtype=jnp.int32)
    second_bits = jax.random.randint(second_key, shape_full, 0, 256, dtype=jnp.int32)
    return jnp.bitwise_and(first_bits, second_bits).astype(jnp.int32)


def draw_mig_block(key, part):
    row_keys = jax.random.split(jax.random.fold_in(key, 37), DEVICES)
    orders = jax.vmap(lambda row_key: jax.random.permutation(row_key, BLOCKS))(row_keys)
    return orders[:, :MIG].astype(jnp.int32)


def draw_mig_dest(key, part):
    picked = jax.random.randint(jax.random.fold_in(key, 41), (DEVICES, MIG), 0, 8)
    return (picked + (picked >= 4).astype(picked.dtype)).astype(jnp.int32)


def plant(values, own_key, least, high):
    dims = values.shape
    place = [jax.random.randint(jax.random.fold_in(own_key, axis), (), 0, dims[axis]) for axis in range(len(dims))]
    values = values.at[tuple(place)].set(least)
    longest = dims.index(max(dims))
    place[longest] = (place[longest] + 1) % dims[longest]
    return values.at[tuple(place)].set(high)


def steps_of(rng, extent, cuts, least, top_value):
    factor_of = 1.0
    for position, blocks in cuts:
        heights = jax.random.uniform(jax.random.fold_in(jax.random.fold_in(rng, 6), position), (blocks,), jnp.float32, least / len(cuts), top_value / len(cuts))
        factor_of = factor_of * jnp.repeat(jnp.exp(heights), extent[position] // blocks).reshape((-1,) + (1,) * (len(extent) - 1 - position))
    return factor_of


def normal_values(key, dims, scale, reach, shards=(), kind=jnp.bfloat16):
    drawn = jax.random.normal(key, dims, jnp.float32) * scale
    if len(shards) > 0:
        drawn = steps_of(key, dims, shards, -0.22, 0.18) * drawn
    return jnp.clip(drawn, min=-reach, max=reach).astype(kind)


def setup_inputs(seed: int = 0) -> dict:
    splits = jax.random.split(jax.random.key(seed), 15)
    return {
        "positions": draw_positions(jax.random.fold_in(splits[14], 71), 0),
        "velocities": normal_values(splits[1], (3, ATOMS), 1.0, 6.0, ((1, 32),), jnp.float32),
        "forces_old": normal_values(splits[2], (3, ATOMS), 1.0, 6.0, ((1, 32),), jnp.float32),
        "inv_mass": jnp.clip(jnp.exp(math.log(4.0) - 2.7725887 * jax.random.uniform(splits[3], (ATOMS,), jnp.float32) ** steps_of(splits[3], (ATOMS,), ((0, 32),), -0.2, 0.2)), 0.25, 4.0),
        "charges": normal_values(splits[4], (ATOMS,), 0.5, 3.0, ((0, 32),), jnp.float32),
        "block_species": plant(jax.random.randint(splits[5], (DEVICES * BLOCKS,), 0, KINDS), jax.random.fold_in(splits[5], 1), 0, KINDS - 1).astype(jnp.int32),
        "sigma_table": jnp.clip(jnp.exp(jax.random.uniform(splits[6], (KINDS,), jnp.float32, math.log(0.25), math.log(0.5))), 0.25, 0.5),
        "epsilon_table": jnp.clip(jnp.exp(jax.random.uniform(splits[7], (KINDS,), jnp.float32, math.log(0.02), math.log(0.2))), 0.02, 0.2),
        "tower_index": plant(jax.random.randint(splits[8], (DEVICES, PAIRS), 0, N_GZ * BLOCKS), jax.random.fold_in(splits[8], 1), 0, (N_GZ * BLOCKS) - 1).astype(jnp.int32),
        "plate_index": plant(jax.random.randint(splits[9], (DEVICES, PAIRS), 0, 9 * BLOCKS), jax.random.fold_in(splits[9], 1), 0, (9 * BLOCKS) - 1).astype(jnp.int32),
        "tile_counts": draw_tile_counts(jax.random.fold_in(splits[14], 71), 0),
        "exclusions": draw_exclusions(jax.random.fold_in(splits[14], 71), 0),
        "mig_block": draw_mig_block(jax.random.fold_in(splits[14], 71), 0),
        "mig_dest": draw_mig_dest(jax.random.fold_in(splits[14], 71), 0),
    }


time_step = 0.2
soft_core = 0.09
cutoff_sq = 1.44
coulomb_k = 0.5

def tile_terms(tower_rows, plate_rows, mask_words, length_x, length_y):
    tile_width = tower_rows.shape[1]
    raw = tower_rows[0:3, :, None] - plate_rows[0:3, None, :]
    image_x = raw[0] - length_x * jnp.floor(raw[0] / length_x + 0.5)
    image_y = raw[1] - length_y * jnp.floor(raw[1] / length_y + 0.5)
    offsets = jnp.stack([image_x, image_y, raw[2]], axis=0)
    distance_sq = lax.optimization_barrier(jnp.sum(offsets * offsets, axis=0))
    inverse = 1.0 / (distance_sq + soft_core)
    sigma_pair = 0.5 * (tower_rows[4][:, None] + plate_rows[4][None, :])
    ratio_pair = sigma_pair * sigma_pair * inverse
    ratio_cube = ratio_pair * ratio_pair * ratio_pair
    depth_pair = tower_rows[5][:, None] * plate_rows[5][None, :]
    charge_term = coulomb_k * tower_rows[3][:, None] * plate_rows[3][None, :] * jnp.sqrt(inverse)
    falloff = 1.0 - distance_sq / cutoff_sq
    switch = jnp.where(distance_sq < cutoff_sq, falloff * falloff, 0.0)
    spread = jnp.repeat(mask_words.T, 8, axis=1)
    shifts = jnp.arange(tile_width, dtype=jnp.int32) % 8
    excluded = jnp.bitwise_and(jnp.right_shift(spread, shifts[None, :]), 1)
    kept_pairs = (1 - excluded).astype(jnp.float32)
    strength = (depth_pair * (12.0 * ratio_cube * ratio_cube - 6.0 * ratio_cube) + charge_term) * inverse * switch * kept_pairs
    weighted = strength[None] * offsets
    return (lax.optimization_barrier(jnp.sum(weighted, axis=2)), -lax.optimization_barrier(jnp.sum(weighted, axis=1)))

def box_number(coord_x, coord_y, coord_z):
    return (coord_x * N_GY + coord_y) * N_GZ + coord_z

def reference(positions, velocities, forces_old, inv_mass, charges, block_species, sigma_table, epsilon_table, tower_index, plate_index, tile_counts, exclusions, mig_block, mig_dest):
    half_kick = velocities + 0.5 * time_step * forces_old * inv_mass[None, :]
    moved = positions + time_step * half_kick
    sigma_atom = jnp.repeat(sigma_table[block_species], TILE)
    depth_atom = jnp.repeat(jnp.sqrt(epsilon_table)[block_species], TILE)
    features = jnp.concatenate([moved, charges[None, :], sigma_atom[None, :], depth_atom[None, :]], axis=0)
    block_rows = features.reshape(6, DEVICES * BLOCKS, TILE)
    pair_slots = jnp.arange(PAIRS, dtype=jnp.int32)
    length_x = float(N_GX)
    length_y = float(N_GY)

    def pair_terms(tower_rows, plate_rows, mask_words):
        return tile_terms(tower_rows, plate_rows, mask_words, length_x, length_y)

    def one_box(totals, inputs):
        box_index, tower_list, plate_list, pair_count, mask_list = inputs
        coord_x = box_index // (N_GY * N_GZ)
        coord_y = box_index // N_GZ % N_GY
        coord_z = box_index % N_GZ
        tower_ids = box_number(coord_x, coord_y, tower_list // BLOCKS) * BLOCKS + tower_list % BLOCKS
        neighbour = plate_list // BLOCKS
        plate_ids = box_number((coord_x + neighbour // 3 - 1) % N_GX, (coord_y + neighbour % 3 - 1) % N_GY, coord_z) * BLOCKS + plate_list % BLOCKS
        tower_tiles = jnp.take(block_rows, tower_ids, axis=1)
        plate_tiles = jnp.take(block_rows, plate_ids, axis=1)
        on_tower, on_plate = jax.vmap(pair_terms, in_axes=(1, 1, 0), out_axes=1)(tower_tiles, plate_tiles, mask_list)
        listed = (pair_slots < pair_count).astype(jnp.float32)[None, :, None]
        totals = totals.at[:, tower_ids].add(on_tower * listed)
        totals = totals.at[:, plate_ids].add(on_plate * listed)
        return (totals, None)
    boxes = jnp.arange(DEVICES, dtype=jnp.int32)
    start = jnp.zeros((3, DEVICES * BLOCKS, TILE), jnp.float32)
    totals = lax.scan(one_box, start, (boxes, tower_index, plate_index, tile_counts, exclusions))[0]
    forces_new = totals.reshape(3, DEVICES * BLOCKS * TILE)
    velocity_full = half_kick + 0.5 * time_step * forces_new * inv_mass[None, :]
    departed = jnp.zeros((DEVICES, BLOCKS), jnp.float32).at[boxes[:, None], mig_block].set(1.0)
    staying = jnp.repeat((1.0 - departed).reshape(-1), TILE)[None, :]
    positions_new = moved * staying
    velocities_new = velocity_full * staying
    state = jnp.concatenate([moved, velocity_full], axis=0).reshape(6, DEVICES * BLOCKS, TILE)
    shift_x = jnp.array([-1, -1, -1, 0, 0, 1, 1, 1], dtype=jnp.int32)
    shift_y = jnp.array([-1, 0, 1, -1, 1, -1, 0, 1], dtype=jnp.int32)
    coord_x = boxes // (N_GY * N_GZ)
    coord_y = boxes // N_GZ % N_GY
    coord_z = boxes % N_GZ
    sources = box_number((coord_x[:, None] + shift_x[None, :]) % N_GX, (coord_y[:, None] + shift_y[None, :]) % N_GY, coord_z[:, None])
    source_ids = sources[:, :, None] * BLOCKS + mig_block[sources]
    wanted = (mig_dest[sources] == ((1 - shift_x) * 3 + (1 - shift_y))[None, :, None]).astype(jnp.float32)
    picked = jnp.take(state, source_ids.reshape(-1), axis=1).reshape(6, DEVICES, 8, MIG, TILE)
    arrivals = (picked * wanted[None, :, :, :, None]).reshape(6, DEVICES, 8, MIG * TILE)
    return (positions_new, velocities_new, forces_new, arrivals)
```

```python
import functools
import jax
import jax.numpy as jnp
from jax import lax
from jax.experimental import pallas as pl
from jax.experimental.pallas import tpu as pltpu
from jax.sharding import PartitionSpec as P

time_step = 0.2
soft_core = 0.09
cutoff_sq = 1.44
coulomb_k = 0.5
MESH = pl.DeviceIdType.MESH
UNROLL = 4
HALVES = 2
TERMS = 16
source_offsets = ((-1, -1), (-1, 0), (-1, 1), (0, -1), (0, 1), (1, -1), (1, 0), (1, 1))


class Slots:
    def __init__(self, nx, ny, nz):
        self.nx, self.ny, self.nz = nx, ny, nz
        self.offsets = [(0, 0, 0)] + [(0, 0, k) for k in range(1, nz)]
        self.cell = {(0, 0): 0}
        for da in range(-1, 2):
            for db in range(-1, 2):
                key = (da % nx, db % ny)
                if key not in self.cell:
                    self.cell[key] = len(self.offsets)
                    self.offsets.append((key[0], key[1], 0))
        self.count = len(self.offsets)
        self.cells = 1 + self.count - nz

    def cell_slot(self, da, db):
        return self.cell[(da % self.nx, db % self.ny)]

    def cell_number(self, slot):
        return slot - self.nz + 1 if slot else 0

    def opposite(self, slot):
        dx, dy, dz = self.offsets[slot]
        if dz:
            return (self.nz - dz) % self.nz
        return self.cell_slot(-dx, -dy)

    def device(self, slot):
        dx, dy, dz = self.offsets[slot]
        return (
            lax.rem(lax.axis_index("gx") + dx, self.nx),
            lax.rem(lax.axis_index("gy") + dy, self.ny),
            lax.rem(lax.axis_index("gz") + dz, self.nz),
        )


def split3(value):
    high = value.astype(jnp.bfloat16).astype(jnp.float32)
    rest = value - high
    mid = rest.astype(jnp.bfloat16).astype(jnp.float32)
    return high, mid, rest - mid


def step_kernel(
    slots, blocks,
    pos_h, vel_h, fold_h, mass_h, charge_h, species_h, sigma_h, eps_h, tower_h, plate_h, counts_h, excl_h,
    mig_block_h, mig_dest_h,
    force, arrived,
    pos, vel, fold, mass, charge, species, sigma_s, eps_s, tower, plate, tower_v, plate_v, counts, excl,
    mig_block, mig_dest,
    half_b, moved_b, mass_b, dense, tow, near0, near1, allowed, rep_tab, att_tab, towers, plates, right, left0, left1,
    made_a, made_b, tower_sum, plate_sum0, plate_sum1, out_t, out_p0, out_p1, land_t, land_p0, land_p1, outgoing,
    cell_table, local_sem,
    tow_s, tow_r, n0_s, n0_r, n1_s, n1_r, rt_s, rt_r, r0_s, r0_r, r1_s, r1_r, mg_s, mg_r,
):
    atoms = pos.shape[1]
    width = atoms // blocks
    pairs = tower.shape[1]
    words = excl.shape[2]
    part = width // HALVES
    nx, ny, nz, cells = slots.nx, slots.ny, slots.nz, slots.cells
    lx, ly = float(nx), float(ny)
    lengths = (lx, ly, lx)
    f32 = jnp.float32
    bf16 = jnp.bfloat16
    near = (near0, near1)
    left = (left0, left1)
    plate_sum = (plate_sum0, plate_sum1)
    out_p = (out_p0, out_p1)
    land_p = (land_p0, land_p1)
    ratio = (ly / lx) ** 2
    shift_h = soft_core / (lx * lx)
    edge = (cutoff_sq + soft_core) / (lx * lx)
    scale = lx * lx / (cutoff_sq * cutoff_sq)

    barrier = pltpu.get_barrier_semaphore()
    for s in range(1, slots.count):
        pl.semaphore_signal(barrier, inc=1, device_id=slots.device(s), device_id_type=MESH)
    fetches = []
    for src, dst in (
        (pos_h, pos), (vel_h, vel), (fold_h, fold), (mass_h, mass), (charge_h, charge), (species_h, species),
        (sigma_h, sigma_s), (eps_h, eps_s), (excl_h, excl), (tower_h, tower), (plate_h, plate),
        (tower_h, tower_v), (plate_h, plate_v), (counts_h, counts), (mig_block_h, mig_block), (mig_dest_h, mig_dest),
    ):
        copy = pltpu.make_async_copy(src, dst, local_sem.at[len(fetches)])
        copy.start()
        fetches.append(copy)
    for o in range(9):
        cell_table[o] = slots.cell_number(slots.cell_slot(o // 3 - 1, o % 3 - 1))
    for copy in fetches[:8]:
        copy.wait()

    half = vel[...] + 0.5 * time_step * fold[...] * mass[...]
    moved = pos[...] + time_step * half
    row3 = lax.broadcasted_iota(jnp.int32, (3, atoms), 0)
    scaled = moved * jnp.where(row3 == 1, f32(1.0 / ly), f32(1.0 / lx))
    tower_charge = charge[...] * (coulomb_k * scale / lx)
    for b in range(blocks):
        at = slice(b * width, (b + 1) * width)
        tow[0, b, 0:3, :] = scaled[:, at]
        tow[0, b, 3:4, :] = tower_charge[:, at]
        for r in range(3):
            dense[r * blocks + b : r * blocks + b + 1, :] = scaled[r : r + 1, at]
        dense[3 * blocks + b : 3 * blocks + b + 1, :] = charge[:, at]
    which = species[...]
    sigma = jnp.zeros((1, blocks), f32)
    eps = jnp.zeros((1, blocks), f32)
    for k in range(sigma_s.shape[0]):
        sigma = jnp.where(which == k, sigma_s[k], sigma)
        eps = jnp.where(which == k, eps_s[k], eps)
    depth_row = jnp.sqrt(eps)
    tow[0, blocks] = jnp.zeros((4, width), f32)
    tow[0, blocks, 0:1, 0:blocks] = sigma
    tow[0, blocks, 1:2, 0:blocks] = depth_row
    near0[0, 2 * blocks : 2 * blocks + 8, :] = jnp.zeros((8, width), f32)
    near0[0, 2 * blocks : 2 * blocks + 1, 0:blocks] = sigma
    near0[0, 2 * blocks + 1 : 2 * blocks + 2, 0:blocks] = depth_row
    low = lax.broadcasted_iota(jnp.int32, (blocks, width), 1) < part
    comp = [dense[r * blocks : (r + 1) * blocks, :] for r in range(4)]
    turned = [pltpu.roll(v, part, 1) for v in comp]
    near0[0, 0:blocks, :] = jnp.where(low, comp[0], turned[1])
    near0[0, blocks : 2 * blocks, :] = jnp.where(low, comp[2], turned[3])
    near1[0, 0:blocks, :] = jnp.where(low, turned[0], comp[1])
    near1[0, blocks : 2 * blocks, :] = jnp.where(low, turned[2], comp[3])

    pl.semaphore_wait(barrier, slots.count - 1)

    def send(src, dst, ss, rs, s):
        copy = pltpu.make_async_remote_copy(
            src_ref=src, dst_ref=dst, send_sem=ss, recv_sem=rs, device_id=slots.device(s), device_id_type=MESH
        )
        copy.start()
        return copy

    def send_cells(source, landing, ss, rs):
        copies = []
        for s in range(nz, slots.count):
            here, there = slots.cell_number(s), slots.cell_number(slots.opposite(s))
            copies.append(send(source(here), landing.at[there], ss.at[here], rs.at[there], s))
        return copies

    first = send_cells(lambda c: near0.at[0], near0, n0_s, n0_r)
    for s in range(1, nz):
        there = slots.opposite(s)
        first.append(send(tow.at[0], tow.at[there], tow_s.at[s], tow_r.at[there], s))
    second = send_cells(lambda c: near1.at[0], near1, n1_s, n1_r)

    bit = jnp.left_shift(1, lax.broadcasted_iota(jnp.int32, (8, width), 0))
    group = lax.broadcasted_iota(jnp.int32, (TERMS, 4 * width), 1) // width
    term = lax.broadcasted_iota(jnp.int32, (TERMS, 4 * width), 0)
    plain = jnp.where(((group == 0) | (group == 2)) & (term < 3), -1.0, 0.0)
    plain = jnp.where((group == 1) & (term >= 3) & (term < 6), -1.0, plain)
    term1 = lax.broadcasted_iota(jnp.int32, (TERMS, width), 0)
    ones = jnp.where((term1 >= 9) & (term1 < 12), 1.0, 0.0)
    for copy in fetches[8:]:
        copy.wait()

    def expand(k, carry):
        for w in range(words):
            hit = excl[0, k, w : w + 1, :] & bit
            allowed[pl.ds(pl.multiple_of(k * width + w * 8, 8), 8), :] = jnp.where(hit == 0, edge, -1.0)
        at = pl.ds(pl.multiple_of(k * TERMS, TERMS), TERMS)
        for g in range(4):
            at_g = pl.ds(pl.multiple_of((g * pairs + k) * TERMS, TERMS), TERMS)
            right[at_g, :] = plain[:, g * width : (g + 1) * width]
        left0[at, :] = ones
        left1[at, :] = ones
        return carry

    lax.fori_loop(0, pairs, expand, 0)
    for c in range(HALVES):
        plate_sum[c][...] = jnp.zeros(plate_sum[c].shape, f32)
        out_p[c][...] = jnp.zeros(out_p[c].shape, f32)
    half = vel[...] + 0.5 * time_step * fold[...] * mass[...]
    moved = pos[...] + time_step * half
    for b in range(blocks):
        at = slice(b * width, (b + 1) * width)
        half_b[b] = half[:, at]
        moved_b[b] = moved[:, at]
        mass_b[b] = mass[:, at]
    for q in range(mig_block.shape[1]):
        at = slice(q * width, (q + 1) * width)
        outgoing[0:3, at] = moved_b[mig_block[0, q]]
        outgoing[6:8, at] = jnp.full((2, width), mig_dest[0, q], jnp.int32).astype(f32)

    my_layer = lax.axis_index("gz")
    t_all = tower_v[...]
    p_all = plate_v[...]
    live = lax.broadcasted_iota(jnp.int32, (1, pairs), 1) < counts[0]
    t_layer = t_all // blocks
    t_turn = t_layer - my_layer
    t_turn = jnp.where(t_turn < 0, t_turn + nz, t_turn)
    t_row = jnp.where(live, t_turn * blocks + (t_all - t_layer * blocks), -1)
    p_cell = p_all // blocks
    p_number = jnp.zeros((1, pairs), jnp.int32)
    for o in range(9):
        number = slots.cell_number(slots.cell_slot(o // 3 - 1, o % 3 - 1))
        p_number = jnp.where(p_cell == o, number, p_number)
    p_row = jnp.where(live, p_number * blocks + (p_all - p_cell * blocks), -1)
    t_pick = jnp.where(
        lax.broadcasted_iota(jnp.int32, (nz * blocks, pairs), 0) == t_row, 1.0, 0.0
    ).astype(bf16)
    p_pick = jnp.where(
        lax.broadcasted_iota(jnp.int32, (cells * blocks, pairs), 0) == p_row, 1.0, 0.0
    ).astype(bf16)
    same = lax.broadcasted_iota(jnp.int32, (pairs, pairs), 0) == lax.broadcasted_iota(jnp.int32, (pairs, pairs), 1)
    t_col = jnp.sum(jnp.where(same, t_row.astype(f32), 0.0), axis=1, keepdims=True)
    p_col = jnp.sum(jnp.where(same, p_row.astype(f32), 0.0), axis=1, keepdims=True)

    for copy in first:
        copy.wait()

    lane_f = lax.broadcasted_iota(jnp.int32, (pairs, width), 1).astype(f32)

    def of_block(column, rows):
        found = jnp.zeros((pairs, width), f32)
        for s, row in enumerate(rows):
            found = found + jnp.where(lane_f == column - float(s * blocks), row, 0.0)
        return jnp.sum(found, axis=1, keepdims=True)

    sig_t = of_block(t_col, [tow[s, blocks, 0:1, :] for s in range(nz)])
    dep_t = of_block(t_col, [tow[s, blocks, 1:2, :] for s in range(nz)])
    sig_p = of_block(p_col, [near0[c, 2 * blocks : 2 * blocks + 1, :] for c in range(cells)])
    dep_p = of_block(p_col, [near0[c, 2 * blocks + 1 : 2 * blocks + 2, :] for c in range(cells)])
    sig = 0.5 * (sig_t + sig_p)
    sig2 = sig * sig
    sig6 = sig2 * sig2 * sig2
    depth = dep_t * dep_p
    att_tab[...] = jnp.broadcast_to((6.0 * scale / lx**6) * depth * sig6, (pairs, width))
    rep_tab[...] = jnp.broadcast_to((12.0 * scale / lx**12) * depth * sig6 * sig6, (pairs, width))

    def collect_towers(i, carry):
        for u in range(0, 8, 2):
            two = []
            for v in range(2):
                t = tower[0, i * 8 + u + v]
                layer = lax.div(t, blocks)
                turn = layer - my_layer
                two.append(tow[lax.rem(turn + nz, nz), t - layer * blocks])
            towers[pl.ds(pl.multiple_of(i * 32 + u * 4, 8), 8), :] = jnp.concatenate(two, axis=0)
        return carry

    def collect_plates(c):
        def body(i, carry):
            for u in range(8):
                p = plate[0, i * 8 + u]
                cell = lax.div(p, blocks)
                number = cell_table[cell]
                block = p - cell * blocks
                plates[i * 8 + u] = near[c][number, block]
                plates[pairs + i * 8 + u] = near[c][number, blocks + block]
            return carry

        lax.fori_loop(0, pairs // 8, body, 0)
        for r, terms in ((0, ((0,), (1,), (2,))), (1, ((3, 6, 7), (4, 8), (5,)))):
            for value, places in zip(split3(plates[r * pairs : (r + 1) * pairs, :]), terms):
                for t in places:
                    left[c][pl.ds(t, pairs, stride=TERMS), :] = value

    lax.fori_loop(0, pairs // 8, collect_towers, 0)
    for r, g in ((0, 0), (2, 1), (1, 2), (3, 3)):
        terms = ((3, 4, 5), (6, 8), (7,)) if r == 3 else ((9,), (10,), (11,))
        for value, places in zip(split3(towers[pl.ds(r, pairs, stride=4), :]), terms):
            for t in places:
                right[pl.ds(g * pairs * TERMS + t, pairs, stride=TERMS), :] = value
    collect_plates(0)

    lane = lax.broadcasted_iota(jnp.int32, (8, pairs), 1)

    def prepare(k, c, made):
        at = pl.ds(pl.multiple_of(k * TERMS, TERMS), TERMS)
        a = left[c][at, :].T.astype(bf16)
        b = [right[pl.ds(pl.multiple_of((g * pairs + k) * TERMS, TERMS), TERMS), :] for g in range(4)]
        first_two = jnp.concatenate(b[0:2], axis=1).astype(bf16)
        last_two = jnp.concatenate(b[2:4], axis=1).astype(bf16)
        made[:, 0 : 2 * width] = jnp.dot(a[0:part], first_two, preferred_element_type=f32)
        made[:, 2 * width :] = jnp.dot(a[part:], last_two, preferred_element_type=f32)

    def arithmetic(k, c, made):
        rep = rep_tab[pl.ds(k, 1), :]
        att = att_tab[pl.ds(k, 1), :]
        here = lane == k
        sums = [None, None, None]
        for w in range(part // 8):
            at = slice(w * 8, (w + 1) * 8)
            dx = made[at, 0:width]
            dz = made[at, width : 2 * width]
            dy = made[at, 2 * width : 3 * width]
            dx = dx - jnp.floor(dx + 0.5)
            dy = dy - jnp.floor(dy + 0.5)
            h = (dx * dx + dz * dz) + (ratio * (dy * dy) + shift_h)
            q = lax.rsqrt(h)
            f = jnp.maximum(allowed[pl.ds(pl.multiple_of(k * width + (c * part + w * 8), 8), 8), :] - h, 0.0)
            s = q * q
            s3 = s * s * s
            fq = f * q
            g = fq * fq
            e = s3 * (rep * s3 - att) + made[at, 3 * width : 4 * width] * q
            force_c = e * g
            parts = (force_c * dx, force_c * dy, force_c * dz)
            sums = [v if u is None else u + v for u, v in zip(sums, parts)]
            for r in range(3):
                total = jnp.broadcast_to(jnp.sum(parts[r], axis=1, keepdims=True), (8, pairs))
                pltpu.store(plate_sum[c].at[r * part + w * 8 : r * part + (w + 1) * 8, :], total, mask=here)
        for r in range(3):
            total = jnp.sum(sums[r], axis=0, keepdims=True)
            at = pl.ds(r * pairs + k, 1)
            tower_sum[at, :] = total if c == 0 else tower_sum[at, :] + total

    def run(c):
        prepare(0, c, made_a)

        def step(i, carry):
            for u in range(0, UNROLL, 2):
                k = i * UNROLL + u
                prepare(k + 1, c, made_b)
                arithmetic(k, c, made_a)
                prepare(lax.rem(k + 2, pairs), c, made_a)
                arithmetic(k + 1, c, made_b)
            return carry

        lax.fori_loop(0, pairs // UNROLL, step, 0)
        total = jnp.zeros((cells * blocks, 3 * part), f32)
        for piece in split3(plate_sum[c][...]):
            total = total + lax.dot_general(
                p_pick, piece.astype(bf16), (((1,), (1,)), ((), ())), preferred_element_type=f32
            )
        for s in range(cells):
            out_p[c][s, :, 0 : 3 * part] = total[s * blocks : (s + 1) * blocks]
        return send_cells(lambda s: out_p[c].at[s], land_p[c], (r0_s, r1_s)[c], (r0_r, r1_r)[c])

    returns = run(0)
    for copy in second:
        copy.wait()
    collect_plates(1)
    returns += run(1)
    for r in range(3):
        total = jnp.zeros((nz * blocks, width), f32)
        for piece in split3(tower_sum[r * pairs : (r + 1) * pairs, :]):
            total = total + jnp.dot(t_pick, piece.astype(bf16), preferred_element_type=f32)
        for s in range(nz):
            out_t[s, :, r * width : (r + 1) * width] = total[s * blocks : (s + 1) * blocks]
    for s in range(1, nz):
        there = slots.opposite(s)
        returns.append(send(out_t.at[s], land_t.at[there], rt_s.at[s], rt_r.at[there], s))
    for copy in returns:
        copy.wait()

    back = []
    for c in range(HALVES):
        total = out_p[c][0]
        for s in range(1, cells):
            total = total + land_p[c][s]
        back.append(total)
    on_tower = out_t[0]
    for s in range(1, nz):
        on_tower = on_tower + land_t[s]
    a0, b0 = back[0][:, 0:width], back[0][:, width : 2 * width]
    a1, b1 = back[1][:, 0:width], back[1][:, width : 2 * width]
    on_plate = (
        jnp.where(low, a0, pltpu.roll(a1, part, 1)),
        jnp.where(low, pltpu.roll(a0, part, 1), a1),
        jnp.where(low, b0, pltpu.roll(b1, part, 1)),
    )
    for r in range(3):
        force[r] = (
            on_tower[:, r * width : (r + 1) * width] - on_plate[r]
        ) * lengths[r]
    for q in range(mig_block.shape[1]):
        at = slice(q * width, (q + 1) * width)
        block = mig_block[0, q]
        kick = 0.5 * time_step * mass_b[block]
        old = half_b[block]
        for r in range(3):
            outgoing[3 + r : 4 + r, at] = old[r : r + 1] + kick * force[r, block][None, :]
    arrived[0] = outgoing[...]
    for copy in send_cells(lambda s: outgoing, arrived, mg_s, mg_r):
        copy.wait()


def output_kernel(slots, blocks, mig_block, force, arrived, pos, vel, fold, mass, pos_out, vel_out, force_out, arrive):
    atoms = pos.shape[1]
    width = atoms // blocks
    for r in range(3):
        for b in range(blocks):
            force_out[r : r + 1, b * width : (b + 1) * width] = force[r, b : b + 1]
    block_of = lax.broadcasted_iota(jnp.int32, pos.shape, 1) // width
    gone = block_of == mig_block[0, 0]
    for q in range(1, mig_block.shape[1]):
        gone = gone | (block_of == mig_block[0, q])
    half = vel[...] + 0.5 * time_step * fold[...] * mass[...]
    pos_out[...] = jnp.where(gone, 0.0, pos[...] + time_step * half)
    vel_out[...] = jnp.where(gone, 0.0, half + 0.5 * time_step * force_out[...] * mass[...])
    for i, (a, b) in enumerate(source_offsets):
        got = arrived[slots.cell_number(slots.cell_slot(a, b))]
        wanted = float((1 - a) * 3 + (1 - b))
        arrive[:, 0, i, :] = jnp.where(got[6:7] == wanted, got[0:6], 0.0)


def local(
    slots, positions, velocities, forces_old, inv_mass, charges, block_species, sigma_table, epsilon_table,
    tower_index, plate_index, tile_counts, exclusions, mig_block, mig_dest,
):
    atoms = positions.shape[1]
    blocks = block_species.shape[0]
    width = atoms // blocks
    nz, cells = slots.nz, slots.cells
    pairs = tower_index.shape[1]
    leaving = mig_block.shape[1]
    kinds = sigma_table.shape[0]
    part = width // HALVES
    any_spec = pl.BlockSpec(memory_space=pl.ANY)
    vmem = pl.BlockSpec(memory_space=pltpu.VMEM)
    smem = pl.BlockSpec(memory_space=pltpu.SMEM)
    mass = inv_mass[None, :]
    f32, i32 = jnp.float32, jnp.int32

    def sems(n):
        return pltpu.SemaphoreType.DMA((n,))

    def v(*shape):
        return pltpu.VMEM(shape, f32)

    rows = jax.ShapeDtypeStruct((3, atoms), f32)
    force, arrived = pl.pallas_call(
        functools.partial(step_kernel, slots, blocks),
        out_shape=(
            jax.ShapeDtypeStruct((3, blocks, width), f32),
            jax.ShapeDtypeStruct((cells, 8, leaving * width), f32),
        ),
        in_specs=[any_spec] * 14,
        out_specs=(vmem, vmem),
        scratch_shapes=[
            v(3, atoms), v(3, atoms), v(3, atoms), v(1, atoms), v(1, atoms), pltpu.VMEM((1, blocks), i32),
            pltpu.SMEM((kinds,), f32), pltpu.SMEM((kinds,), f32),
            pltpu.SMEM((1, pairs), i32), pltpu.SMEM((1, pairs), i32),
            pltpu.VMEM((1, pairs), i32), pltpu.VMEM((1, pairs), i32),
            pltpu.SMEM((1,), i32), pltpu.VMEM(exclusions.shape, i32),
            pltpu.SMEM((1, leaving), i32), pltpu.SMEM((1, leaving), i32),
            v(blocks, 3, width), v(blocks, 3, width), v(blocks, 1, width), v(4 * blocks, width), v(nz, blocks + 1, 4, width),
            v(cells, 2 * blocks + 8, width), v(cells, 2 * blocks, width),
            v(pairs * width, width), v(pairs, width), v(pairs, width), v(4 * pairs, width), v(2 * pairs, width),
            v(4 * pairs * TERMS, width), v(pairs * TERMS, width), v(pairs * TERMS, width),
            v(part, 4 * width), v(part, 4 * width), v(3 * pairs, width), v(3 * part, pairs), v(3 * part, pairs),
            v(nz, blocks, 3 * width), v(cells, blocks, 2 * width), v(cells, blocks, 2 * width),
            v(nz, blocks, 3 * width), v(cells, blocks, 2 * width), v(cells, blocks, 2 * width),
            v(8, leaving * width),
            pltpu.SMEM((9,), i32), sems(16),
        ]
        + [sems(nz)] * 2 + [sems(cells)] * 4 + [sems(nz)] * 2 + [sems(cells)] * 6,
        compiler_params=pltpu.CompilerParams(
            collective_id=0, has_side_effects=True, vmem_limit_bytes=40 * 1024 * 1024
        ),
        name="membrane_step",
    )(
        positions, velocities, forces_old, mass, charges[None, :], block_species[None, :], sigma_table,
        epsilon_table, tower_index, plate_index, tile_counts, exclusions, mig_block, mig_dest,
    )
    positions_new, velocities_new, forces_new, arrivals = pl.pallas_call(
        functools.partial(output_kernel, slots, blocks),
        out_shape=(rows, rows, rows, jax.ShapeDtypeStruct((6, 1, len(source_offsets), leaving * width), f32)),
        in_specs=[smem] + [vmem] * 6,
        out_specs=(vmem,) * 4,
        name="outputs",
    )(mig_block, force, arrived, positions, velocities, forces_old, mass)
    return positions_new, velocities_new, forces_new, arrivals


def solution(mesh):
    cells = ("gx", "gy", "gz")
    slots = Slots(mesh.shape["gx"], mesh.shape["gy"], mesh.shape["gz"])
    row = P(None, cells)
    flat = P(cells)
    pair = P(cells, None)
    in_specs = (
        row, row, row, flat, flat, flat, P(), P(), pair, pair, flat, P(cells, None, None, None), pair, pair,
    )
    out_specs = (row, row, row, P(None, cells, None, None))
    return jax.shard_map(
        functools.partial(local, slots), mesh=mesh, in_specs=in_specs, out_specs=out_specs, check_vma=False
    )
```

```python
import functools
import jax
import jax.numpy as jnp
from jax import lax
from jax.experimental import pallas as pl
from jax.experimental.pallas import tpu as pltpu
from jax.sharding import PartitionSpec as P

time_step = 0.2
soft_core = 0.09
cutoff_sq = 1.44
coulomb_k = 0.5
MESH = pl.DeviceIdType.MESH
UNROLL = 4
HALVES = 2
TERMS = 16
source_offsets = ((-1, -1), (-1, 0), (-1, 1), (0, -1), (0, 1), (1, -1), (1, 0), (1, 1))


class Slots:
    def __init__(self, nx, ny, nz):
        self.nx, self.ny, self.nz = nx, ny, nz
        self.offsets = [(0, 0, 0)] + [(0, 0, k) for k in range(1, nz)]
        self.cell = {(0, 0): 0}
        for da in range(-1, 2):
            for db in range(-1, 2):
                key = (da % nx, db % ny)
                if key not in self.cell:
                    self.cell[key] = len(self.offsets)
                    self.offsets.append((key[0], key[1], 0))
        self.count = len(self.offsets)
        self.cells = 1 + self.count - nz

    def cell_slot(self, da, db):
        return self.cell[(da % self.nx, db % self.ny)]

    def cell_number(self, slot):
        return slot - self.nz + 1 if slot else 0

    def opposite(self, slot):
        dx, dy, dz = self.offsets[slot]
        if dz:
            return (self.nz - dz) % self.nz
        return self.cell_slot(-dx, -dy)

    def device(self, slot):
        dx, dy, dz = self.offsets[slot]
        return (
            lax.rem(lax.axis_index("gx") + dx, self.nx),
            lax.rem(lax.axis_index("gy") + dy, self.ny),
            lax.rem(lax.axis_index("gz") + dz, self.nz),
        )


def split3(value):
    high = value.astype(jnp.bfloat16).astype(jnp.float32)
    rest = value - high
    mid = rest.astype(jnp.bfloat16).astype(jnp.float32)
    return high, mid, rest - mid


def step_kernel(
    slots, blocks,
    pos_h, vel_h, fold_h, mass_h, charge_h, species_h, sigma_h, eps_h, tower_h, plate_h, counts_h, excl_h,
    mig_block_h, mig_dest_h,
    force, arrived,
    pos, vel, fold, mass, charge, species, sigma_s, eps_s, tower, plate, tower_v, plate_v, counts, excl,
    mig_block, mig_dest,
    half_b, moved_b, mass_b, dense, tow, near0, near1, allowed, rep_tab, att_tab, towers, plates, right, left0, left1,
    made_a, made_b, tower_sum, plate_sum0, plate_sum1, out_t, out_p0, out_p1, land_t, land_p0, land_p1, outgoing,
    t_flat, p_flat, local_sem,
    tow_s, tow_r, n0_s, n0_r, n1_s, n1_r, rt_s, rt_r, r0_s, r0_r, r1_s, r1_r, mg_s, mg_r,
):
    atoms = pos.shape[1]
    width = atoms // blocks
    pairs = tower.shape[1]
    words = excl.shape[2]
    part = width // HALVES
    pitch = 2 * blocks + 8
    nx, ny, nz, cells = slots.nx, slots.ny, slots.nz, slots.cells
    lx, ly = float(nx), float(ny)
    lengths = (lx, ly, lx)
    f32 = jnp.float32
    bf16 = jnp.bfloat16
    near = (near0, near1)
    left = (left0, left1)
    plate_sum = (plate_sum0, plate_sum1)
    out_p = (out_p0, out_p1)
    land_p = (land_p0, land_p1)
    ratio = (ly / lx) ** 2
    shift_h = soft_core / (lx * lx)
    edge = (cutoff_sq + soft_core) / (lx * lx)
    scale = lx * lx / (cutoff_sq * cutoff_sq)

    barrier = pltpu.get_barrier_semaphore()
    for s in range(1, slots.count):
        pl.semaphore_signal(barrier, inc=1, device_id=slots.device(s), device_id_type=MESH)
    fetches = []
    for src, dst in (
        (pos_h, pos), (vel_h, vel), (fold_h, fold), (mass_h, mass), (charge_h, charge), (species_h, species),
        (sigma_h, sigma_s), (eps_h, eps_s), (excl_h, excl),
        (tower_h, tower_v), (plate_h, plate_v), (counts_h, counts), (mig_block_h, mig_block), (mig_dest_h, mig_dest),
    ):
        copy = pltpu.make_async_copy(src, dst, local_sem.at[len(fetches)])
        copy.start()
        fetches.append(copy)
    for copy in fetches[:8]:
        copy.wait()

    half = vel[...] + 0.5 * time_step * fold[...] * mass[...]
    moved = pos[...] + time_step * half
    row3 = lax.broadcasted_iota(jnp.int32, (3, atoms), 0)
    scaled = moved * jnp.where(row3 == 1, f32(1.0 / ly), f32(1.0 / lx))
    tower_charge = charge[...] * (coulomb_k * scale / lx)
    for b in range(blocks):
        at = slice(b * width, (b + 1) * width)
        tow[b, 0:3, :] = scaled[:, at]
        tow[b, 3:4, :] = tower_charge[:, at]
        for r in range(3):
            dense[r * blocks + b : r * blocks + b + 1, :] = scaled[r : r + 1, at]
        dense[3 * blocks + b : 3 * blocks + b + 1, :] = charge[:, at]
    which = species[...]
    sigma = jnp.zeros((1, blocks), f32)
    eps = jnp.zeros((1, blocks), f32)
    for k in range(sigma_s.shape[0]):
        sigma = jnp.where(which == k, sigma_s[k], sigma)
        eps = jnp.where(which == k, eps_s[k], eps)
    depth_row = jnp.sqrt(eps)
    tow[blocks] = jnp.zeros((4, width), f32)
    tow[blocks, 0:1, 0:blocks] = sigma
    tow[blocks, 1:2, 0:blocks] = depth_row
    near0[2 * blocks : pitch, :] = jnp.zeros((8, width), f32)
    near0[2 * blocks : 2 * blocks + 1, 0:blocks] = sigma
    near0[2 * blocks + 1 : 2 * blocks + 2, 0:blocks] = depth_row
    low = lax.broadcasted_iota(jnp.int32, (blocks, width), 1) < part
    comp = [dense[r * blocks : (r + 1) * blocks, :] for r in range(4)]
    turned = [pltpu.roll(v, part, 1) for v in comp]
    near0[0:blocks, :] = jnp.where(low, comp[0], turned[1])
    near0[blocks : 2 * blocks, :] = jnp.where(low, comp[2], turned[3])
    near1[0:blocks, :] = jnp.where(low, turned[0], comp[1])
    near1[blocks : 2 * blocks, :] = jnp.where(low, turned[2], comp[3])

    pl.semaphore_wait(barrier, slots.count - 1)

    def send(src, dst, ss, rs, s):
        copy = pltpu.make_async_remote_copy(
            src_ref=src, dst_ref=dst, send_sem=ss, recv_sem=rs, device_id=slots.device(s), device_id_type=MESH
        )
        copy.start()
        return copy

    def send_cells(source, landing, ss, rs):
        copies = []
        for s in range(nz, slots.count):
            here, there = slots.cell_number(s), slots.cell_number(slots.opposite(s))
            copies.append(send(source(here), landing(there), ss.at[here], rs.at[there], s))
        return copies

    def rows_of(ref, size):
        return lambda c: ref.at[c * pitch : c * pitch + size]

    first = send_cells(lambda c: near0.at[0:pitch], rows_of(near0, pitch), n0_s, n0_r)
    above = []
    for s in range(1, nz):
        there = slots.opposite(s) * (blocks + 1)
        above.append(
            send(tow.at[0 : blocks + 1], tow.at[there : there + blocks + 1], tow_s.at[s], tow_r.at[slots.opposite(s)], s)
        )
    second = send_cells(lambda c: near1.at[0 : 2 * blocks], rows_of(near1, 2 * blocks), n1_s, n1_r)

    bit = jnp.left_shift(1, lax.broadcasted_iota(jnp.int32, (8, width), 0))
    group = lax.broadcasted_iota(jnp.int32, (TERMS, 4 * width), 1) // width
    term = lax.broadcasted_iota(jnp.int32, (TERMS, 4 * width), 0)
    plain = jnp.where(((group == 0) | (group == 2)) & (term < 3), -1.0, 0.0)
    plain = jnp.where((group == 1) & (term >= 3) & (term < 6), -1.0, plain)
    term1 = lax.broadcasted_iota(jnp.int32, (TERMS, width), 0)
    ones = jnp.where((term1 >= 9) & (term1 < 12), 1.0, 0.0)
    for copy in fetches[8:]:
        copy.wait()

    def expand(k, carry):
        for w in range(words):
            hit = excl[0, k, w : w + 1, :] & bit
            allowed[pl.ds(pl.multiple_of(k * width + w * 8, 8), 8), :] = jnp.where(hit == 0, edge, -1.0)
        at = pl.ds(pl.multiple_of(k * TERMS, TERMS), TERMS)
        for g in range(4):
            at_g = pl.ds(pl.multiple_of((g * pairs + k) * TERMS, TERMS), TERMS)
            right[at_g, :] = plain[:, g * width : (g + 1) * width]
        left0[at, :] = ones
        left1[at, :] = ones
        return carry

    lax.fori_loop(0, pairs, expand, 0)
    for c in range(HALVES):
        plate_sum[c][...] = jnp.zeros(plate_sum[c].shape, f32)
        out_p[c][...] = jnp.zeros(out_p[c].shape, f32)
    half = vel[...] + 0.5 * time_step * fold[...] * mass[...]
    moved = pos[...] + time_step * half
    for b in range(blocks):
        at = slice(b * width, (b + 1) * width)
        half_b[b] = half[:, at]
        moved_b[b] = moved[:, at]
        mass_b[b] = mass[:, at]
    for q in range(mig_block.shape[1]):
        at = slice(q * width, (q + 1) * width)
        outgoing[0:3, at] = moved_b[mig_block[0, q]]
        outgoing[6:8, at] = jnp.full((2, width), mig_dest[0, q], jnp.int32).astype(f32)

    my_layer = lax.axis_index("gz")
    t_all = tower_v[...]
    p_all = plate_v[...]
    live = lax.broadcasted_iota(jnp.int32, (1, pairs), 1) < counts[0, 0]
    t_layer = t_all // blocks
    t_turn = t_layer - my_layer
    t_turn = jnp.where(t_turn < 0, t_turn + nz, t_turn)
    t_block = t_all - t_layer * blocks
    t_flat[...] = t_turn * (blocks + 1) + t_block
    t_row = jnp.where(live, t_turn * blocks + t_block, -1)
    p_cell = p_all // blocks
    p_number = jnp.zeros((1, pairs), jnp.int32)
    for o in range(9):
        number = slots.cell_number(slots.cell_slot(o // 3 - 1, o % 3 - 1))
        p_number = jnp.where(p_cell == o, number, p_number)
    p_block = p_all - p_cell * blocks
    p_flat[...] = p_number * pitch + p_block
    p_row = jnp.where(live, p_number * blocks + p_block, -1)
    tables = []
    for src, dst in ((t_flat, tower), (p_flat, plate)):
        tables.append(pltpu.make_async_copy(src, dst, local_sem.at[14 + len(tables)]))
        tables[-1].start()
    t_pick = jnp.where(
        lax.broadcasted_iota(jnp.int32, (nz * blocks, pairs), 0) == t_row, 1.0, 0.0
    ).astype(bf16)
    p_pick = jnp.where(
        lax.broadcasted_iota(jnp.int32, (cells * blocks, pairs), 0) == p_row, 1.0, 0.0
    ).astype(bf16)
    same = lax.broadcasted_iota(jnp.int32, (pairs, pairs), 0) == lax.broadcasted_iota(jnp.int32, (pairs, pairs), 1)
    t_col = jnp.sum(jnp.where(same, t_row.astype(f32), 0.0), axis=1, keepdims=True)
    p_col = jnp.sum(jnp.where(same, p_row.astype(f32), 0.0), axis=1, keepdims=True)

    for copy in tables:
        copy.wait()
    for copy in above:
        copy.wait()

    lane_f = lax.broadcasted_iota(jnp.int32, (pairs, width), 1).astype(f32)

    def of_block(column, rows):
        found = jnp.zeros((pairs, width), f32)
        for s, row in enumerate(rows):
            found = found + jnp.where(lane_f == column - float(s * blocks), row, 0.0)
        return jnp.sum(found, axis=1, keepdims=True)

    sig_t = of_block(t_col, [tow[s * (blocks + 1) + blocks, 0:1, :] for s in range(nz)])
    dep_t = of_block(t_col, [tow[s * (blocks + 1) + blocks, 1:2, :] for s in range(nz)])
    def collect_towers(i, carry):
        for u in range(0, 16, 2):
            two = [tow[tower[0, i * 16 + u + v]] for v in range(2)]
            towers[pl.ds(pl.multiple_of(i * 64 + u * 4, 8), 8), :] = jnp.concatenate(two, axis=0)
        return carry

    lax.fori_loop(0, pairs // 16, collect_towers, 0)
    for r, g in ((0, 0), (2, 1), (1, 2), (3, 3)):
        terms = ((3, 4, 5), (6, 8), (7,)) if r == 3 else ((9,), (10,), (11,))
        for value, places in zip(split3(towers[pl.ds(r, pairs, stride=4), :]), terms):
            for t in places:
                right[pl.ds(g * pairs * TERMS + t, pairs, stride=TERMS), :] = value
    for copy in first:
        copy.wait()
    sig_p = of_block(p_col, [near0[c * pitch + 2 * blocks : c * pitch + 2 * blocks + 1, :] for c in range(cells)])
    dep_p = of_block(p_col, [near0[c * pitch + 2 * blocks + 1 : c * pitch + 2 * blocks + 2, :] for c in range(cells)])
    sig = 0.5 * (sig_t + sig_p)
    sig2 = sig * sig
    sig6 = sig2 * sig2 * sig2
    depth = dep_t * dep_p
    att_tab[...] = jnp.broadcast_to((6.0 * scale / lx**6) * depth * sig6, (pairs, width))
    rep_tab[...] = jnp.broadcast_to((12.0 * scale / lx**12) * depth * sig6 * sig6, (pairs, width))

    def collect_plates(c):
        def body(i, carry):
            for u in range(16):
                p = plate[0, i * 16 + u]
                plates[i * 16 + u] = near[c][p]
                plates[pairs + i * 16 + u] = near[c][p + blocks]
            return carry

        lax.fori_loop(0, pairs // 16, body, 0)
        for r, terms in ((0, ((0,), (1,), (2,))), (1, ((3, 6, 7), (4, 8), (5,)))):
            for value, places in zip(split3(plates[r * pairs : (r + 1) * pairs, :]), terms):
                for t in places:
                    left[c][pl.ds(t, pairs, stride=TERMS), :] = value

    collect_plates(0)

    lane = lax.broadcasted_iota(jnp.int32, (8, pairs), 1)

    def prepare(k, c, made):
        at = pl.ds(pl.multiple_of(k * TERMS, TERMS), TERMS)
        a = left[c][at, :].T.astype(bf16)
        b = [right[pl.ds(pl.multiple_of((g * pairs + k) * TERMS, TERMS), TERMS), :] for g in range(4)]
        first_two = jnp.concatenate(b[0:2], axis=1).astype(bf16)
        last_two = jnp.concatenate(b[2:4], axis=1).astype(bf16)
        made[:, 0 : 2 * width] = jnp.dot(a[0:part], first_two, preferred_element_type=f32)
        made[:, 2 * width :] = jnp.dot(a[part:], last_two, preferred_element_type=f32)

    def arithmetic(k, c, made):
        rep = rep_tab[pl.ds(k, 1), :]
        att = att_tab[pl.ds(k, 1), :]
        here = lane == k
        sums = [None, None, None]
        for w in range(part // 8):
            at = slice(w * 8, (w + 1) * 8)
            dx = made[at, 0:width]
            dz = made[at, width : 2 * width]
            dy = made[at, 2 * width : 3 * width]
            dx = dx - jnp.floor(dx + 0.5)
            dy = dy - jnp.floor(dy + 0.5)
            h = (dx * dx + dz * dz) + (ratio * (dy * dy) + shift_h)
            q = lax.rsqrt(h)
            f = jnp.maximum(allowed[pl.ds(pl.multiple_of(k * width + (c * part + w * 8), 8), 8), :] - h, 0.0)
            s = q * q
            s3 = s * s * s
            fq = f * q
            g = fq * fq
            e = s3 * (rep * s3 - att) + made[at, 3 * width : 4 * width] * q
            force_c = e * g
            parts = (force_c * dx, force_c * dy, force_c * dz)
            sums = [v if u is None else u + v for u, v in zip(sums, parts)]
            for r in range(3):
                total = jnp.broadcast_to(jnp.sum(parts[r], axis=1, keepdims=True), (8, pairs))
                pltpu.store(plate_sum[c].at[r * part + w * 8 : r * part + (w + 1) * 8, :], total, mask=here)
        for r in range(3):
            total = jnp.sum(sums[r], axis=0, keepdims=True)
            at = pl.ds(r * pairs + k, 1)
            tower_sum[at, :] = total if c == 0 else tower_sum[at, :] + total

    def run(c):
        for u in range(UNROLL):
            prepare(u, c, made_a.at[u])

        def step(i, carry):
            k = i * (2 * UNROLL)
            for u in range(UNROLL):
                prepare(k + UNROLL + u, c, made_b.at[u])
                arithmetic(k + u, c, made_a.at[u])
            for u in range(UNROLL):
                prepare(lax.rem(k + 2 * UNROLL + u, pairs), c, made_a.at[u])
                arithmetic(k + UNROLL + u, c, made_b.at[u])
            return carry

        lax.fori_loop(0, pairs // (2 * UNROLL), step, 0)
        total = jnp.zeros((cells * blocks, 3 * part), f32)
        for piece in split3(plate_sum[c][...]):
            total = total + lax.dot_general(
                p_pick, piece.astype(bf16), (((1,), (1,)), ((), ())), preferred_element_type=f32
            )
        for s in range(cells):
            out_p[c][s, :, 0 : 3 * part] = total[s * blocks : (s + 1) * blocks]
        return send_cells(lambda s: out_p[c].at[s], lambda s: land_p[c].at[s], (r0_s, r1_s)[c], (r0_r, r1_r)[c])

    returns = run(0)
    for copy in second:
        copy.wait()
    collect_plates(1)
    returns += run(1)
    for r in range(3):
        total = jnp.zeros((nz * blocks, width), f32)
        for piece in split3(tower_sum[r * pairs : (r + 1) * pairs, :]):
            total = total + jnp.dot(t_pick, piece.astype(bf16), preferred_element_type=f32)
        for s in range(nz):
            out_t[s, :, r * width : (r + 1) * width] = total[s * blocks : (s + 1) * blocks]
    for s in range(1, nz):
        there = slots.opposite(s)
        returns.append(send(out_t.at[s], land_t.at[there], rt_s.at[s], rt_r.at[there], s))
    for copy in returns:
        copy.wait()

    back = []
    for c in range(HALVES):
        total = out_p[c][0]
        for s in range(1, cells):
            total = total + land_p[c][s]
        back.append(total)
    on_tower = out_t[0]
    for s in range(1, nz):
        on_tower = on_tower + land_t[s]
    a0, b0 = back[0][:, 0:width], back[0][:, width : 2 * width]
    a1, b1 = back[1][:, 0:width], back[1][:, width : 2 * width]
    on_plate = (
        jnp.where(low, a0, pltpu.roll(a1, part, 1)),
        jnp.where(low, pltpu.roll(a0, part, 1), a1),
        jnp.where(low, b0, pltpu.roll(b1, part, 1)),
    )
    for r in range(3):
        force[r] = (
            on_tower[:, r * width : (r + 1) * width] - on_plate[r]
        ) * lengths[r]
    for q in range(mig_block.shape[1]):
        at = slice(q * width, (q + 1) * width)
        block = mig_block[0, q]
        kick = 0.5 * time_step * mass_b[block]
        old = half_b[block]
        for r in range(3):
            outgoing[3 + r : 4 + r, at] = old[r : r + 1] + kick * force[r, block][None, :]
    arrived[0] = outgoing[...]
    for copy in send_cells(lambda s: outgoing, lambda s: arrived.at[s], mg_s, mg_r):
        copy.wait()


def output_kernel(slots, blocks, mig_block, force, arrived, pos, vel, fold, mass, pos_out, vel_out, force_out, arrive):
    atoms = pos.shape[1]
    width = atoms // blocks
    for r in range(3):
        for b in range(blocks):
            force_out[r : r + 1, b * width : (b + 1) * width] = force[r, b : b + 1]
    block_of = lax.broadcasted_iota(jnp.int32, pos.shape, 1) // width
    gone = block_of == mig_block[0, 0]
    for q in range(1, mig_block.shape[1]):
        gone = gone | (block_of == mig_block[0, q])
    half = vel[...] + 0.5 * time_step * fold[...] * mass[...]
    pos_out[...] = jnp.where(gone, 0.0, pos[...] + time_step * half)
    vel_out[...] = jnp.where(gone, 0.0, half + 0.5 * time_step * force_out[...] * mass[...])
    for i, (a, b) in enumerate(source_offsets):
        got = arrived[slots.cell_number(slots.cell_slot(a, b))]
        wanted = float((1 - a) * 3 + (1 - b))
        arrive[:, 0, i, :] = jnp.where(got[6:7] == wanted, got[0:6], 0.0)


def local(
    slots, positions, velocities, forces_old, inv_mass, charges, block_species, sigma_table, epsilon_table,
    tower_index, plate_index, tile_counts, exclusions, mig_block, mig_dest,
):
    atoms = positions.shape[1]
    blocks = block_species.shape[0]
    width = atoms // blocks
    nz, cells = slots.nz, slots.cells
    pairs = tower_index.shape[1]
    leaving = mig_block.shape[1]
    kinds = sigma_table.shape[0]
    part = width // HALVES
    pitch = 2 * blocks + 8
    any_spec = pl.BlockSpec(memory_space=pl.ANY)
    vmem = pl.BlockSpec(memory_space=pltpu.VMEM)
    smem = pl.BlockSpec(memory_space=pltpu.SMEM)
    mass = inv_mass[None, :]
    f32, i32 = jnp.float32, jnp.int32

    def sems(n):
        return pltpu.SemaphoreType.DMA((n,))

    def v(*shape):
        return pltpu.VMEM(shape, f32)

    rows = jax.ShapeDtypeStruct((3, atoms), f32)
    force, arrived = pl.pallas_call(
        functools.partial(step_kernel, slots, blocks),
        out_shape=(
            jax.ShapeDtypeStruct((3, blocks, width), f32),
            jax.ShapeDtypeStruct((cells, 8, leaving * width), f32),
        ),
        in_specs=[any_spec] * 14,
        out_specs=(vmem, vmem),
        scratch_shapes=[
            v(3, atoms), v(3, atoms), v(3, atoms), v(1, atoms), v(1, atoms), pltpu.VMEM((1, blocks), i32),
            pltpu.SMEM((kinds,), f32), pltpu.SMEM((kinds,), f32),
            pltpu.SMEM((1, pairs), i32), pltpu.SMEM((1, pairs), i32),
            pltpu.VMEM((1, pairs), i32), pltpu.VMEM((1, pairs), i32),
            pltpu.SMEM((1, 1), i32), pltpu.VMEM(exclusions.shape, i32),
            pltpu.SMEM((1, leaving), i32), pltpu.SMEM((1, leaving), i32),
            v(blocks, 3, width), v(blocks, 3, width), v(blocks, 1, width), v(4 * blocks, width), v(nz * (blocks + 1), 4, width),
            v(cells * pitch, width), v(cells * pitch, width),
            v(pairs * width, width), v(pairs, width), v(pairs, width), v(4 * pairs, width), v(2 * pairs, width),
            v(4 * pairs * TERMS, width), v(pairs * TERMS, width), v(pairs * TERMS, width),
            v(UNROLL, part, 4 * width), v(UNROLL, part, 4 * width), v(3 * pairs, width), v(3 * part, pairs), v(3 * part, pairs),
            v(nz, blocks, 3 * width), v(cells, blocks, 2 * width), v(cells, blocks, 2 * width),
            v(nz, blocks, 3 * width), v(cells, blocks, 2 * width), v(cells, blocks, 2 * width),
            v(8, leaving * width),
            pltpu.VMEM((1, pairs), i32), pltpu.VMEM((1, pairs), i32), sems(16),
        ]
        + [sems(nz)] * 2 + [sems(cells)] * 4 + [sems(nz)] * 2 + [sems(cells)] * 6,
        compiler_params=pltpu.CompilerParams(
            collective_id=0, has_side_effects=True, vmem_limit_bytes=60 * 1024 * 1024
        ),
        name="membrane_step",
    )(
        positions, velocities, forces_old, mass, charges[None, :], block_species[None, :], sigma_table,
        epsilon_table, tower_index, plate_index, tile_counts[None, :], exclusions, mig_block, mig_dest,
    )
    positions_new, velocities_new, forces_new, arrivals = pl.pallas_call(
        functools.partial(output_kernel, slots, blocks),
        out_shape=(rows, rows, rows, jax.ShapeDtypeStruct((6, 1, len(source_offsets), leaving * width), f32)),
        in_specs=[smem] + [vmem] * 6,
        out_specs=(vmem,) * 4,
        name="outputs",
    )(mig_block, force, arrived, positions, velocities, forces_old, mass)
    return positions_new, velocities_new, forces_new, arrivals


def solution(mesh):
    cells = ("gx", "gy", "gz")
    slots = Slots(mesh.shape["gx"], mesh.shape["gy"], mesh.shape["gz"])
    row = P(None, cells)
    flat = P(cells)
    pair = P(cells, None)
    in_specs = (
        row, row, row, flat, flat, flat, P(), P(), pair, pair, flat, P(cells, None, None, None), pair, pair,
    )
    out_specs = (row, row, row, P(None, cells, None, None))
    return jax.shard_map(
        functools.partial(local, slots), mesh=mesh, in_specs=in_specs, out_specs=out_specs, check_vma=False
    )
```

```python
import functools
import jax
import jax.numpy as jnp
from jax import lax
from jax.experimental import pallas as pl
from jax.experimental.pallas import tpu as pltpu
from jax.sharding import PartitionSpec as P

time_step = 0.2
soft_core = 0.09
cutoff_sq = 1.44
coulomb_k = 0.5
MESH = pl.DeviceIdType.MESH
UNROLL = 4
HALVES = 2
TERMS = 16
source_offsets = ((-1, -1), (-1, 0), (-1, 1), (0, -1), (0, 1), (1, -1), (1, 0), (1, 1))


class Slots:
    def __init__(self, nx, ny, nz):
        self.nx, self.ny, self.nz = nx, ny, nz
        self.offsets = [(0, 0, 0)] + [(0, 0, k) for k in range(1, nz)]
        self.cell = {(0, 0): 0}
        for da in range(-1, 2):
            for db in range(-1, 2):
                key = (da % nx, db % ny)
                if key not in self.cell:
                    self.cell[key] = len(self.offsets)
                    self.offsets.append((key[0], key[1], 0))
        self.count = len(self.offsets)
        self.cells = 1 + self.count - nz

    def cell_slot(self, da, db):
        return self.cell[(da % self.nx, db % self.ny)]

    def cell_number(self, slot):
        return slot - self.nz + 1 if slot else 0

    def opposite(self, slot):
        dx, dy, dz = self.offsets[slot]
        if dz:
            return (self.nz - dz) % self.nz
        return self.cell_slot(-dx, -dy)

    def device(self, slot):
        dx, dy, dz = self.offsets[slot]
        return (
            lax.rem(lax.axis_index("gx") + dx, self.nx),
            lax.rem(lax.axis_index("gy") + dy, self.ny),
            lax.rem(lax.axis_index("gz") + dz, self.nz),
        )


def split3(value):
    high = value.astype(jnp.bfloat16).astype(jnp.float32)
    rest = value - high
    mid = rest.astype(jnp.bfloat16).astype(jnp.float32)
    return high, mid, rest - mid


def split2(value):
    high = value.astype(jnp.bfloat16)
    return high, (value - high.astype(jnp.float32)).astype(jnp.bfloat16)


def step_kernel(
    slots, blocks,
    pos_h, vel_h, fold_h, mass_h, charge_h, species_h, sigma_h, eps_h, tower_h, plate_h, counts_h, excl_h,
    mig_block_h, mig_dest_h,
    pos_out_h, vel_out_h, force_out_h, arrive_h,
    pos, vel, fold, mass, charge, species, sigma_s, eps_s, tower, plate, tower_v, plate_v, counts, excl,
    mig_block, mig_dest,
    half_b, moved_b, mass_b, dense, tow, near0, near1, allowed, att_tab, towers, plates, right, left0, left1,
    made_a, made_b, tower_sum, plate_sum0, plate_sum1, out_t, out_p0, out_p1, land_t, land_p0, land_p1, going_m, going_v, come_m, come_v,
    force, pos_out, vel_out, force_out, arrive,
    t_flat, p_flat, local_sem,
    tow_s, tow_r, n0_s, n0_r, n1_s, n1_r, rt_s, rt_r, r0_s, r0_r, r1_s, r1_r, mm_s, mm_r, mv_s, mv_r,
):
    atoms = pos.shape[1]
    width = atoms // blocks
    pairs = tower.shape[1]
    words = excl.shape[2]
    part = width // HALVES
    pitch = 2 * blocks + 8
    nx, ny, nz, cells = slots.nx, slots.ny, slots.nz, slots.cells
    lx, ly = float(nx), float(ny)
    lengths = (lx, ly, lx)
    f32 = jnp.float32
    bf16 = jnp.bfloat16
    near = (near0, near1)
    left = (left0, left1)
    plate_sum = (plate_sum0, plate_sum1)
    out_p = (out_p0, out_p1)
    land_p = (land_p0, land_p1)
    ratio = (ly / lx) ** 2
    shift_h = soft_core / (lx * lx)
    edge = (cutoff_sq + soft_core) / (lx * lx)
    scale = lx * lx / (cutoff_sq * cutoff_sq)

    barrier = pltpu.get_barrier_semaphore()
    for s in range(1, slots.count):
        pl.semaphore_signal(barrier, inc=1, device_id=slots.device(s), device_id_type=MESH)
    fetches = []
    for src, dst in (
        (pos_h, pos), (vel_h, vel), (fold_h, fold), (mass_h, mass), (charge_h, charge), (species_h, species),
        (sigma_h, sigma_s), (eps_h, eps_s), (excl_h, excl),
        (tower_h, tower_v), (plate_h, plate_v), (counts_h, counts), (mig_block_h, mig_block), (mig_dest_h, mig_dest),
    ):
        copy = pltpu.make_async_copy(src, dst, local_sem.at[len(fetches)])
        copy.start()
        fetches.append(copy)
    for copy in fetches[:8]:
        copy.wait()

    half = vel[...] + 0.5 * time_step * fold[...] * mass[...]
    moved = pos[...] + time_step * half
    row3 = lax.broadcasted_iota(jnp.int32, (3, atoms), 0)
    scaled = moved * jnp.where(row3 == 1, f32(1.0 / ly), f32(1.0 / lx))
    tower_charge = charge[...] * (coulomb_k * scale / lx)
    for b in range(blocks):
        at = slice(b * width, (b + 1) * width)
        tow[b, 0:3, :] = scaled[:, at]
        tow[b, 3:4, :] = tower_charge[:, at]
        for r in range(3):
            dense[r * blocks + b : r * blocks + b + 1, :] = scaled[r : r + 1, at]
        dense[3 * blocks + b : 3 * blocks + b + 1, :] = charge[:, at]
    which = species[...]
    sigma = jnp.zeros((1, blocks), f32)
    eps = jnp.zeros((1, blocks), f32)
    for k in range(sigma_s.shape[0]):
        sigma = jnp.where(which == k, sigma_s[k], sigma)
        eps = jnp.where(which == k, eps_s[k], eps)
    depth_row = jnp.sqrt(eps)
    tow[blocks] = jnp.zeros((4, width), f32)
    tow[blocks, 0:1, 0:blocks] = sigma
    tow[blocks, 1:2, 0:blocks] = depth_row
    near0[2 * blocks : pitch, :] = jnp.zeros((8, width), f32)
    near0[2 * blocks : 2 * blocks + 1, 0:blocks] = sigma
    near0[2 * blocks + 1 : 2 * blocks + 2, 0:blocks] = depth_row
    low = lax.broadcasted_iota(jnp.int32, (blocks, width), 1) < part
    comp = [dense[r * blocks : (r + 1) * blocks, :] for r in range(4)]
    turned = [pltpu.roll(v, part, 1) for v in comp]
    near0[0:blocks, :] = jnp.where(low, comp[0], turned[1])
    near0[blocks : 2 * blocks, :] = jnp.where(low, comp[2], turned[3])
    near1[0:blocks, :] = jnp.where(low, turned[0], comp[1])
    near1[blocks : 2 * blocks, :] = jnp.where(low, turned[2], comp[3])

    pl.semaphore_wait(barrier, slots.count - 1)

    def send(src, dst, ss, rs, s):
        copy = pltpu.make_async_remote_copy(
            src_ref=src, dst_ref=dst, send_sem=ss, recv_sem=rs, device_id=slots.device(s), device_id_type=MESH
        )
        copy.start()
        return copy

    def send_cells(source, landing, ss, rs):
        copies = []
        for s in range(nz, slots.count):
            here, there = slots.cell_number(s), slots.cell_number(slots.opposite(s))
            copies.append(send(source(here), landing(there), ss.at[here], rs.at[there], s))
        return copies

    def rows_of(ref, size):
        return lambda c: ref.at[c * pitch : c * pitch + size]

    above = []
    for s in range(1, nz):
        there = slots.opposite(s) * (blocks + 1)
        above.append(
            send(tow.at[0 : blocks + 1], tow.at[there : there + blocks + 1], tow_s.at[s], tow_r.at[slots.opposite(s)], s)
        )
    first = send_cells(lambda c: near0.at[0:pitch], rows_of(near0, pitch), n0_s, n0_r)
    second = send_cells(lambda c: near1.at[0 : 2 * blocks], rows_of(near1, 2 * blocks), n1_s, n1_r)

    bit = jnp.left_shift(1, lax.broadcasted_iota(jnp.int32, (8, width), 0))
    term = lax.broadcasted_iota(jnp.int32, (TERMS, width), 0)
    early = jnp.where(term < 3, -1.0, 0.0)
    late = jnp.where((term >= 3) & (term < 6), -1.0, 0.0)
    shifted = jnp.where(term == 12, 0.5, early)
    plain = (early, late, shifted, early, jnp.zeros((TERMS, width), f32), shifted)
    ones = jnp.where((term >= 9) & (term < 13), 1.0, 0.0)
    for copy in fetches[8:]:
        copy.wait()

    def expand(k, carry):
        for w in range(words):
            hit = excl[0, k, w : w + 1, :] & bit
            allowed[pl.ds(pl.multiple_of(k * width + w * 8, 8), 8), :] = jnp.where(hit == 0, edge, -1.0)
        at = pl.ds(pl.multiple_of(k * TERMS, TERMS), TERMS)
        for g in range(6):
            at_g = pl.ds(pl.multiple_of((g * pairs + k) * TERMS, TERMS), TERMS)
            right[at_g, :] = plain[g]
        left0[at, :] = ones
        left1[at, :] = ones
        return carry

    lax.fori_loop(0, pairs, expand, 0)
    for c in range(HALVES):
        plate_sum[c][...] = jnp.zeros(plate_sum[c].shape, f32)
    half = vel[...] + 0.5 * time_step * fold[...] * mass[...]
    moved = pos[...] + time_step * half
    for b in range(blocks):
        at = slice(b * width, (b + 1) * width)
        half_b[b] = half[:, at]
        moved_b[b] = moved[:, at]
        mass_b[b] = mass[:, at]
    for q in range(mig_block.shape[1]):
        at = slice(q * width, (q + 1) * width)
        going_m[0:3, at] = moved_b[mig_block[0, q]]
        going_m[3:4, at] = jnp.full((1, width), mig_dest[0, q], jnp.int32).astype(f32)
    going_v[...] = jnp.zeros(going_v.shape, f32)
    come_m[0] = going_m[...]
    leavers = send_cells(lambda s: going_m, lambda s: come_m.at[s], mm_s, mm_r)
    block_of = lax.broadcasted_iota(jnp.int32, pos.shape, 1) // width
    gone = block_of == mig_block[0, 0]
    for q in range(1, mig_block.shape[1]):
        gone = gone | (block_of == mig_block[0, q])
    pos_out[...] = jnp.where(gone, 0.0, moved)
    stores = [pltpu.make_async_copy(pos_out, pos_out_h, local_sem.at[16])]
    stores[0].start()

    my_layer = lax.axis_index("gz")
    t_all = tower_v[...]
    p_all = plate_v[...]
    live = lax.broadcasted_iota(jnp.int32, (1, pairs), 1) < counts[0, 0]
    t_layer = t_all // blocks
    t_turn = t_layer - my_layer
    t_turn = jnp.where(t_turn < 0, t_turn + nz, t_turn)
    t_block = t_all - t_layer * blocks
    t_flat[...] = t_turn * (blocks + 1) + t_block
    t_row = jnp.where(live, t_turn * blocks + t_block, -1)
    p_cell = p_all // blocks
    p_number = jnp.zeros((1, pairs), jnp.int32)
    for o in range(9):
        number = slots.cell_number(slots.cell_slot(o // 3 - 1, o % 3 - 1))
        p_number = jnp.where(p_cell == o, number, p_number)
    p_block = p_all - p_cell * blocks
    p_flat[...] = p_number * pitch + p_block
    p_row = jnp.where(live, p_number * blocks + p_block, -1)
    tables = []
    for src, dst in ((t_flat, tower), (p_flat, plate)):
        tables.append(pltpu.make_async_copy(src, dst, local_sem.at[14 + len(tables)]))
        tables[-1].start()
    t_pick = jnp.where(
        lax.broadcasted_iota(jnp.int32, (nz * blocks, pairs), 0) == t_row, 1.0, 0.0
    ).astype(bf16)
    p_pick = jnp.where(
        lax.broadcasted_iota(jnp.int32, (cells * blocks, pairs), 0) == p_row, 1.0, 0.0
    ).astype(bf16)
    same = lax.broadcasted_iota(jnp.int32, (pairs, pairs), 0) == lax.broadcasted_iota(jnp.int32, (pairs, pairs), 1)
    t_col = jnp.sum(jnp.where(same, (t_turn * blocks + t_block).astype(f32), 0.0), axis=1, keepdims=True)
    p_col = jnp.sum(jnp.where(same, (p_number * blocks + p_block).astype(f32), 0.0), axis=1, keepdims=True)

    for copy in tables:
        copy.wait()
    for copy in above:
        copy.wait()

    lane_f = lax.broadcasted_iota(jnp.int32, (pairs, width), 1).astype(f32)

    def of_block(column, rows):
        found = jnp.zeros((pairs, width), f32)
        for s, row in enumerate(rows):
            found = found + jnp.where(lane_f == column - float(s * blocks), row, 0.0)
        return jnp.sum(found, axis=1, keepdims=True)

    sig_t = of_block(t_col, [tow[s * (blocks + 1) + blocks, 0:1, :] for s in range(nz)])
    dep_t = of_block(t_col, [tow[s * (blocks + 1) + blocks, 1:2, :] for s in range(nz)])
    def collect_towers(i, carry):
        for u in range(0, 16, 2):
            two = [tow[tower[0, i * 16 + u + v]] for v in range(2)]
            towers[pl.ds(pl.multiple_of(i * 64 + u * 4, 8), 8), :] = jnp.concatenate(two, axis=0)
        return carry

    lax.fori_loop(0, pairs // 16, collect_towers, 0)
    for r, groups in ((0, (0, 2)), (2, (1,)), (1, (3, 5)), (3, (4,))):
        terms = ((3, 4, 5), (6, 8), (7,)) if r == 3 else ((9,), (10,), (11,))
        for value, places in zip(split3(towers[pl.ds(r, pairs, stride=4), :]), terms):
            for t in places:
                for g in groups:
                    right[pl.ds(g * pairs * TERMS + t, pairs, stride=TERMS), :] = value
    for copy in first:
        copy.wait()
    sig_p = of_block(p_col, [near0[c * pitch + 2 * blocks : c * pitch + 2 * blocks + 1, :] for c in range(cells)])
    dep_p = of_block(p_col, [near0[c * pitch + 2 * blocks + 1 : c * pitch + 2 * blocks + 2, :] for c in range(cells)])
    sig = 0.5 * (sig_t + sig_p)
    sig2 = sig * sig
    sig6 = sig2 * sig2 * sig2
    depth = dep_t * dep_p
    att_tab[...] = jnp.broadcast_to((0.5 * lx**6) / sig6, (pairs, width))
    rep_col = (12.0 * scale / lx**12) * depth * sig6 * sig6
    rep_row = jnp.sum(jnp.where(same, rep_col, 0.0), axis=0, keepdims=True)
    charge_lanes = lax.broadcasted_iota(jnp.int32, (pairs, width), 1) >= part
    charge_scale = jnp.where(charge_lanes, 1.0 / rep_col, 1.0)

    def collect_plates(c):
        def body(i, carry):
            for u in range(16):
                p = plate[0, i * 16 + u]
                plates[i * 16 + u] = near[c][p]
                plates[pairs + i * 16 + u] = near[c][p + blocks]
            return carry

        lax.fori_loop(0, pairs // 16, body, 0)
        for r, terms in ((0, ((0,), (1,), (2,))), (1, ((3, 6, 7), (4, 8), (5,)))):
            rows = plates[r * pairs : (r + 1) * pairs, :]
            for value, places in zip(split3(rows * charge_scale if r else rows), terms):
                for t in places:
                    left[c][pl.ds(t, pairs, stride=TERMS), :] = value

    collect_plates(0)

    lane = lax.broadcasted_iota(jnp.int32, (8, pairs), 1)

    def prepare(k, c, made):
        at = pl.ds(pl.multiple_of(k * TERMS, TERMS), TERMS)
        a = left[c][at, :].T
        b = [right[pl.ds(pl.multiple_of((g * pairs + k) * TERMS, TERMS), TERMS), :].astype(bf16) for g in range(6)]
        for i in range(2):
            made[:, 3 * i * width : 3 * (i + 1) * width] = jnp.dot(
                a[i * part : (i + 1) * part].astype(bf16),
                jnp.concatenate(b[3 * i : 3 * (i + 1)], axis=1),
                preferred_element_type=f32,
            )

    def arithmetic(k, c, made):
        att = att_tab[pl.ds(k, 1), :]
        here = lane == k
        sums = [None, None, None]
        for w in range(part // 8):
            at = slice(w * 8, (w + 1) * 8)
            dx = made[at, 0:width] - jnp.floor(made[at, 2 * width : 3 * width])
            dz = made[at, width : 2 * width]
            dy = made[at, 3 * width : 4 * width] - jnp.floor(made[at, 5 * width : 6 * width])
            h = (dx * dx + dz * dz) + (ratio * (dy * dy) + shift_h)
            q = lax.rsqrt(h)
            f = jnp.maximum(allowed[pl.ds(pl.multiple_of(k * width + (c * part + w * 8), 8), 8), :] - h, 0.0)
            s = pl.reciprocal(h, approx=True)
            s3 = s * s * s
            fq = f * q
            g = fq * fq
            e = s3 * (s3 - att) + made[at, 4 * width : 5 * width] * q
            force_c = e * g
            parts = (force_c * dx, force_c * dy, force_c * dz)
            sums = [v if u is None else u + v for u, v in zip(sums, parts)]
            for r in range(3):
                total = jnp.broadcast_to(jnp.sum(parts[r], axis=1, keepdims=True), (8, pairs))
                pltpu.store(plate_sum[c].at[r * part + w * 8 : r * part + (w + 1) * 8, :], total, mask=here)
        for r in range(3):
            total = jnp.sum(sums[r], axis=0, keepdims=True)
            at = pl.ds(r * pairs + k, 1)
            tower_sum[at, :] = total if c == 0 else tower_sum[at, :] + total

    def run(c):
        for u in range(UNROLL):
            prepare(u, c, made_a.at[u])

        def step(i, carry):
            k = i * (2 * UNROLL)
            for u in range(UNROLL):
                prepare(k + UNROLL + u, c, made_b.at[u])
                arithmetic(k + u, c, made_a.at[u])
            for u in range(UNROLL):
                prepare(lax.rem(k + 2 * UNROLL + u, pairs), c, made_a.at[u])
                arithmetic(k + UNROLL + u, c, made_b.at[u])
            return carry

        lax.fori_loop(0, pairs // (2 * UNROLL), step, 0)
        total = jnp.zeros((cells * blocks, 4 * part), f32)
        for piece in split2(plate_sum[c][...] * rep_row):
            total = total + lax.dot_general(p_pick, piece, (((1,), (1,)), ((), ())), preferred_element_type=f32)
        for s in range(cells):
            mine = total[s * blocks : (s + 1) * blocks]
            out_p[c][s, 0:blocks, :] = mine[:, 0:width]
            last = mine[:, width:]
            out_p[c][s, blocks:, :] = last[0 : blocks // 2] + pltpu.roll(last[blocks // 2 :], part, 1)
        return send_cells(lambda s: out_p[c].at[s], lambda s: land_p[c].at[s], (r0_s, r1_s)[c], (r0_r, r1_r)[c])

    returns = run(0)
    for copy in second:
        copy.wait()
    collect_plates(1)
    returns += run(1)
    for r in range(3):
        total = jnp.zeros((nz * blocks, width), f32)
        for piece in split2(tower_sum[r * pairs : (r + 1) * pairs, :] * rep_col):
            total = total + jnp.dot(t_pick, piece, preferred_element_type=f32)
        for s in range(nz):
            out_t[s, :, r * width : (r + 1) * width] = total[s * blocks : (s + 1) * blocks]
    for s in range(1, nz):
        there = slots.opposite(s)
        returns.append(send(out_t.at[s], land_t.at[there], rt_s.at[s], rt_r.at[there], s))
    for copy in returns:
        copy.wait()

    back = []
    for c in range(HALVES):
        total = out_p[c][0]
        for s in range(1, cells):
            total = total + land_p[c][s]
        back.append(total)
    on_tower = out_t[0]
    for s in range(1, nz):
        on_tower = on_tower + land_t[s]
    (a0, a1), (z0, z1) = [v[0:blocks] for v in back], [v[blocks:] for v in back]
    low_z = low[0 : blocks // 2]
    on_plate = (
        jnp.where(low, a0, pltpu.roll(a1, part, 1)),
        jnp.where(low, pltpu.roll(a0, part, 1), a1),
        jnp.concatenate(
            [jnp.where(low_z, z0, pltpu.roll(z1, part, 1)), jnp.where(low_z, pltpu.roll(z0, part, 1), z1)], axis=0
        ),
    )
    for r in range(3):
        force[r] = (on_tower[:, r * width : (r + 1) * width] - on_plate[r]) * lengths[r]
    for q in range(mig_block.shape[1]):
        at = slice(q * width, (q + 1) * width)
        block = mig_block[0, q]
        kick = 0.5 * time_step * mass_b[block]
        old = half_b[block]
        for r in range(3):
            going_v[r : r + 1, at] = old[r : r + 1] + kick * force[r, block][None, :]
    come_v[0] = going_v[...]
    last_hop = send_cells(lambda s: going_v, lambda s: come_v.at[s], mv_s, mv_r)
    for r in range(3):
        for b in range(blocks):
            force_out[r : r + 1, b * width : (b + 1) * width] = force[r, b : b + 1]
    stores.append(pltpu.make_async_copy(force_out, force_out_h, local_sem.at[17]))
    stores[-1].start()
    half = vel[...] + 0.5 * time_step * fold[...] * mass[...]
    block_of = lax.broadcasted_iota(jnp.int32, pos.shape, 1) // width
    gone = block_of == mig_block[0, 0]
    for q in range(1, mig_block.shape[1]):
        gone = gone | (block_of == mig_block[0, q])
    vel_out[...] = jnp.where(gone, 0.0, half + 0.5 * time_step * force_out[...] * mass[...])
    stores.append(pltpu.make_async_copy(vel_out, vel_out_h, local_sem.at[18]))
    stores[-1].start()
    for copy in leavers:
        copy.wait()
    wanted = []
    for i, (a, b) in enumerate(source_offsets):
        cell = slots.cell_number(slots.cell_slot(a, b))
        wanted.append((cell, come_m[cell, 3:4, :] == float((1 - a) * 3 + (1 - b))))
        for r in range(3):
            arrive[r, 0, i : i + 1, :] = jnp.where(wanted[i][1], come_m[cell, r : r + 1, :], 0.0)
    for copy in last_hop:
        copy.wait()
    for i, (cell, chosen) in enumerate(wanted):
        for r in range(3):
            arrive[3 + r, 0, i : i + 1, :] = jnp.where(chosen, come_v[cell, r : r + 1, :], 0.0)
    stores.append(pltpu.make_async_copy(arrive, arrive_h, local_sem.at[19]))
    stores[-1].start()
    for copy in stores:
        copy.wait()


def output_kernel(a, b, c, d, a_out, b_out, c_out, d_out, sem):
    copies = [
        pltpu.make_async_copy(src, dst, sem.at[i])
        for i, (src, dst) in enumerate(((a, a_out), (b, b_out), (c, c_out), (d, d_out)))
    ]
    for copy in copies:
        copy.start()
    for copy in copies:
        copy.wait()


def local(
    slots, positions, velocities, forces_old, inv_mass, charges, block_species, sigma_table, epsilon_table,
    tower_index, plate_index, tile_counts, exclusions, mig_block, mig_dest,
):
    atoms = positions.shape[1]
    blocks = block_species.shape[0]
    width = atoms // blocks
    nz, cells = slots.nz, slots.cells
    pairs = tower_index.shape[1]
    leaving = mig_block.shape[1]
    kinds = sigma_table.shape[0]
    part = width // HALVES
    pitch = 2 * blocks + 8
    any_spec = pl.BlockSpec(memory_space=pl.ANY)
    mass = inv_mass[None, :]
    f32, i32 = jnp.float32, jnp.int32

    def sems(n):
        return pltpu.SemaphoreType.DMA((n,))

    def v(*shape):
        return pltpu.VMEM(shape, f32)

    rows = jax.ShapeDtypeStruct((3, atoms), f32)
    arrive = jax.ShapeDtypeStruct((6, 1, len(source_offsets), leaving * width), f32)
    made = pl.pallas_call(
        functools.partial(step_kernel, slots, blocks),
        out_shape=(rows, rows, rows, arrive),
        in_specs=[any_spec] * 14,
        out_specs=(any_spec,) * 4,
        scratch_shapes=[
            v(3, atoms), v(3, atoms), v(3, atoms), v(1, atoms), v(1, atoms), pltpu.VMEM((1, blocks), i32),
            pltpu.SMEM((kinds,), f32), pltpu.SMEM((kinds,), f32),
            pltpu.SMEM((1, pairs), i32), pltpu.SMEM((1, pairs), i32),
            pltpu.VMEM((1, pairs), i32), pltpu.VMEM((1, pairs), i32),
            pltpu.SMEM((1, 1), i32), pltpu.VMEM(exclusions.shape, i32),
            pltpu.SMEM((1, leaving), i32), pltpu.SMEM((1, leaving), i32),
            v(blocks, 3, width), v(blocks, 3, width), v(blocks, 1, width), v(4 * blocks, width), v(nz * (blocks + 1), 4, width),
            v(cells * pitch, width), v(cells * pitch, width),
            v(pairs * width, width), v(pairs, width), v(4 * pairs, width), v(2 * pairs, width),
            v(6 * pairs * TERMS, width), v(pairs * TERMS, width), v(pairs * TERMS, width),
            v(UNROLL, part, 6 * width), v(UNROLL, part, 6 * width), v(3 * pairs, width), v(4 * part, pairs), v(4 * part, pairs),
            v(nz, blocks, 3 * width), v(cells, blocks + blocks // 2, width), v(cells, blocks + blocks // 2, width),
            v(nz, blocks, 3 * width), v(cells, blocks + blocks // 2, width), v(cells, blocks + blocks // 2, width),
            v(4, leaving * width), v(4, leaving * width), v(cells, 4, leaving * width), v(cells, 4, leaving * width),
            v(3, blocks, width), v(3, atoms), v(3, atoms), v(3, atoms), v(6, 1, len(source_offsets), leaving * width),
            pltpu.VMEM((1, pairs), i32), pltpu.VMEM((1, pairs), i32), sems(20),
        ]
        + [sems(nz)] * 2 + [sems(cells)] * 4 + [sems(nz)] * 2 + [sems(cells)] * 8,
        compiler_params=pltpu.CompilerParams(
            collective_id=0, has_side_effects=True, vmem_limit_bytes=60 * 1024 * 1024
        ),
        name="membrane_step",
    )(
        positions, velocities, forces_old, mass, charges[None, :], block_species[None, :], sigma_table,
        epsilon_table, tower_index, plate_index, tile_counts[None, :], exclusions, mig_block, mig_dest,
    )
    return pl.pallas_call(
        output_kernel,
        out_shape=(rows, rows, rows, arrive),
        in_specs=[any_spec] * 4,
        out_specs=(any_spec,) * 4,
        scratch_shapes=[sems(4)],
        compiler_params=pltpu.CompilerParams(vmem_limit_bytes=60 * 1024 * 1024),
        name="outputs",
    )(*made)


def solution(mesh):
    cells = ("gx", "gy", "gz")
    slots = Slots(mesh.shape["gx"], mesh.shape["gy"], mesh.shape["gz"])
    row = P(None, cells)
    flat = P(cells)
    pair = P(cells, None)
    in_specs = (
        row, row, row, flat, flat, flat, P(), P(), pair, pair, flat, P(cells, None, None, None), pair, pair,
    )
    out_specs = (row, row, row, P(None, cells, None, None))
    return jax.shard_map(
        functools.partial(local, slots), mesh=mesh, in_specs=in_specs, out_specs=out_specs, check_vma=False
    )
```

```python
import functools
import jax
import jax.numpy as jnp
from jax import lax
from jax.experimental import pallas as pl
from jax.experimental.pallas import tpu as pltpu
from jax.sharding import PartitionSpec as P

time_step = 0.2
soft_core = 0.09
cutoff_sq = 1.44
coulomb_k = 0.5
MESH = pl.DeviceIdType.MESH
UNROLL = 4
HALVES = 2
TERMS = 16
source_offsets = ((-1, -1), (-1, 0), (-1, 1), (0, -1), (0, 1), (1, -1), (1, 0), (1, 1))


class Slots:
    def __init__(self, nx, ny, nz):
        self.nx, self.ny, self.nz = nx, ny, nz
        self.offsets = [(0, 0, 0)] + [(0, 0, k) for k in range(1, nz)]
        self.cell = {(0, 0): 0}
        for da in range(-1, 2):
            for db in range(-1, 2):
                key = (da % nx, db % ny)
                if key not in self.cell:
                    self.cell[key] = len(self.offsets)
                    self.offsets.append((key[0], key[1], 0))
        self.count = len(self.offsets)
        self.cells = 1 + self.count - nz

    def cell_slot(self, da, db):
        return self.cell[(da % self.nx, db % self.ny)]

    def cell_number(self, slot):
        return slot - self.nz + 1 if slot else 0

    def opposite(self, slot):
        dx, dy, dz = self.offsets[slot]
        if dz:
            return (self.nz - dz) % self.nz
        return self.cell_slot(-dx, -dy)

    def device(self, slot):
        dx, dy, dz = self.offsets[slot]
        return (
            lax.rem(lax.axis_index("gx") + dx, self.nx),
            lax.rem(lax.axis_index("gy") + dy, self.ny),
            lax.rem(lax.axis_index("gz") + dz, self.nz),
        )


def split3(value):
    high = value.astype(jnp.bfloat16).astype(jnp.float32)
    rest = value - high
    mid = rest.astype(jnp.bfloat16).astype(jnp.float32)
    return high, mid, rest - mid


def split2(value):
    high = value.astype(jnp.bfloat16)
    return high, (value - high.astype(jnp.float32)).astype(jnp.bfloat16)


def step_kernel(
    slots, blocks,
    pos_h, vel_h, fold_h, mass_h, charge_h, species_h, sigma_h, eps_h, tower_h, plate_h, counts_h, excl_h,
    mig_block_h, mig_dest_h,
    pos_out_h, vel_out_h, force_out_h, arrive_h,
    pos, vel, fold, mass, charge, species, sigma_s, eps_s, tower, plate, tower_v, plate_v, counts, excl,
    mig_block, mig_dest,
    half_b, moved_b, mass_b, dense, tow, near0, near1, allowed, att_tab, towers, plates, right, left0, left1,
    made_a, made_b, tower_sum, plate_sum0, plate_sum1, out_t, out_p0, out_p1, land_t, land_p0, land_p1, going_m, going_v, come_m, come_v,
    force, pos_out, vel_out, force_out, arrive,
    t_flat, p_flat, local_sem,
    tow_s, tow_r, n0_s, n0_r, n1_s, n1_r, rt_s, rt_r, r0_s, r0_r, r1_s, r1_r, mm_s, mm_r, mv_s, mv_r,
):
    atoms = pos.shape[1]
    width = atoms // blocks
    pairs = tower.shape[1]
    words = excl.shape[2]
    part = width // HALVES
    pitch = 2 * blocks + 8
    nx, ny, nz, cells = slots.nx, slots.ny, slots.nz, slots.cells
    lx, ly = float(nx), float(ny)
    lengths = (lx, ly, lx)
    f32 = jnp.float32
    bf16 = jnp.bfloat16
    near = (near0, near1)
    left = (left0, left1)
    plate_sum = (plate_sum0, plate_sum1)
    out_p = (out_p0, out_p1)
    land_p = (land_p0, land_p1)
    ratio = (ly / lx) ** 2
    shift_h = soft_core / (lx * lx)
    edge = (cutoff_sq + soft_core) / (lx * lx)
    scale = lx * lx / (cutoff_sq * cutoff_sq)

    barrier = pltpu.get_barrier_semaphore()
    for s in range(1, slots.count):
        pl.semaphore_signal(barrier, inc=1, device_id=slots.device(s), device_id_type=MESH)
    fetches = []
    for src, dst in (
        (pos_h, pos), (vel_h, vel), (fold_h, fold), (mass_h, mass), (charge_h, charge), (species_h, species),
        (sigma_h, sigma_s), (eps_h, eps_s), (excl_h, excl),
        (tower_h, tower_v), (plate_h, plate_v), (counts_h, counts), (mig_block_h, mig_block), (mig_dest_h, mig_dest),
    ):
        copy = pltpu.make_async_copy(src, dst, local_sem.at[len(fetches)])
        copy.start()
        fetches.append(copy)
    for copy in fetches[:8]:
        copy.wait()

    half = vel[...] + 0.5 * time_step * fold[...] * mass[...]
    moved = pos[...] + time_step * half
    row3 = lax.broadcasted_iota(jnp.int32, (3, atoms), 0)
    scaled = moved * jnp.where(row3 == 1, f32(1.0 / ly), f32(1.0 / lx))
    tower_charge = charge[...] * (coulomb_k * scale / lx)
    for b in range(blocks):
        at = slice(b * width, (b + 1) * width)
        tow[b, 0:3, :] = scaled[:, at]
        tow[b, 3:4, :] = tower_charge[:, at]
        for r in range(3):
            dense[r * blocks + b : r * blocks + b + 1, :] = scaled[r : r + 1, at]
        dense[3 * blocks + b : 3 * blocks + b + 1, :] = charge[:, at]
    which = species[...]
    sigma = jnp.zeros((1, blocks), f32)
    eps = jnp.zeros((1, blocks), f32)
    for k in range(sigma_s.shape[0]):
        sigma = jnp.where(which == k, sigma_s[k], sigma)
        eps = jnp.where(which == k, eps_s[k], eps)
    depth_row = jnp.sqrt(eps)
    tow[blocks] = jnp.zeros((4, width), f32)
    tow[blocks, 0:1, 0:blocks] = sigma
    tow[blocks, 1:2, 0:blocks] = depth_row
    near0[2 * blocks : pitch, :] = jnp.zeros((8, width), f32)
    near0[2 * blocks : 2 * blocks + 1, 0:blocks] = sigma
    near0[2 * blocks + 1 : 2 * blocks + 2, 0:blocks] = depth_row
    low = lax.broadcasted_iota(jnp.int32, (blocks, width), 1) < part
    comp = [dense[r * blocks : (r + 1) * blocks, :] for r in range(4)]
    turned = [pltpu.roll(v, part, 1) for v in comp]
    near0[0:blocks, :] = jnp.where(low, comp[0], turned[1])
    near0[blocks : 2 * blocks, :] = jnp.where(low, comp[2], turned[3])
    near1[0:blocks, :] = jnp.where(low, turned[0], comp[1])
    near1[blocks : 2 * blocks, :] = jnp.where(low, turned[2], comp[3])

    pl.semaphore_wait(barrier, slots.count - 1)

    def send(src, dst, ss, rs, s):
        copy = pltpu.make_async_remote_copy(
            src_ref=src, dst_ref=dst, send_sem=ss, recv_sem=rs, device_id=slots.device(s), device_id_type=MESH
        )
        copy.start()
        return copy

    def send_cells(source, landing, ss, rs):
        copies = []
        for s in range(nz, slots.count):
            here, there = slots.cell_number(s), slots.cell_number(slots.opposite(s))
            copies.append(send(source(here), landing(there), ss.at[here], rs.at[there], s))
        return copies

    def rows_of(ref, size):
        return lambda c: ref.at[c * pitch : c * pitch + size]

    above = []
    for s in range(1, nz):
        there = slots.opposite(s) * (blocks + 1)
        above.append(
            send(tow.at[0 : blocks + 1], tow.at[there : there + blocks + 1], tow_s.at[s], tow_r.at[slots.opposite(s)], s)
        )
    first = send_cells(lambda c: near0.at[0:pitch], rows_of(near0, pitch), n0_s, n0_r)
    second = send_cells(lambda c: near1.at[0 : 2 * blocks], rows_of(near1, 2 * blocks), n1_s, n1_r)

    bit = jnp.left_shift(1, lax.broadcasted_iota(jnp.int32, (8, width), 0))
    term = lax.broadcasted_iota(jnp.int32, (TERMS, width), 0)
    early = jnp.where(term < 3, -1.0, 0.0)
    late = jnp.where((term >= 3) & (term < 6), -1.0, 0.0)
    shifted = jnp.where(term == 12, 0.5, early)
    plain = (early, late, shifted, early, jnp.zeros((TERMS, width), f32), shifted)
    ones = jnp.where((term >= 9) & (term < 13), 1.0, 0.0)
    for copy in fetches[8:]:
        copy.wait()

    def expand(k, carry):
        for w in range(words):
            hit = excl[0, k, w : w + 1, :] & bit
            allowed[pl.ds(pl.multiple_of(k * width + w * 8, 8), 8), :] = jnp.where(hit == 0, edge, -1.0)
        at = pl.ds(pl.multiple_of(k * TERMS, TERMS), TERMS)
        for g in range(6):
            at_g = pl.ds(pl.multiple_of((g * pairs + k) * TERMS, TERMS), TERMS)
            right[at_g, :] = plain[g]
        left0[at, :] = ones
        left1[at, :] = ones
        return carry

    lax.fori_loop(0, pairs, expand, 0)
    for c in range(HALVES):
        plate_sum[c][...] = jnp.zeros(plate_sum[c].shape, f32)
    half = vel[...] + 0.5 * time_step * fold[...] * mass[...]
    moved = pos[...] + time_step * half
    for b in range(blocks):
        at = slice(b * width, (b + 1) * width)
        half_b[b] = half[:, at]
        moved_b[b] = moved[:, at]
        mass_b[b] = mass[:, at]
    for q in range(mig_block.shape[1]):
        at = slice(q * width, (q + 1) * width)
        going_m[0:3, at] = moved_b[mig_block[0, q]]
        going_m[3:4, at] = jnp.full((1, width), mig_dest[0, q], jnp.int32).astype(f32)
    going_v[...] = jnp.zeros(going_v.shape, f32)
    come_m[0] = going_m[...]
    leavers = send_cells(lambda s: going_m, lambda s: come_m.at[s], mm_s, mm_r)
    block_of = lax.broadcasted_iota(jnp.int32, pos.shape, 1) // width
    gone = block_of == mig_block[0, 0]
    for q in range(1, mig_block.shape[1]):
        gone = gone | (block_of == mig_block[0, q])
    pos_out[...] = jnp.where(gone, 0.0, moved)
    stores = [pltpu.make_async_copy(pos_out, pos_out_h, local_sem.at[16])]
    stores[0].start()

    my_layer = lax.axis_index("gz")
    t_all = tower_v[...]
    p_all = plate_v[...]
    live = lax.broadcasted_iota(jnp.int32, (1, pairs), 1) < counts[0, 0]
    t_layer = t_all // blocks
    t_turn = t_layer - my_layer
    t_turn = jnp.where(t_turn < 0, t_turn + nz, t_turn)
    t_block = t_all - t_layer * blocks
    t_flat[...] = t_turn * (blocks + 1) + t_block
    t_row = jnp.where(live, t_turn * blocks + t_block, -1)
    p_cell = p_all // blocks
    p_number = jnp.zeros((1, pairs), jnp.int32)
    for o in range(9):
        number = slots.cell_number(slots.cell_slot(o // 3 - 1, o % 3 - 1))
        p_number = jnp.where(p_cell == o, number, p_number)
    p_block = p_all - p_cell * blocks
    p_flat[...] = p_number * pitch + p_block
    p_row = jnp.where(live, p_number * blocks + p_block, -1)
    tables = []
    for src, dst in ((t_flat, tower), (p_flat, plate)):
        tables.append(pltpu.make_async_copy(src, dst, local_sem.at[14 + len(tables)]))
        tables[-1].start()
    t_pick = jnp.where(
        lax.broadcasted_iota(jnp.int32, (nz * blocks, pairs), 0) == t_row, 1.0, 0.0
    ).astype(bf16)
    p_pick = jnp.where(
        lax.broadcasted_iota(jnp.int32, (cells * blocks, pairs), 0) == p_row, 1.0, 0.0
    ).astype(bf16)
    same = lax.broadcasted_iota(jnp.int32, (pairs, pairs), 0) == lax.broadcasted_iota(jnp.int32, (pairs, pairs), 1)
    t_col = jnp.sum(jnp.where(same, (t_turn * blocks + t_block).astype(f32), 0.0), axis=1, keepdims=True)
    p_col = jnp.sum(jnp.where(same, (p_number * blocks + p_block).astype(f32), 0.0), axis=1, keepdims=True)

    for copy in tables:
        copy.wait()
    for copy in above:
        copy.wait()

    lane_f = lax.broadcasted_iota(jnp.int32, (pairs, width), 1).astype(f32)

    def of_block(column, rows):
        found = jnp.zeros((pairs, width), f32)
        for s, row in enumerate(rows):
            found = found + jnp.where(lane_f == column - float(s * blocks), row, 0.0)
        return jnp.sum(found, axis=1, keepdims=True)

    sig_t = of_block(t_col, [tow[s * (blocks + 1) + blocks, 0:1, :] for s in range(nz)])
    dep_t = of_block(t_col, [tow[s * (blocks + 1) + blocks, 1:2, :] for s in range(nz)])
    def collect_towers(i, carry):
        for u in range(0, 16, 2):
            two = [tow[tower[0, i * 16 + u + v]] for v in range(2)]
            towers[pl.ds(pl.multiple_of(i * 64 + u * 4, 8), 8), :] = jnp.concatenate(two, axis=0)
        return carry

    lax.fori_loop(0, pairs // 16, collect_towers, 0)
    for r, groups in ((0, (0, 2)), (2, (1,)), (1, (3, 5)), (3, (4,))):
        terms = ((3, 4, 5), (6, 8), (7,)) if r == 3 else ((9,), (10,), (11,))
        for value, places in zip(split3(towers[pl.ds(r, pairs, stride=4), :]), terms):
            for t in places:
                for g in groups:
                    right[pl.ds(g * pairs * TERMS + t, pairs, stride=TERMS), :] = value
    for copy in first:
        copy.wait()
    sig_p = of_block(p_col, [near0[c * pitch + 2 * blocks : c * pitch + 2 * blocks + 1, :] for c in range(cells)])
    dep_p = of_block(p_col, [near0[c * pitch + 2 * blocks + 1 : c * pitch + 2 * blocks + 2, :] for c in range(cells)])
    sig = 0.5 * (sig_t + sig_p)
    sig2 = sig * sig
    sig6 = sig2 * sig2 * sig2
    depth = dep_t * dep_p
    att_tab[...] = jnp.broadcast_to((0.5 * lx**6) / sig6, (pairs, width))
    rep_col = (12.0 * scale / lx**12) * depth * sig6 * sig6
    rep_row = jnp.sum(jnp.where(same, rep_col, 0.0), axis=0, keepdims=True)
    charge_lanes = lax.broadcasted_iota(jnp.int32, (pairs, width), 1) >= part
    charge_scale = jnp.where(charge_lanes, 1.0 / rep_col, 1.0)

    def collect_plates(c):
        def body(i, carry):
            for u in range(16):
                p = plate[0, i * 16 + u]
                plates[i * 16 + u] = near[c][p]
                plates[pairs + i * 16 + u] = near[c][p + blocks]
            return carry

        lax.fori_loop(0, pairs // 16, body, 0)
        for r, terms in ((0, ((0,), (1,), (2,))), (1, ((3, 6, 7), (4, 8), (5,)))):
            rows = plates[r * pairs : (r + 1) * pairs, :]
            for value, places in zip(split3(rows * charge_scale if r else rows), terms):
                for t in places:
                    left[c][pl.ds(t, pairs, stride=TERMS), :] = value

    collect_plates(0)

    lane = lax.broadcasted_iota(jnp.int32, (8, pairs), 1)

    def prepare(k, c, made):
        at = pl.ds(pl.multiple_of(k * TERMS, TERMS), TERMS)
        a = left[c][at, :].T
        b = [right[pl.ds(pl.multiple_of((g * pairs + k) * TERMS, TERMS), TERMS), :].astype(bf16) for g in range(6)]
        for i in range(2):
            made[:, 3 * i * width : 3 * (i + 1) * width] = jnp.dot(
                a[i * part : (i + 1) * part].astype(bf16),
                jnp.concatenate(b[3 * i : 3 * (i + 1)], axis=1),
                preferred_element_type=f32,
            )

    def arithmetic(k, c, made):
        att = att_tab[pl.ds(k, 1), :]
        here = lane == k
        sums = [None, None, None]
        for w in range(part // 8):
            at = slice(w * 8, (w + 1) * 8)
            dx = made[at, 0:width] - jnp.floor(made[at, 2 * width : 3 * width])
            dz = made[at, width : 2 * width]
            dy = made[at, 3 * width : 4 * width] - jnp.floor(made[at, 5 * width : 6 * width])
            h = (dx * dx + dz * dz) + (ratio * (dy * dy) + shift_h)
            q = lax.rsqrt(h)
            f = jnp.maximum(allowed[pl.ds(pl.multiple_of(k * width + (c * part + w * 8), 8), 8), :] - h, 0.0)
            s = pl.reciprocal(h, approx=True)
            s3 = s * s * s
            fq = f * q
            g = fq * fq
            e = s3 * (s3 - att) + made[at, 4 * width : 5 * width] * q
            force_c = e * g
            parts = (force_c * dx, force_c * dy, force_c * dz)
            sums = [v if u is None else u + v for u, v in zip(sums, parts)]
            for r in range(3):
                total = jnp.broadcast_to(jnp.sum(parts[r], axis=1, keepdims=True), (8, pairs))
                pltpu.store(plate_sum[c].at[r * part + w * 8 : r * part + (w + 1) * 8, :], total, mask=here)
        for r in range(3):
            total = jnp.sum(sums[r], axis=0, keepdims=True)
            at = pl.ds(r * pairs + k, 1)
            tower_sum[at, :] = total if c == 0 else tower_sum[at, :] + total

    def run(c):
        for u in range(UNROLL):
            prepare(u, c, made_a.at[u])

        def step(i, carry):
            k = i * (2 * UNROLL)
            for u in range(UNROLL):
                prepare(k + UNROLL + u, c, made_b.at[u])
                arithmetic(k + u, c, made_a.at[u])
            for u in range(UNROLL):
                prepare(lax.rem(k + 2 * UNROLL + u, pairs), c, made_a.at[u])
                arithmetic(k + UNROLL + u, c, made_b.at[u])
            return carry

        lax.fori_loop(0, pairs // (2 * UNROLL), step, 0)
        total = jnp.zeros((cells * blocks, 4 * part), f32)
        for piece in split2(plate_sum[c][...] * rep_row):
            total = total + lax.dot_general(p_pick, piece, (((1,), (1,)), ((), ())), preferred_element_type=f32)
        for s in range(cells):
            mine = total[s * blocks : (s + 1) * blocks]
            out_p[c][s, 0:blocks, :] = mine[:, 0:width]
            last = mine[:, width:]
            out_p[c][s, blocks:, :] = last[0 : blocks // 2] + pltpu.roll(last[blocks // 2 :], part, 1)
        return send_cells(lambda s: out_p[c].at[s], lambda s: land_p[c].at[s], (r0_s, r1_s)[c], (r0_r, r1_r)[c])

    returns = run(0)
    for copy in second:
        copy.wait()
    collect_plates(1)
    returns += run(1)
    for r in range(3):
        total = jnp.zeros((nz * blocks, width), f32)
        for piece in split2(tower_sum[r * pairs : (r + 1) * pairs, :] * rep_col):
            total = total + jnp.dot(t_pick, piece, preferred_element_type=f32)
        for s in range(nz):
            out_t[s, :, r * width : (r + 1) * width] = total[s * blocks : (s + 1) * blocks]
    for s in range(1, nz):
        there = slots.opposite(s)
        returns.append(send(out_t.at[s], land_t.at[there], rt_s.at[s], rt_r.at[there], s))
    for copy in returns:
        copy.wait()

    back = []
    for c in range(HALVES):
        total = out_p[c][0]
        for s in range(1, cells):
            total = total + land_p[c][s]
        back.append(total)
    on_tower = out_t[0]
    for s in range(1, nz):
        on_tower = on_tower + land_t[s]
    (a0, a1), (z0, z1) = [v[0:blocks] for v in back], [v[blocks:] for v in back]
    low_z = low[0 : blocks // 2]
    on_plate = (
        jnp.where(low, a0, pltpu.roll(a1, part, 1)),
        jnp.where(low, pltpu.roll(a0, part, 1), a1),
        jnp.concatenate(
            [jnp.where(low_z, z0, pltpu.roll(z1, part, 1)), jnp.where(low_z, pltpu.roll(z0, part, 1), z1)], axis=0
        ),
    )
    for r in range(3):
        force[r] = (on_tower[:, r * width : (r + 1) * width] - on_plate[r]) * lengths[r]
    for q in range(mig_block.shape[1]):
        at = slice(q * width, (q + 1) * width)
        block = mig_block[0, q]
        kick = 0.5 * time_step * mass_b[block]
        old = half_b[block]
        for r in range(3):
            going_v[r : r + 1, at] = old[r : r + 1] + kick * force[r, block][None, :]
    come_v[0] = going_v[...]
    last_hop = send_cells(lambda s: going_v, lambda s: come_v.at[s], mv_s, mv_r)
    for r in range(3):
        for b in range(blocks):
            force_out[r : r + 1, b * width : (b + 1) * width] = force[r, b : b + 1]
    stores.append(pltpu.make_async_copy(force_out, force_out_h, local_sem.at[17]))
    stores[-1].start()
    half = vel[...] + 0.5 * time_step * fold[...] * mass[...]
    block_of = lax.broadcasted_iota(jnp.int32, pos.shape, 1) // width
    gone = block_of == mig_block[0, 0]
    for q in range(1, mig_block.shape[1]):
        gone = gone | (block_of == mig_block[0, q])
    vel_out[...] = jnp.where(gone, 0.0, half + 0.5 * time_step * force_out[...] * mass[...])
    stores.append(pltpu.make_async_copy(vel_out, vel_out_h, local_sem.at[18]))
    stores[-1].start()
    for copy in leavers:
        copy.wait()
    wanted = []
    for i, (a, b) in enumerate(source_offsets):
        cell = slots.cell_number(slots.cell_slot(a, b))
        wanted.append((cell, come_m[cell, 3:4, :] == float((1 - a) * 3 + (1 - b))))
        for r in range(3):
            arrive[r, 0, i : i + 1, :] = jnp.where(wanted[i][1], come_m[cell, r : r + 1, :], 0.0)
    for copy in last_hop:
        copy.wait()
    for i, (cell, chosen) in enumerate(wanted):
        for r in range(3):
            arrive[3 + r, 0, i : i + 1, :] = jnp.where(chosen, come_v[cell, r : r + 1, :], 0.0)
    stores.append(pltpu.make_async_copy(arrive, arrive_h, local_sem.at[19]))
    stores[-1].start()
    for copy in stores:
        copy.wait()


def output_kernel(*refs):
    sem = refs[-1]
    sources, results, held = refs[0:4], refs[4:8], refs[8:12]
    copies = []
    for i in range(4):
        copies.append(pltpu.make_async_copy(sources[i], held[i], sem.at[i]))
        copies[-1].start()
    for i in range(4):
        copies[i].wait()
        copies.append(pltpu.make_async_copy(held[i], results[i], sem.at[4 + i]))
        copies[-1].start()
    for copy in copies[4:]:
        copy.wait()


def local(
    slots, positions, velocities, forces_old, inv_mass, charges, block_species, sigma_table, epsilon_table,
    tower_index, plate_index, tile_counts, exclusions, mig_block, mig_dest,
):
    atoms = positions.shape[1]
    blocks = block_species.shape[0]
    width = atoms // blocks
    nz, cells = slots.nz, slots.cells
    pairs = tower_index.shape[1]
    leaving = mig_block.shape[1]
    kinds = sigma_table.shape[0]
    part = width // HALVES
    pitch = 2 * blocks + 8
    any_spec = pl.BlockSpec(memory_space=pl.ANY)
    mass = inv_mass[None, :]
    f32, i32 = jnp.float32, jnp.int32

    def sems(n):
        return pltpu.SemaphoreType.DMA((n,))

    def v(*shape):
        return pltpu.VMEM(shape, f32)

    rows = jax.ShapeDtypeStruct((3, atoms), f32)
    arrive = jax.ShapeDtypeStruct((6, 1, len(source_offsets), leaving * width), f32)
    made = pl.pallas_call(
        functools.partial(step_kernel, slots, blocks),
        out_shape=(rows, rows, rows, arrive),
        in_specs=[any_spec] * 14,
        out_specs=(any_spec,) * 4,
        scratch_shapes=[
            v(3, atoms), v(3, atoms), v(3, atoms), v(1, atoms), v(1, atoms), pltpu.VMEM((1, blocks), i32),
            pltpu.SMEM((kinds,), f32), pltpu.SMEM((kinds,), f32),
            pltpu.SMEM((1, pairs), i32), pltpu.SMEM((1, pairs), i32),
            pltpu.VMEM((1, pairs), i32), pltpu.VMEM((1, pairs), i32),
            pltpu.SMEM((1, 1), i32), pltpu.VMEM(exclusions.shape, i32),
            pltpu.SMEM((1, leaving), i32), pltpu.SMEM((1, leaving), i32),
            v(blocks, 3, width), v(blocks, 3, width), v(blocks, 1, width), v(4 * blocks, width), v(nz * (blocks + 1), 4, width),
            v(cells * pitch, width), v(cells * pitch, width),
            v(pairs * width, width), v(pairs, width), v(4 * pairs, width), v(2 * pairs, width),
            v(6 * pairs * TERMS, width), v(pairs * TERMS, width), v(pairs * TERMS, width),
            v(UNROLL, part, 6 * width), v(UNROLL, part, 6 * width), v(3 * pairs, width), v(4 * part, pairs), v(4 * part, pairs),
            v(nz, blocks, 3 * width), v(cells, blocks + blocks // 2, width), v(cells, blocks + blocks // 2, width),
            v(nz, blocks, 3 * width), v(cells, blocks + blocks // 2, width), v(cells, blocks + blocks // 2, width),
            v(4, leaving * width), v(4, leaving * width), v(cells, 4, leaving * width), v(cells, 4, leaving * width),
            v(3, blocks, width), v(3, atoms), v(3, atoms), v(3, atoms), v(6, 1, len(source_offsets), leaving * width),
            pltpu.VMEM((1, pairs), i32), pltpu.VMEM((1, pairs), i32), sems(20),
        ]
        + [sems(nz)] * 2 + [sems(cells)] * 4 + [sems(nz)] * 2 + [sems(cells)] * 8,
        compiler_params=pltpu.CompilerParams(
            collective_id=0, has_side_effects=True, vmem_limit_bytes=60 * 1024 * 1024
        ),
        name="membrane_step",
    )(
        positions, velocities, forces_old, mass, charges[None, :], block_species[None, :], sigma_table,
        epsilon_table, tower_index, plate_index, tile_counts[None, :], exclusions, mig_block, mig_dest,
    )
    return pl.pallas_call(
        output_kernel,
        out_shape=(rows, rows, rows, arrive),
        in_specs=[any_spec] * 4,
        out_specs=(any_spec,) * 4,
        scratch_shapes=[v(3, atoms), v(3, atoms), v(3, atoms), v(*arrive.shape), sems(8)],
        compiler_params=pltpu.CompilerParams(vmem_limit_bytes=60 * 1024 * 1024),
        name="outputs",
    )(*made)


def solution(mesh):
    cells = ("gx", "gy", "gz")
    slots = Slots(mesh.shape["gx"], mesh.shape["gy"], mesh.shape["gz"])
    row = P(None, cells)
    flat = P(cells)
    pair = P(cells, None)
    in_specs = (
        row, row, row, flat, flat, flat, P(), P(), pair, pair, flat, P(cells, None, None, None), pair, pair,
    )
    out_specs = (row, row, row, P(None, cells, None, None))
    return jax.shard_map(
        functools.partial(local, slots), mesh=mesh, in_specs=in_specs, out_specs=out_specs, check_vma=False
    )
```

```python
import functools
import jax
import jax.numpy as jnp
from jax import lax
from jax.experimental import pallas as pl
from jax.experimental.pallas import tpu as pltpu
from jax.sharding import PartitionSpec as P

time_step = 0.2
soft_core = 0.09
cutoff_sq = 1.44
coulomb_k = 0.5
MESH = pl.DeviceIdType.MESH
UNROLL = 4
HALVES = 2
TERMS = 16
source_offsets = ((-1, -1), (-1, 0), (-1, 1), (0, -1), (0, 1), (1, -1), (1, 0), (1, 1))


class Slots:
    def __init__(self, nx, ny, nz):
        self.nx, self.ny, self.nz = nx, ny, nz
        self.offsets = [(0, 0, 0)] + [(0, 0, k) for k in range(1, nz)]
        self.cell = {(0, 0): 0}
        for da in range(-1, 2):
            for db in range(-1, 2):
                key = (da % nx, db % ny)
                if key not in self.cell:
                    self.cell[key] = len(self.offsets)
                    self.offsets.append((key[0], key[1], 0))
        self.count = len(self.offsets)
        self.cells = 1 + self.count - nz

    def cell_slot(self, da, db):
        return self.cell[(da % self.nx, db % self.ny)]

    def cell_number(self, slot):
        return slot - self.nz + 1 if slot else 0

    def opposite(self, slot):
        dx, dy, dz = self.offsets[slot]
        if dz:
            return (self.nz - dz) % self.nz
        return self.cell_slot(-dx, -dy)

    def device(self, slot):
        dx, dy, dz = self.offsets[slot]
        return (
            lax.rem(lax.axis_index("gx") + dx, self.nx),
            lax.rem(lax.axis_index("gy") + dy, self.ny),
            lax.rem(lax.axis_index("gz") + dz, self.nz),
        )


def split3(value):
    high = value.astype(jnp.bfloat16).astype(jnp.float32)
    rest = value - high
    mid = rest.astype(jnp.bfloat16).astype(jnp.float32)
    return high, mid, rest - mid


def split2(value):
    high = value.astype(jnp.bfloat16)
    return high, (value - high.astype(jnp.float32)).astype(jnp.bfloat16)


def step_kernel(
    slots, blocks,
    pos_h, vel_h, fold_h, mass_h, charge_h, species_h, sigma_h, eps_h, tower_h, plate_h, counts_h, excl_h,
    mig_block_h, mig_dest_h,
    pos_out, vel_out, force_out, arrive,
    pos, vel, fold, mass, charge, species, sigma_s, eps_s, tower, plate, tower_v, plate_v, counts, excl,
    mig_block, mig_dest,
    half_b, moved_b, mass_b, dense, tow, kin, near0, near1, allowed, att_tab, towers, plates, right, right_b, left0, left1,
    made_a, made_b, tower_sum, plate_sum0, plate_sum1, out_t, out_p0, out_p1, land_t, land_p0, land_p1, going_m, going_v, come_m, come_v,
    force,
    t_flat, p_flat, local_sem,
    kn_s, kn_r, tow_s, tow_r, n0_s, n0_r, n1_s, n1_r, rt_s, rt_r, r0_s, r0_r, r1_s, r1_r, mm_s, mm_r, mv_s, mv_r,
):
    atoms = pos.shape[1]
    width = atoms // blocks
    pairs = tower.shape[1]
    words = excl.shape[2]
    part = width // HALVES
    pitch = 2 * blocks
    nx, ny, nz, cells = slots.nx, slots.ny, slots.nz, slots.cells
    lx, ly = float(nx), float(ny)
    lengths = (lx, ly, lx)
    f32 = jnp.float32
    bf16 = jnp.bfloat16
    near = (near0, near1)
    left = (left0, left1)
    plate_sum = (plate_sum0, plate_sum1)
    out_p = (out_p0, out_p1)
    land_p = (land_p0, land_p1)
    ratio = (ly / lx) ** 2
    shift_h = soft_core / (lx * lx)
    edge = (cutoff_sq + soft_core) / (lx * lx)
    scale = lx * lx / (cutoff_sq * cutoff_sq)

    barrier = pltpu.get_barrier_semaphore()
    for s in range(1, slots.count):
        pl.semaphore_signal(barrier, inc=1, device_id=slots.device(s), device_id_type=MESH)
    fetches = []
    for src, dst in (
        (pos_h, pos), (vel_h, vel), (fold_h, fold), (mass_h, mass), (charge_h, charge), (species_h, species),
        (sigma_h, sigma_s), (eps_h, eps_s), (excl_h, excl),
        (tower_h, tower_v), (plate_h, plate_v), (counts_h, counts), (mig_block_h, mig_block), (mig_dest_h, mig_dest),
    ):
        copy = pltpu.make_async_copy(src, dst, local_sem.at[len(fetches)])
        copy.start()
        fetches.append(copy)
    for copy in fetches[:8]:
        copy.wait()

    half = vel[...] + 0.5 * time_step * fold[...] * mass[...]
    moved = pos[...] + time_step * half
    row3 = lax.broadcasted_iota(jnp.int32, (3, atoms), 0)
    scaled = moved * jnp.where(row3 == 1, f32(1.0 / ly), f32(1.0 / lx))
    tower_charge = charge[...] * (coulomb_k * scale / lx)
    for b in range(blocks):
        at = slice(b * width, (b + 1) * width)
        tow[b, 0:3, :] = scaled[:, at]
        tow[b, 3:4, :] = tower_charge[:, at]
        for r in range(3):
            dense[r * blocks + b : r * blocks + b + 1, :] = scaled[r : r + 1, at]
        dense[3 * blocks + b : 3 * blocks + b + 1, :] = charge[:, at]
    which = species[...]
    sigma = jnp.zeros((1, blocks), f32)
    eps = jnp.zeros((1, blocks), f32)
    for k in range(sigma_s.shape[0]):
        sigma = jnp.where(which == k, sigma_s[k], sigma)
        eps = jnp.where(which == k, eps_s[k], eps)
    depth_row = jnp.sqrt(eps)
    tow[blocks] = jnp.zeros((4, width), f32)
    tow[blocks, 0:1, 0:blocks] = sigma
    tow[blocks, 1:2, 0:blocks] = depth_row
    kin[0:8, :] = jnp.zeros((8, width), f32)
    kin[0:1, 0:blocks] = sigma
    kin[1:2, 0:blocks] = depth_row
    low = lax.broadcasted_iota(jnp.int32, (blocks, width), 1) < part
    comp = [dense[r * blocks : (r + 1) * blocks, :] for r in range(4)]
    turned = [pltpu.roll(v, part, 1) for v in comp]
    near0[0:blocks, :] = jnp.where(low, comp[0], turned[1])
    near0[blocks : 2 * blocks, :] = jnp.where(low, comp[2], turned[3])
    near1[0:blocks, :] = jnp.where(low, turned[0], comp[1])
    near1[blocks : 2 * blocks, :] = jnp.where(low, turned[2], comp[3])

    pl.semaphore_wait(barrier, slots.count - 1)

    def send(src, dst, ss, rs, s):
        copy = pltpu.make_async_remote_copy(
            src_ref=src, dst_ref=dst, send_sem=ss, recv_sem=rs, device_id=slots.device(s), device_id_type=MESH
        )
        copy.start()
        return copy

    def send_cells(source, landing, ss, rs):
        copies = []
        for s in range(nz, slots.count):
            here, there = slots.cell_number(s), slots.cell_number(slots.opposite(s))
            copies.append(send(source(here), landing(there), ss.at[here], rs.at[there], s))
        return copies

    def rows_of(ref, size):
        return lambda c: ref.at[c * size : (c + 1) * size]

    named = send_cells(lambda c: kin.at[0:8], rows_of(kin, 8), kn_s, kn_r)
    above = []
    for s in range(1, nz):
        there = slots.opposite(s) * (blocks + 1)
        above.append(
            send(tow.at[0 : blocks + 1], tow.at[there : there + blocks + 1], tow_s.at[s], tow_r.at[slots.opposite(s)], s)
        )
    first = send_cells(lambda c: near0.at[0:pitch], rows_of(near0, pitch), n0_s, n0_r)
    second = send_cells(lambda c: near1.at[0:pitch], rows_of(near1, pitch), n1_s, n1_r)

    bit = jnp.left_shift(1, lax.broadcasted_iota(jnp.int32, (8, width), 0))
    term = lax.broadcasted_iota(jnp.int32, (TERMS, width), 0)
    early = jnp.where(term < 3, -1.0, 0.0)
    late = jnp.where((term >= 3) & (term < 6), -1.0, 0.0)
    shifted = jnp.where(term == 12, 0.5, early)
    ones = jnp.where((term >= 9) & (term < 13), 1.0, 0.0)
    plain = (early, late, shifted, early, jnp.zeros((TERMS, width), f32), shifted)
    for copy in fetches[8:]:
        copy.wait()

    def expand(k, carry):
        for w in range(words):
            hit = excl[0, k, w : w + 1, :] & bit
            allowed[pl.ds(pl.multiple_of(k * width + w * 8, 8), 8), :] = jnp.where(hit == 0, edge, -1.0)
        at = pl.ds(pl.multiple_of(k * TERMS, TERMS), TERMS)
        left0[at, :] = ones
        left1[at, :] = ones
        for g in range(6):
            at_g = pl.ds(pl.multiple_of((g * pairs + k) * TERMS, TERMS), TERMS)
            right[at_g, :] = plain[g]
        return carry

    lax.fori_loop(0, pairs, expand, 0)
    for c in range(HALVES):
        plate_sum[c][...] = jnp.zeros(plate_sum[c].shape, f32)
    half = vel[...] + 0.5 * time_step * fold[...] * mass[...]
    moved = pos[...] + time_step * half
    for b in range(blocks):
        at = slice(b * width, (b + 1) * width)
        half_b[b] = half[:, at]
        moved_b[b] = moved[:, at]
        mass_b[b] = mass[:, at]
    for q in range(mig_block.shape[1]):
        at = slice(q * width, (q + 1) * width)
        going_m[0:3, at] = moved_b[mig_block[0, q]]
        going_m[3:4, at] = jnp.full((1, width), mig_dest[0, q], jnp.int32).astype(f32)
    going_v[...] = jnp.zeros(going_v.shape, f32)
    come_m[0] = going_m[...]
    leavers = send_cells(lambda s: going_m, lambda s: come_m.at[s], mm_s, mm_r)
    block_of = lax.broadcasted_iota(jnp.int32, pos.shape, 1) // width
    gone = block_of == mig_block[0, 0]
    for q in range(1, mig_block.shape[1]):
        gone = gone | (block_of == mig_block[0, q])
    pos_out[...] = jnp.where(gone, 0.0, moved)

    my_layer = lax.axis_index("gz")
    t_all = tower_v[...]
    p_all = plate_v[...]
    live = lax.broadcasted_iota(jnp.int32, (1, pairs), 1) < counts[0]
    t_layer = t_all // blocks
    t_turn = t_layer - my_layer
    t_turn = jnp.where(t_turn < 0, t_turn + nz, t_turn)
    t_block = t_all - t_layer * blocks
    t_flat[...] = t_turn * (blocks + 1) + t_block
    t_row = jnp.where(live, t_turn * blocks + t_block, -1)
    p_cell = p_all // blocks
    p_number = jnp.zeros((1, pairs), jnp.int32)
    for o in range(9):
        number = slots.cell_number(slots.cell_slot(o // 3 - 1, o % 3 - 1))
        p_number = jnp.where(p_cell == o, number, p_number)
    p_block = p_all - p_cell * blocks
    p_flat[...] = p_number * pitch + p_block
    p_row = jnp.where(live, p_number * blocks + p_block, -1)
    tables = []
    for src, dst in ((t_flat, tower), (p_flat, plate)):
        tables.append(pltpu.make_async_copy(src, dst, local_sem.at[14 + len(tables)]))
        tables[-1].start()
    t_pick = jnp.where(
        lax.broadcasted_iota(jnp.int32, (nz * blocks, pairs), 0) == t_row, 1.0, 0.0
    ).astype(bf16)
    p_pick = jnp.where(
        lax.broadcasted_iota(jnp.int32, (cells * blocks, pairs), 0) == p_row, 1.0, 0.0
    ).astype(bf16)
    same = lax.broadcasted_iota(jnp.int32, (pairs, pairs), 0) == lax.broadcasted_iota(jnp.int32, (pairs, pairs), 1)
    t_col = jnp.sum(jnp.where(same, (t_turn * blocks + t_block).astype(f32), 0.0), axis=1, keepdims=True)
    p_col = jnp.sum(jnp.where(same, (p_number * blocks + p_block).astype(f32), 0.0), axis=1, keepdims=True)

    for copy in tables:
        copy.wait()
    for copy in above:
        copy.wait()

    lane_f = lax.broadcasted_iota(jnp.int32, (pairs, width), 1).astype(f32)

    def of_block(column, rows):
        found = jnp.zeros((pairs, width), f32)
        for s, row in enumerate(rows):
            found = found + jnp.where(lane_f == column - float(s * blocks), row, 0.0)
        return jnp.sum(found, axis=1, keepdims=True)

    sig_t = of_block(t_col, [tow[s * (blocks + 1) + blocks, 0:1, :] for s in range(nz)])
    dep_t = of_block(t_col, [tow[s * (blocks + 1) + blocks, 1:2, :] for s in range(nz)])
    def collect_towers(i, carry):
        for u in range(0, 16, 2):
            two = [tow[tower[0, i * 16 + u + v]] for v in range(2)]
            towers[pl.ds(pl.multiple_of(i * 64 + u * 4, 8), 8), :] = jnp.concatenate(two, axis=0)
        return carry

    lax.fori_loop(0, pairs // 16, collect_towers, 0)
    for r, groups in ((0, (0, 2)), (2, (1,)), (1, (3, 5)), (3, (4,))):
        terms = ((3, 4, 5), (6, 8), (7,)) if r == 3 else ((9,), (10,), (11,))
        for value, places in zip(split3(towers[pl.ds(r, pairs, stride=4), :]), terms):
            for t in places:
                for g in groups:
                    right[pl.ds(g * pairs * TERMS + t, pairs, stride=TERMS), :] = value
    def narrow(k, carry):
        row = pl.ds(pl.multiple_of(k * TERMS, TERMS), TERMS)
        for g in range(6):
            at = pl.ds(pl.multiple_of((g * pairs + k) * TERMS, TERMS), TERMS)
            right_b[row, g * width : (g + 1) * width] = right[at, :].astype(bf16)
        return carry

    lax.fori_loop(0, pairs, narrow, 0)
    for copy in named:
        copy.wait()
    sig_p = of_block(p_col, [kin[8 * c : 8 * c + 1, :] for c in range(cells)])
    dep_p = of_block(p_col, [kin[8 * c + 1 : 8 * c + 2, :] for c in range(cells)])
    sig = 0.5 * (sig_t + sig_p)
    sig2 = sig * sig
    sig6 = sig2 * sig2 * sig2
    depth = dep_t * dep_p
    att_tab[...] = jnp.broadcast_to((0.5 * lx**6) / sig6, (pairs, width))
    rep_col = (12.0 * scale / lx**12) * depth * sig6 * sig6
    rep_row = jnp.sum(jnp.where(same, rep_col, 0.0), axis=0, keepdims=True)
    charge_lanes = lax.broadcasted_iota(jnp.int32, (pairs, width), 1) >= part
    charge_scale = jnp.where(charge_lanes, 1.0 / rep_col, 1.0)

    def collect_plates(c):
        def body(i, carry):
            for u in range(16):
                p = plate[0, i * 16 + u]
                plates[i * 16 + u] = near[c][p]
                plates[pairs + i * 16 + u] = near[c][p + blocks]
            return carry

        lax.fori_loop(0, pairs // 16, body, 0)
        for r, terms in ((0, ((0,), (1,), (2,))), (1, ((3, 6, 7), (4, 8), (5,)))):
            rows = plates[r * pairs : (r + 1) * pairs, :]
            for value, places in zip(split3(rows * charge_scale if r else rows), terms):
                for t in places:
                    left[c][pl.ds(t, pairs, stride=TERMS), :] = value

    for copy in first:
        copy.wait()
    collect_plates(0)

    lane = lax.broadcasted_iota(jnp.int32, (8, pairs), 1)

    def prepare(k, c, made):
        at = pl.ds(pl.multiple_of(k * TERMS, TERMS), TERMS)
        a = left[c][at, :].T
        for i in range(2):
            made[:, 3 * i * width : 3 * (i + 1) * width] = jnp.dot(
                a[i * part : (i + 1) * part].astype(bf16),
                right_b[at, 3 * i * width : 3 * (i + 1) * width],
                preferred_element_type=f32,
            )

    def arithmetic(k, c, made):
        att = att_tab[pl.ds(k, 1), :]
        here = lane == k
        sums = [None, None, None]
        for w in range(part // 8):
            at = slice(w * 8, (w + 1) * 8)
            dx = made[at, 0:width] - jnp.floor(made[at, 2 * width : 3 * width])
            dz = made[at, width : 2 * width]
            dy = made[at, 3 * width : 4 * width] - jnp.floor(made[at, 5 * width : 6 * width])
            h = (dx * dx + dz * dz) + (ratio * (dy * dy) + shift_h)
            q = lax.rsqrt(h)
            f = jnp.maximum(allowed[pl.ds(pl.multiple_of(k * width + (c * part + w * 8), 8), 8), :] - h, 0.0)
            s = pl.reciprocal(h, approx=True)
            s3 = s * s * s
            fq = f * q
            g = fq * fq
            e = s3 * (s3 - att) + made[at, 4 * width : 5 * width] * q
            force_c = e * g
            parts = (force_c * dx, force_c * dy, force_c * dz)
            sums = [v if u is None else u + v for u, v in zip(sums, parts)]
            for r in range(3):
                total = jnp.broadcast_to(jnp.sum(parts[r], axis=1, keepdims=True), (8, pairs))
                pltpu.store(plate_sum[c].at[r * part + w * 8 : r * part + (w + 1) * 8, :], total, mask=here)
        for r in range(3):
            at = pl.ds(pl.multiple_of((r * pairs + k) * 8, 8), 8)
            tower_sum[at, :] = sums[r] if c == 0 else tower_sum[at, :] + sums[r]

    def run(c):
        for u in range(UNROLL):
            prepare(u, c, made_a.at[u])

        def step(i, carry):
            k = i * (2 * UNROLL)
            for u in range(UNROLL):
                prepare(k + UNROLL + u, c, made_b.at[u])
                arithmetic(k + u, c, made_a.at[u])
            for u in range(UNROLL):
                prepare(lax.rem(k + 2 * UNROLL + u, pairs), c, made_a.at[u])
                arithmetic(k + UNROLL + u, c, made_b.at[u])
            return carry

        lax.fori_loop(0, pairs // (2 * UNROLL), step, 0)
        total = jnp.zeros((cells * blocks, 4 * part), f32)
        for piece in split2(plate_sum[c][...] * rep_row):
            total = total + lax.dot_general(p_pick, piece, (((1,), (1,)), ((), ())), preferred_element_type=f32)
        for s in range(cells):
            mine = total[s * blocks : (s + 1) * blocks]
            out_p[c][s, 0:blocks, :] = mine[:, 0:width]
            last = mine[:, width:]
            out_p[c][s, blocks:, :] = last[0 : blocks // 2] + pltpu.roll(last[blocks // 2 :], part, 1)
        return send_cells(lambda s: out_p[c].at[s], lambda s: land_p[c].at[s], (r0_s, r1_s)[c], (r0_r, r1_r)[c])

    returns = run(0)
    for copy in second:
        copy.wait()
    collect_plates(1)
    returns += run(1)
    for r in range(3):
        on_slot = tower_sum[pl.ds(r * pairs * 8, pairs, stride=8), :]
        for j in range(1, 8):
            on_slot = on_slot + tower_sum[pl.ds(r * pairs * 8 + j, pairs, stride=8), :]
        total = jnp.zeros((nz * blocks, width), f32)
        for piece in split2(on_slot * rep_col):
            total = total + jnp.dot(t_pick, piece, preferred_element_type=f32)
        for s in range(nz):
            out_t[s, :, r * width : (r + 1) * width] = total[s * blocks : (s + 1) * blocks]
    for s in range(1, nz):
        there = slots.opposite(s)
        returns.append(send(out_t.at[s], land_t.at[there], rt_s.at[s], rt_r.at[there], s))
    for copy in returns:
        copy.wait()

    back = []
    for c in range(HALVES):
        total = out_p[c][0]
        for s in range(1, cells):
            total = total + land_p[c][s]
        back.append(total)
    on_tower = out_t[0]
    for s in range(1, nz):
        on_tower = on_tower + land_t[s]
    (a0, a1), (z0, z1) = [v[0:blocks] for v in back], [v[blocks:] for v in back]
    low_z = low[0 : blocks // 2]
    on_plate = (
        jnp.where(low, a0, pltpu.roll(a1, part, 1)),
        jnp.where(low, pltpu.roll(a0, part, 1), a1),
        jnp.concatenate(
            [jnp.where(low_z, z0, pltpu.roll(z1, part, 1)), jnp.where(low_z, pltpu.roll(z0, part, 1), z1)], axis=0
        ),
    )
    for r in range(3):
        force[r] = (on_tower[:, r * width : (r + 1) * width] - on_plate[r]) * lengths[r]
    for q in range(mig_block.shape[1]):
        at = slice(q * width, (q + 1) * width)
        block = mig_block[0, q]
        kick = 0.5 * time_step * mass_b[block]
        old = half_b[block]
        for r in range(3):
            going_v[r : r + 1, at] = old[r : r + 1] + kick * force[r, block][None, :]
    come_v[0] = going_v[...]
    last_hop = send_cells(lambda s: going_v, lambda s: come_v.at[s], mv_s, mv_r)
    for r in range(3):
        for b in range(blocks):
            force_out[r : r + 1, b * width : (b + 1) * width] = force[r, b : b + 1]
    half = vel[...] + 0.5 * time_step * fold[...] * mass[...]
    block_of = lax.broadcasted_iota(jnp.int32, pos.shape, 1) // width
    gone = block_of == mig_block[0, 0]
    for q in range(1, mig_block.shape[1]):
        gone = gone | (block_of == mig_block[0, q])
    vel_out[...] = jnp.where(gone, 0.0, half + 0.5 * time_step * force_out[...] * mass[...])
    for copy in leavers:
        copy.wait()
    wanted = []
    for i, (a, b) in enumerate(source_offsets):
        cell = slots.cell_number(slots.cell_slot(a, b))
        wanted.append((cell, come_m[cell, 3:4, :] == float((1 - a) * 3 + (1 - b))))
        for r in range(3):
            arrive[r, 0, i : i + 1, :] = jnp.where(wanted[i][1], come_m[cell, r : r + 1, :], 0.0)
    for copy in last_hop:
        copy.wait()
    for i, (cell, chosen) in enumerate(wanted):
        for r in range(3):
            arrive[3 + r, 0, i : i + 1, :] = jnp.where(chosen, come_v[cell, r : r + 1, :], 0.0)


def output_kernel(*refs):
    sem = refs[-1]
    copies = [pltpu.make_async_copy(refs[i], refs[4 + i], sem.at[i]) for i in range(4)]
    for copy in copies:
        copy.start()
    for copy in copies:
        copy.wait()


def local(
    slots, positions, velocities, forces_old, inv_mass, charges, block_species, sigma_table, epsilon_table,
    tower_index, plate_index, tile_counts, exclusions, mig_block, mig_dest,
):
    atoms = positions.shape[1]
    blocks = block_species.shape[0]
    width = atoms // blocks
    nz, cells = slots.nz, slots.cells
    pairs = tower_index.shape[1]
    leaving = mig_block.shape[1]
    kinds = sigma_table.shape[0]
    part = width // HALVES
    pitch = 2 * blocks
    hbm = pl.BlockSpec(memory_space=pltpu.HBM)
    vmem = pl.BlockSpec(memory_space=pltpu.VMEM)
    mass = inv_mass[None, :]
    f32, i32 = jnp.float32, jnp.int32

    def sems(n):
        return pltpu.SemaphoreType.DMA((n,))

    def v(*shape):
        return pltpu.VMEM(shape, f32)

    rows = jax.ShapeDtypeStruct((3, atoms), f32)
    arrive = jax.ShapeDtypeStruct((6, 1, len(source_offsets), leaving * width), f32)
    held = tuple(pltpu.VMEM(a.shape, f32) for a in (rows, rows, rows, arrive))
    made = pl.pallas_call(
        functools.partial(step_kernel, slots, blocks),
        out_shape=held,
        in_specs=[hbm] * 14,
        out_specs=(vmem,) * 4,
        scratch_shapes=[
            v(3, atoms), v(3, atoms), v(3, atoms), v(1, atoms), v(1, atoms), pltpu.VMEM((1, blocks), i32),
            pltpu.SMEM((kinds,), f32), pltpu.SMEM((kinds,), f32),
            pltpu.SMEM((1, pairs), i32), pltpu.SMEM((1, pairs), i32),
            pltpu.VMEM((1, pairs), i32), pltpu.VMEM((1, pairs), i32),
            pltpu.SMEM((1,), i32), pltpu.VMEM(exclusions.shape, i32),
            pltpu.SMEM((1, leaving), i32), pltpu.SMEM((1, leaving), i32),
            v(blocks, 3, width), v(blocks, 3, width), v(blocks, 1, width), v(4 * blocks, width), v(nz * (blocks + 1), 4, width),
            v(8 * cells, width), v(cells * pitch, width), v(cells * pitch, width),
            v(pairs * width, width), v(pairs, width), v(4 * pairs, width), v(2 * pairs, width),
            v(6 * pairs * TERMS, width), pltpu.VMEM((pairs * TERMS, 6 * width), jnp.bfloat16), v(pairs * TERMS, width), v(pairs * TERMS, width),
            v(UNROLL, part, 6 * width), v(UNROLL, part, 6 * width), v(3 * 8 * pairs, width), v(4 * part, pairs), v(4 * part, pairs),
            v(nz, blocks, 3 * width), v(cells, blocks + blocks // 2, width), v(cells, blocks + blocks // 2, width),
            v(nz, blocks, 3 * width), v(cells, blocks + blocks // 2, width), v(cells, blocks + blocks // 2, width),
            v(4, leaving * width), v(4, leaving * width), v(cells, 4, leaving * width), v(cells, 4, leaving * width),
            v(3, blocks, width),
            pltpu.VMEM((1, pairs), i32), pltpu.VMEM((1, pairs), i32), sems(16),
        ]
        + [sems(cells)] * 2 + [sems(nz)] * 2 + [sems(cells)] * 4 + [sems(nz)] * 2 + [sems(cells)] * 8,
        compiler_params=pltpu.CompilerParams(
            collective_id=0, has_side_effects=True, vmem_limit_bytes=60 * 1024 * 1024
        ),
        name="membrane_step",
    )(
        positions, velocities, forces_old, mass, charges[None, :], block_species[None, :], sigma_table,
        epsilon_table, tower_index, plate_index, tile_counts, exclusions, mig_block, mig_dest,
    )
    return pl.pallas_call(
        output_kernel,
        out_shape=(rows, rows, rows, arrive),
        in_specs=[vmem] * 4,
        out_specs=(hbm,) * 4,
        scratch_shapes=[sems(4)],
        compiler_params=pltpu.CompilerParams(vmem_limit_bytes=1024 * 1024),
        name="outputs",
    )(*made)


def solution(mesh):
    cells = ("gx", "gy", "gz")
    slots = Slots(mesh.shape["gx"], mesh.shape["gy"], mesh.shape["gz"])
    row = P(None, cells)
    flat = P(cells)
    pair = P(cells, None)
    in_specs = (
        row, row, row, flat, flat, flat, P(), P(), pair, pair, flat, P(cells, None, None, None), pair, pair,
    )
    out_specs = (row, row, row, P(None, cells, None, None))
    return jax.shard_map(
        functools.partial(local, slots), mesh=mesh, in_specs=in_specs, out_specs=out_specs, check_vma=False
    )
```

```python
import functools
import jax
import jax.numpy as jnp
from jax import lax
from jax.experimental import pallas as pl
from jax.experimental.pallas import tpu as pltpu
from jax.sharding import PartitionSpec as P

time_step = 0.2
soft_core = 0.09
cutoff_sq = 1.44
coulomb_k = 0.5
MESH = pl.DeviceIdType.MESH
UNROLL = 8
HALVES = 2
TERMS = 16
source_offsets = ((-1, -1), (-1, 0), (-1, 1), (0, -1), (0, 1), (1, -1), (1, 0), (1, 1))


class Slots:
    def __init__(self, nx, ny, nz):
        self.nx, self.ny, self.nz = nx, ny, nz
        self.offsets = [(0, 0, 0)] + [(0, 0, k) for k in range(1, nz)]
        self.cell = {(0, 0): 0}
        for da in range(-1, 2):
            for db in range(-1, 2):
                key = (da % nx, db % ny)
                if key not in self.cell:
                    self.cell[key] = len(self.offsets)
                    self.offsets.append((key[0], key[1], 0))
        self.count = len(self.offsets)
        self.cells = 1 + self.count - nz

    def cell_slot(self, da, db):
        return self.cell[(da % self.nx, db % self.ny)]

    def cell_number(self, slot):
        return slot - self.nz + 1 if slot else 0

    def opposite(self, slot):
        dx, dy, dz = self.offsets[slot]
        if dz:
            return (self.nz - dz) % self.nz
        return self.cell_slot(-dx, -dy)

    def device(self, slot):
        dx, dy, dz = self.offsets[slot]
        return (
            lax.rem(lax.axis_index("gx") + dx, self.nx),
            lax.rem(lax.axis_index("gy") + dy, self.ny),
            lax.rem(lax.axis_index("gz") + dz, self.nz),
        )


def split3(value):
    high = value.astype(jnp.bfloat16).astype(jnp.float32)
    rest = value - high
    mid = rest.astype(jnp.bfloat16).astype(jnp.float32)
    return high, mid, rest - mid


def split2(value):
    high = value.astype(jnp.bfloat16)
    return high, (value - high.astype(jnp.float32)).astype(jnp.bfloat16)


def step_kernel(
    slots, blocks,
    pos_h, vel_h, fold_h, mass_h, charge_h, species_h, sigma_h, eps_h, tower_h, plate_h, counts_h, excl_h,
    mig_block_h, mig_dest_h,
    pos_out, vel_out, force_out, arrive,
    pos, vel, fold, mass, charge, species, sigma_s, eps_s, tower, plate, tower_v, plate_v, counts, excl,
    mig_block, mig_dest,
    half_b, moved_b, mass_b, dense, tow, kin, near0, near1, allowed, att_tab, towers, plates, right, right_b, left0, left1,
    made_a, made_b, tower_sum, plate_sum0, plate_sum1, out_t, out_p0, out_p1, land_t, land_p0, land_p1, going_m, going_v, come_m, come_v,
    force,
    t_flat, p_flat, local_sem,
    kn_s, kn_r, tow_s, tow_r, n0_s, n0_r, n1_s, n1_r, rt_s, rt_r, r0_s, r0_r, r1_s, r1_r, mm_s, mm_r, mv_s, mv_r,
):
    atoms = pos.shape[1]
    width = atoms // blocks
    pairs = tower.shape[1]
    words = excl.shape[2]
    part = width // HALVES
    pitch = 2 * blocks
    nx, ny, nz, cells = slots.nx, slots.ny, slots.nz, slots.cells
    lx, ly = float(nx), float(ny)
    lengths = (lx, ly, lx)
    f32 = jnp.float32
    bf16 = jnp.bfloat16
    near = (near0, near1)
    left = (left0, left1)
    plate_sum = (plate_sum0, plate_sum1)
    out_p = (out_p0, out_p1)
    land_p = (land_p0, land_p1)
    ratio = (ly / lx) ** 2
    shift_h = soft_core / (lx * lx)
    edge = (cutoff_sq + soft_core) / (lx * lx)
    scale = lx * lx / (cutoff_sq * cutoff_sq)

    barrier = pltpu.get_barrier_semaphore()
    for s in range(1, slots.count):
        pl.semaphore_signal(barrier, inc=1, device_id=slots.device(s), device_id_type=MESH)
    fetches = []
    for src, dst in (
        (pos_h, pos), (vel_h, vel), (fold_h, fold), (mass_h, mass), (charge_h, charge), (species_h, species),
        (sigma_h, sigma_s), (eps_h, eps_s), (excl_h, excl),
        (tower_h, tower_v), (plate_h, plate_v), (counts_h, counts), (mig_block_h, mig_block), (mig_dest_h, mig_dest),
    ):
        copy = pltpu.make_async_copy(src, dst, local_sem.at[len(fetches)])
        copy.start()
        fetches.append(copy)
    for copy in fetches[:8]:
        copy.wait()

    half = vel[...] + 0.5 * time_step * fold[...] * mass[...]
    moved = pos[...] + time_step * half
    row3 = lax.broadcasted_iota(jnp.int32, (3, atoms), 0)
    scaled = moved * jnp.where(row3 == 1, f32(1.0 / ly), f32(1.0 / lx))
    tower_charge = charge[...] * (coulomb_k * scale / lx)
    for b in range(blocks):
        at = slice(b * width, (b + 1) * width)
        tow[b, 0:3, :] = scaled[:, at]
        tow[b, 3:4, :] = tower_charge[:, at]
        for r in range(3):
            dense[r * blocks + b : r * blocks + b + 1, :] = scaled[r : r + 1, at]
        dense[3 * blocks + b : 3 * blocks + b + 1, :] = charge[:, at]
    which = species[...]
    sigma = jnp.zeros((1, blocks), f32)
    eps = jnp.zeros((1, blocks), f32)
    for k in range(sigma_s.shape[0]):
        sigma = jnp.where(which == k, sigma_s[k], sigma)
        eps = jnp.where(which == k, eps_s[k], eps)
    depth_row = jnp.sqrt(eps)
    tow[blocks] = jnp.zeros((4, width), f32)
    tow[blocks, 0:1, 0:blocks] = sigma
    tow[blocks, 1:2, 0:blocks] = depth_row
    kin[0:8, :] = jnp.zeros((8, width), f32)
    kin[0:1, 0:blocks] = sigma
    kin[1:2, 0:blocks] = depth_row
    low = lax.broadcasted_iota(jnp.int32, (blocks, width), 1) < part
    comp = [dense[r * blocks : (r + 1) * blocks, :] for r in range(4)]
    turned = [pltpu.roll(v, part, 1) for v in comp]
    near0[0:blocks, :] = jnp.where(low, comp[0], turned[1])
    near0[blocks : 2 * blocks, :] = jnp.where(low, comp[2], turned[3])
    near1[0:blocks, :] = jnp.where(low, turned[0], comp[1])
    near1[blocks : 2 * blocks, :] = jnp.where(low, turned[2], comp[3])

    pl.semaphore_wait(barrier, slots.count - 1)

    def send(src, dst, ss, rs, s):
        copy = pltpu.make_async_remote_copy(
            src_ref=src, dst_ref=dst, send_sem=ss, recv_sem=rs, device_id=slots.device(s), device_id_type=MESH
        )
        copy.start()
        return copy

    def send_cells(source, landing, ss, rs):
        copies = []
        for s in range(nz, slots.count):
            here, there = slots.cell_number(s), slots.cell_number(slots.opposite(s))
            copies.append(send(source(here), landing(there), ss.at[here], rs.at[there], s))
        return copies

    def rows_of(ref, size):
        return lambda c: ref.at[c * size : (c + 1) * size]

    named = send_cells(lambda c: kin.at[0:8], rows_of(kin, 8), kn_s, kn_r)
    above = []
    for s in range(1, nz):
        there = slots.opposite(s) * (blocks + 1)
        above.append(
            send(tow.at[0 : blocks + 1], tow.at[there : there + blocks + 1], tow_s.at[s], tow_r.at[slots.opposite(s)], s)
        )
    first = send_cells(lambda c: near0.at[0:pitch], rows_of(near0, pitch), n0_s, n0_r)
    second = send_cells(lambda c: near1.at[0:pitch], rows_of(near1, pitch), n1_s, n1_r)

    bit = jnp.left_shift(1, lax.broadcasted_iota(jnp.int32, (8, width), 0))
    term = lax.broadcasted_iota(jnp.int32, (TERMS, width), 0)
    early = jnp.where(term < 3, -1.0, 0.0)
    late = jnp.where((term >= 3) & (term < 6), -1.0, 0.0)
    shifted = jnp.where(term == 12, 0.5, early)
    ones = jnp.where((term >= 9) & (term < 13), 1.0, 0.0)
    plain = (early, late, shifted, early, jnp.zeros((TERMS, width), f32), shifted)
    for copy in fetches[8:]:
        copy.wait()

    def expand(k, carry):
        for w in range(words):
            hit = excl[0, k, w : w + 1, :] & bit
            allowed[pl.ds(pl.multiple_of(k * width + w * 8, 8), 8), :] = jnp.where(hit == 0, edge, -1.0)
        at = pl.ds(pl.multiple_of(k * TERMS, TERMS), TERMS)
        left0[at, :] = ones
        left1[at, :] = ones
        for g in range(6):
            at_g = pl.ds(pl.multiple_of((g * pairs + k) * TERMS, TERMS), TERMS)
            right[at_g, :] = plain[g]
        return carry

    lax.fori_loop(0, pairs, expand, 0)
    for c in range(HALVES):
        plate_sum[c][...] = jnp.zeros(plate_sum[c].shape, f32)
    half = vel[...] + 0.5 * time_step * fold[...] * mass[...]
    moved = pos[...] + time_step * half
    for b in range(blocks):
        at = slice(b * width, (b + 1) * width)
        half_b[b] = half[:, at]
        moved_b[b] = moved[:, at]
        mass_b[b] = mass[:, at]
    for q in range(mig_block.shape[1]):
        at = slice(q * width, (q + 1) * width)
        going_m[0:3, at] = moved_b[mig_block[0, q]]
        going_m[3:4, at] = jnp.full((1, width), mig_dest[0, q], jnp.int32).astype(f32)
    going_v[...] = jnp.zeros(going_v.shape, f32)
    come_m[0] = going_m[...]
    leavers = send_cells(lambda s: going_m, lambda s: come_m.at[s], mm_s, mm_r)
    block_of = lax.broadcasted_iota(jnp.int32, pos.shape, 1) // width
    gone = block_of == mig_block[0, 0]
    for q in range(1, mig_block.shape[1]):
        gone = gone | (block_of == mig_block[0, q])
    pos_out[...] = jnp.where(gone, 0.0, moved)

    my_layer = lax.axis_index("gz")
    t_all = tower_v[...]
    p_all = plate_v[...]
    live = lax.broadcasted_iota(jnp.int32, (1, pairs), 1) < counts[0]
    t_layer = t_all // blocks
    t_turn = t_layer - my_layer
    t_turn = jnp.where(t_turn < 0, t_turn + nz, t_turn)
    t_block = t_all - t_layer * blocks
    t_flat[...] = t_turn * (blocks + 1) + t_block
    t_row = jnp.where(live, t_turn * blocks + t_block, -1)
    p_cell = p_all // blocks
    p_number = jnp.zeros((1, pairs), jnp.int32)
    for o in range(9):
        number = slots.cell_number(slots.cell_slot(o // 3 - 1, o % 3 - 1))
        p_number = jnp.where(p_cell == o, number, p_number)
    p_block = p_all - p_cell * blocks
    p_flat[...] = p_number * pitch + p_block
    p_row = jnp.where(live, p_number * blocks + p_block, -1)
    tables = []
    for src, dst in ((t_flat, tower), (p_flat, plate)):
        tables.append(pltpu.make_async_copy(src, dst, local_sem.at[14 + len(tables)]))
        tables[-1].start()
    t_pick = jnp.where(
        lax.broadcasted_iota(jnp.int32, (nz * blocks, pairs), 0) == t_row, 1.0, 0.0
    ).astype(bf16)
    p_pick = jnp.where(
        lax.broadcasted_iota(jnp.int32, (cells * blocks, pairs), 0) == p_row, 1.0, 0.0
    ).astype(bf16)
    same = lax.broadcasted_iota(jnp.int32, (pairs, pairs), 0) == lax.broadcasted_iota(jnp.int32, (pairs, pairs), 1)
    t_col = jnp.sum(jnp.where(same, (t_turn * blocks + t_block).astype(f32), 0.0), axis=1, keepdims=True)
    p_col = jnp.sum(jnp.where(same, (p_number * blocks + p_block).astype(f32), 0.0), axis=1, keepdims=True)

    for copy in tables:
        copy.wait()
    for copy in above:
        copy.wait()

    lane_f = lax.broadcasted_iota(jnp.int32, (pairs, width), 1).astype(f32)

    def of_block(column, rows):
        found = jnp.zeros((pairs, width), f32)
        for s, row in enumerate(rows):
            found = found + jnp.where(lane_f == column - float(s * blocks), row, 0.0)
        return jnp.sum(found, axis=1, keepdims=True)

    sig_t = of_block(t_col, [tow[s * (blocks + 1) + blocks, 0:1, :] for s in range(nz)])
    dep_t = of_block(t_col, [tow[s * (blocks + 1) + blocks, 1:2, :] for s in range(nz)])
    def collect_towers(i, carry):
        for u in range(0, 16, 2):
            two = [tow[tower[0, i * 16 + u + v]] for v in range(2)]
            towers[pl.ds(pl.multiple_of(i * 64 + u * 4, 8), 8), :] = jnp.concatenate(two, axis=0)
        return carry

    lax.fori_loop(0, pairs // 16, collect_towers, 0)
    for r, groups in ((0, (0, 2)), (2, (1,)), (1, (3, 5)), (3, (4,))):
        terms = ((3, 4, 5), (6, 8), (7,)) if r == 3 else ((9,), (10,), (11,))
        for value, places in zip(split3(towers[pl.ds(r, pairs, stride=4), :]), terms):
            for t in places:
                for g in groups:
                    right[pl.ds(g * pairs * TERMS + t, pairs, stride=TERMS), :] = value
    def narrow(k, carry):
        row = pl.ds(pl.multiple_of(k * TERMS, TERMS), TERMS)
        for g in range(6):
            at = pl.ds(pl.multiple_of((g * pairs + k) * TERMS, TERMS), TERMS)
            right_b[row, g * width : (g + 1) * width] = right[at, :].astype(bf16)
        return carry

    lax.fori_loop(0, pairs, narrow, 0)
    for copy in named:
        copy.wait()
    sig_p = of_block(p_col, [kin[8 * c : 8 * c + 1, :] for c in range(cells)])
    dep_p = of_block(p_col, [kin[8 * c + 1 : 8 * c + 2, :] for c in range(cells)])
    sig = 0.5 * (sig_t + sig_p)
    sig2 = sig * sig
    sig6 = sig2 * sig2 * sig2
    depth = dep_t * dep_p
    att_tab[...] = jnp.broadcast_to((0.5 * lx**6) / sig6, (pairs, width))
    rep_col = (12.0 * scale / lx**12) * depth * sig6 * sig6
    rep_row = jnp.sum(jnp.where(same, rep_col, 0.0), axis=0, keepdims=True)
    charge_lanes = lax.broadcasted_iota(jnp.int32, (pairs, width), 1) >= part
    charge_scale = jnp.where(charge_lanes, 1.0 / rep_col, 1.0)

    def collect_plates(c):
        def body(i, carry):
            for u in range(16):
                p = plate[0, i * 16 + u]
                plates[i * 16 + u] = near[c][p]
                plates[pairs + i * 16 + u] = near[c][p + blocks]
            return carry

        lax.fori_loop(0, pairs // 16, body, 0)
        for r, terms in ((0, ((0,), (1,), (2,))), (1, ((3, 6, 7), (4, 8), (5,)))):
            rows = plates[r * pairs : (r + 1) * pairs, :]
            for value, places in zip(split3(rows * charge_scale if r else rows), terms):
                for t in places:
                    left[c][pl.ds(t, pairs, stride=TERMS), :] = value

    for copy in first:
        copy.wait()
    collect_plates(0)

    lane = lax.broadcasted_iota(jnp.int32, (8, pairs), 1)

    def prepare(k, c, made):
        at = pl.ds(pl.multiple_of(k * TERMS, TERMS), TERMS)
        a = left[c][at, :].T
        for i in range(2):
            made[:, 3 * i * width : 3 * (i + 1) * width] = jnp.dot(
                a[i * part : (i + 1) * part].astype(bf16),
                right_b[at, 3 * i * width : 3 * (i + 1) * width],
                preferred_element_type=f32,
            )

    def arithmetic(k, c, made):
        att = att_tab[pl.ds(k, 1), :]
        here = lane == k
        sums = [None, None, None]
        for w in range(part // 8):
            at = slice(w * 8, (w + 1) * 8)
            dx = made[at, 0:width] - jnp.floor(made[at, 2 * width : 3 * width])
            dz = made[at, width : 2 * width]
            dy = made[at, 3 * width : 4 * width] - jnp.floor(made[at, 5 * width : 6 * width])
            h = (dx * dx + dz * dz) + (ratio * (dy * dy) + shift_h)
            q = lax.rsqrt(h)
            f = jnp.maximum(allowed[pl.ds(pl.multiple_of(k * width + (c * part + w * 8), 8), 8), :] - h, 0.0)
            s = pl.reciprocal(h, approx=True)
            s3 = s * s * s
            fq = f * q
            g = fq * fq
            e = s3 * (s3 - att) + made[at, 4 * width : 5 * width] * q
            force_c = e * g
            parts = (force_c * dx, force_c * dy, force_c * dz)
            sums = [v if u is None else u + v for u, v in zip(sums, parts)]
            for r in range(3):
                total = jnp.broadcast_to(jnp.sum(parts[r], axis=1, keepdims=True), (8, pairs))
                pltpu.store(plate_sum[c].at[r * part + w * 8 : r * part + (w + 1) * 8, :], total, mask=here)
        for r in range(3):
            at = pl.ds(pl.multiple_of((r * pairs + k) * 8, 8), 8)
            tower_sum[at, :] = sums[r] if c == 0 else tower_sum[at, :] + sums[r]

    def run(c):
        for u in range(UNROLL):
            prepare(u, c, made_a.at[u])

        def step(i, carry):
            k = i * (2 * UNROLL)
            for u in range(UNROLL):
                prepare(k + UNROLL + u, c, made_b.at[u])
                arithmetic(k + u, c, made_a.at[u])
            for u in range(UNROLL):
                prepare(lax.rem(k + 2 * UNROLL + u, pairs), c, made_a.at[u])
                arithmetic(k + UNROLL + u, c, made_b.at[u])
            return carry

        lax.fori_loop(0, pairs // (2 * UNROLL), step, 0)
        total = jnp.zeros((cells * blocks, 4 * part), f32)
        for piece in split2(plate_sum[c][...] * rep_row):
            total = total + lax.dot_general(p_pick, piece, (((1,), (1,)), ((), ())), preferred_element_type=f32)
        for s in range(cells):
            mine = total[s * blocks : (s + 1) * blocks]
            out_p[c][s, 0:blocks, :] = mine[:, 0:width]
            last = mine[:, width:]
            out_p[c][s, blocks:, :] = last[0 : blocks // 2] + pltpu.roll(last[blocks // 2 :], part, 1)
        return send_cells(lambda s: out_p[c].at[s], lambda s: land_p[c].at[s], (r0_s, r1_s)[c], (r0_r, r1_r)[c])

    returns = run(0)
    for copy in second:
        copy.wait()
    collect_plates(1)
    returns += run(1)
    for r in range(3):
        on_slot = tower_sum[pl.ds(r * pairs * 8, pairs, stride=8), :]
        for j in range(1, 8):
            on_slot = on_slot + tower_sum[pl.ds(r * pairs * 8 + j, pairs, stride=8), :]
        total = jnp.zeros((nz * blocks, width), f32)
        for piece in split2(on_slot * rep_col):
            total = total + jnp.dot(t_pick, piece, preferred_element_type=f32)
        for s in range(nz):
            out_t[s, :, r * width : (r + 1) * width] = total[s * blocks : (s + 1) * blocks]
    for s in range(1, nz):
        there = slots.opposite(s)
        returns.append(send(out_t.at[s], land_t.at[there], rt_s.at[s], rt_r.at[there], s))
    for copy in returns:
        copy.wait()

    back = []
    for c in range(HALVES):
        total = out_p[c][0]
        for s in range(1, cells):
            total = total + land_p[c][s]
        back.append(total)
    on_tower = out_t[0]
    for s in range(1, nz):
        on_tower = on_tower + land_t[s]
    (a0, a1), (z0, z1) = [v[0:blocks] for v in back], [v[blocks:] for v in back]
    low_z = low[0 : blocks // 2]
    on_plate = (
        jnp.where(low, a0, pltpu.roll(a1, part, 1)),
        jnp.where(low, pltpu.roll(a0, part, 1), a1),
        jnp.concatenate(
            [jnp.where(low_z, z0, pltpu.roll(z1, part, 1)), jnp.where(low_z, pltpu.roll(z0, part, 1), z1)], axis=0
        ),
    )
    for r in range(3):
        force[r] = (on_tower[:, r * width : (r + 1) * width] - on_plate[r]) * lengths[r]
    for q in range(mig_block.shape[1]):
        at = slice(q * width, (q + 1) * width)
        block = mig_block[0, q]
        kick = 0.5 * time_step * mass_b[block]
        old = half_b[block]
        for r in range(3):
            going_v[r : r + 1, at] = old[r : r + 1] + kick * force[r, block][None, :]
    come_v[0] = going_v[...]
    last_hop = send_cells(lambda s: going_v, lambda s: come_v.at[s], mv_s, mv_r)
    for r in range(3):
        for b in range(blocks):
            force_out[r : r + 1, b * width : (b + 1) * width] = force[r, b : b + 1]
    half = vel[...] + 0.5 * time_step * fold[...] * mass[...]
    block_of = lax.broadcasted_iota(jnp.int32, pos.shape, 1) // width
    gone = block_of == mig_block[0, 0]
    for q in range(1, mig_block.shape[1]):
        gone = gone | (block_of == mig_block[0, q])
    vel_out[...] = jnp.where(gone, 0.0, half + 0.5 * time_step * force_out[...] * mass[...])
    for copy in leavers:
        copy.wait()
    wanted = []
    for i, (a, b) in enumerate(source_offsets):
        cell = slots.cell_number(slots.cell_slot(a, b))
        wanted.append((cell, come_m[cell, 3:4, :] == float((1 - a) * 3 + (1 - b))))
        for r in range(3):
            arrive[r, 0, i : i + 1, :] = jnp.where(wanted[i][1], come_m[cell, r : r + 1, :], 0.0)
    for copy in last_hop:
        copy.wait()
    for i, (cell, chosen) in enumerate(wanted):
        for r in range(3):
            arrive[3 + r, 0, i : i + 1, :] = jnp.where(chosen, come_v[cell, r : r + 1, :], 0.0)


def output_kernel(*refs):
    sem = refs[-1]
    copies = [pltpu.make_async_copy(refs[i], refs[4 + i], sem.at[i]) for i in range(4)]
    for copy in copies:
        copy.start()
    for copy in copies:
        copy.wait()


def local(
    slots, positions, velocities, forces_old, inv_mass, charges, block_species, sigma_table, epsilon_table,
    tower_index, plate_index, tile_counts, exclusions, mig_block, mig_dest,
):
    atoms = positions.shape[1]
    blocks = block_species.shape[0]
    width = atoms // blocks
    nz, cells = slots.nz, slots.cells
    pairs = tower_index.shape[1]
    leaving = mig_block.shape[1]
    kinds = sigma_table.shape[0]
    part = width // HALVES
    pitch = 2 * blocks
    hbm = pl.BlockSpec(memory_space=pltpu.HBM)
    vmem = pl.BlockSpec(memory_space=pltpu.VMEM)
    mass = inv_mass[None, :]
    f32, i32 = jnp.float32, jnp.int32

    def sems(n):
        return pltpu.SemaphoreType.DMA((n,))

    def v(*shape):
        return pltpu.VMEM(shape, f32)

    rows = jax.ShapeDtypeStruct((3, atoms), f32)
    arrive = jax.ShapeDtypeStruct((6, 1, len(source_offsets), leaving * width), f32)
    held = tuple(pltpu.VMEM(a.shape, f32) for a in (rows, rows, rows, arrive))
    made = pl.pallas_call(
        functools.partial(step_kernel, slots, blocks),
        out_shape=held,
        in_specs=[hbm] * 14,
        out_specs=(vmem,) * 4,
        scratch_shapes=[
            v(3, atoms), v(3, atoms), v(3, atoms), v(1, atoms), v(1, atoms), pltpu.VMEM((1, blocks), i32),
            pltpu.SMEM((kinds,), f32), pltpu.SMEM((kinds,), f32),
            pltpu.SMEM((1, pairs), i32), pltpu.SMEM((1, pairs), i32),
            pltpu.VMEM((1, pairs), i32), pltpu.VMEM((1, pairs), i32),
            pltpu.SMEM((1,), i32), pltpu.VMEM(exclusions.shape, i32),
            pltpu.SMEM((1, leaving), i32), pltpu.SMEM((1, leaving), i32),
            v(blocks, 3, width), v(blocks, 3, width), v(blocks, 1, width), v(4 * blocks, width), v(nz * (blocks + 1), 4, width),
            v(8 * cells, width), v(cells * pitch, width), v(cells * pitch, width),
            v(pairs * width, width), v(pairs, width), v(4 * pairs, width), v(2 * pairs, width),
            v(6 * pairs * TERMS, width), pltpu.VMEM((pairs * TERMS, 6 * width), jnp.bfloat16), v(pairs * TERMS, width), v(pairs * TERMS, width),
            v(UNROLL, part, 6 * width), v(UNROLL, part, 6 * width), v(3 * 8 * pairs, width), v(4 * part, pairs), v(4 * part, pairs),
            v(nz, blocks, 3 * width), v(cells, blocks + blocks // 2, width), v(cells, blocks + blocks // 2, width),
            v(nz, blocks, 3 * width), v(cells, blocks + blocks // 2, width), v(cells, blocks + blocks // 2, width),
            v(4, leaving * width), v(4, leaving * width), v(cells, 4, leaving * width), v(cells, 4, leaving * width),
            v(3, blocks, width),
            pltpu.VMEM((1, pairs), i32), pltpu.VMEM((1, pairs), i32), sems(16),
        ]
        + [sems(cells)] * 2 + [sems(nz)] * 2 + [sems(cells)] * 4 + [sems(nz)] * 2 + [sems(cells)] * 8,
        compiler_params=pltpu.CompilerParams(
            collective_id=0, has_side_effects=True, vmem_limit_bytes=60 * 1024 * 1024
        ),
        name="membrane_step",
    )(
        positions, velocities, forces_old, mass, charges[None, :], block_species[None, :], sigma_table,
        epsilon_table, tower_index, plate_index, tile_counts, exclusions, mig_block, mig_dest,
    )
    return pl.pallas_call(
        output_kernel,
        out_shape=(rows, rows, rows, arrive),
        in_specs=[vmem] * 4,
        out_specs=(hbm,) * 4,
        scratch_shapes=[sems(4)],
        compiler_params=pltpu.CompilerParams(vmem_limit_bytes=1024 * 1024),
        name="outputs",
    )(*made)


def solution(mesh):
    cells = ("gx", "gy", "gz")
    slots = Slots(mesh.shape["gx"], mesh.shape["gy"], mesh.shape["gz"])
    row = P(None, cells)
    flat = P(cells)
    pair = P(cells, None)
    in_specs = (
        row, row, row, flat, flat, flat, P(), P(), pair, pair, flat, P(cells, None, None, None), pair, pair,
    )
    out_specs = (row, row, row, P(None, cells, None, None))
    return jax.shard_map(
        functools.partial(local, slots), mesh=mesh, in_specs=in_specs, out_specs=out_specs, check_vma=False
    )
```

```python
import functools
import jax
import jax.numpy as jnp
from jax import lax
from jax.experimental import pallas as pl
from jax.experimental.pallas import tpu as pltpu
from jax.sharding import PartitionSpec as P

time_step = 0.2
soft_core = 0.09
cutoff_sq = 1.44
coulomb_k = 0.5
MESH = pl.DeviceIdType.MESH
UNROLL = 4
GROUPS = 4
HALVES = 2
TERMS = 16
source_offsets = ((-1, -1), (-1, 0), (-1, 1), (0, -1), (0, 1), (1, -1), (1, 0), (1, 1))


class Slots:
    def __init__(self, nx, ny, nz):
        self.nx, self.ny, self.nz = nx, ny, nz
        self.offsets = [(0, 0, 0)] + [(0, 0, k) for k in range(1, nz)]
        self.cell = {(0, 0): 0}
        for da in range(-1, 2):
            for db in range(-1, 2):
                key = (da % nx, db % ny)
                if key not in self.cell:
                    self.cell[key] = len(self.offsets)
                    self.offsets.append((key[0], key[1], 0))
        self.count = len(self.offsets)
        self.cells = 1 + self.count - nz

    def cell_slot(self, da, db):
        return self.cell[(da % self.nx, db % self.ny)]

    def cell_number(self, slot):
        return slot - self.nz + 1 if slot else 0

    def opposite(self, slot):
        dx, dy, dz = self.offsets[slot]
        if dz:
            return (self.nz - dz) % self.nz
        return self.cell_slot(-dx, -dy)

    def device(self, slot):
        dx, dy, dz = self.offsets[slot]
        return (
            lax.rem(lax.axis_index("gx") + dx, self.nx),
            lax.rem(lax.axis_index("gy") + dy, self.ny),
            lax.rem(lax.axis_index("gz") + dz, self.nz),
        )


def split3(value):
    high = value.astype(jnp.bfloat16).astype(jnp.float32)
    rest = value - high
    mid = rest.astype(jnp.bfloat16).astype(jnp.float32)
    return high, mid, rest - mid


def split2(value):
    high = value.astype(jnp.bfloat16)
    return high, (value - high.astype(jnp.float32)).astype(jnp.bfloat16)


def step_kernel(
    slots, blocks,
    pos_h, vel_h, fold_h, mass_h, charge_h, species_h, sigma_h, eps_h, tower_h, plate_h, counts_h, excl_h,
    mig_block_h, mig_dest_h,
    pos_out, vel_out, force_out, arrive,
    pos, vel, fold, mass, charge, species, sigma_s, eps_s, tower, plate, tower_v, plate_v, counts, excl,
    mig_block, mig_dest,
    half_b, moved_b, mass_b, dense, tow, kin, near0, near1, allowed, att_tab, towers, plates, right, right_b, left0, left1,
    made_a, made_b, tower_sum, plate_sum0, plate_sum1, out_t, out_p0, out_p1, land_t, land_p0, land_p1, going_m, going_v, come_m, come_v,
    force,
    t_flat, p_flat, local_sem,
    kn_s, kn_r, tow_s, tow_r, n0_s, n0_r, n1_s, n1_r, rt_s, rt_r, r0_s, r0_r, r1_s, r1_r, mm_s, mm_r, mv_s, mv_r,
):
    atoms = pos.shape[1]
    width = atoms // blocks
    pairs = tower.shape[1]
    words = excl.shape[2]
    part = width // HALVES
    pitch = 2 * blocks
    nx, ny, nz, cells = slots.nx, slots.ny, slots.nz, slots.cells
    lx, ly = float(nx), float(ny)
    lengths = (lx, ly, lx)
    f32 = jnp.float32
    bf16 = jnp.bfloat16
    near = (near0, near1)
    left = (left0, left1)
    plate_sum = (plate_sum0, plate_sum1)
    out_p = (out_p0, out_p1)
    land_p = (land_p0, land_p1)
    ratio = (ly / lx) ** 2
    shift_h = soft_core / (lx * lx)
    edge = (cutoff_sq + soft_core) / (lx * lx)
    scale = lx * lx / (cutoff_sq * cutoff_sq)

    barrier = pltpu.get_barrier_semaphore()
    for s in range(1, slots.count):
        pl.semaphore_signal(barrier, inc=1, device_id=slots.device(s), device_id_type=MESH)
    fetches = []
    for src, dst in (
        (pos_h, pos), (vel_h, vel), (fold_h, fold), (mass_h, mass), (charge_h, charge), (species_h, species),
        (sigma_h, sigma_s), (eps_h, eps_s), (excl_h, excl),
        (tower_h, tower_v), (plate_h, plate_v), (counts_h, counts), (mig_block_h, mig_block), (mig_dest_h, mig_dest),
    ):
        copy = pltpu.make_async_copy(src, dst, local_sem.at[len(fetches)])
        copy.start()
        fetches.append(copy)
    for copy in fetches[:8]:
        copy.wait()

    half = vel[...] + 0.5 * time_step * fold[...] * mass[...]
    moved = pos[...] + time_step * half
    row3 = lax.broadcasted_iota(jnp.int32, (3, atoms), 0)
    scaled = moved * jnp.where(row3 == 1, f32(1.0 / ly), f32(1.0 / lx))
    tower_charge = charge[...] * (coulomb_k * scale / lx)
    for b in range(blocks):
        at = slice(b * width, (b + 1) * width)
        tow[b, 0:3, :] = scaled[:, at]
        tow[b, 3:4, :] = tower_charge[:, at]
        for r in range(3):
            dense[r * blocks + b : r * blocks + b + 1, :] = scaled[r : r + 1, at]
        dense[3 * blocks + b : 3 * blocks + b + 1, :] = charge[:, at]
    which = species[...]
    sigma = jnp.zeros((1, blocks), f32)
    eps = jnp.zeros((1, blocks), f32)
    for k in range(sigma_s.shape[0]):
        sigma = jnp.where(which == k, sigma_s[k], sigma)
        eps = jnp.where(which == k, eps_s[k], eps)
    depth_row = jnp.sqrt(eps)
    tow[blocks] = jnp.zeros((4, width), f32)
    tow[blocks, 0:1, 0:blocks] = sigma
    tow[blocks, 1:2, 0:blocks] = depth_row
    kin[0:8, :] = jnp.zeros((8, width), f32)
    kin[0:1, 0:blocks] = sigma
    kin[1:2, 0:blocks] = depth_row
    low = lax.broadcasted_iota(jnp.int32, (blocks, width), 1) < part
    comp = [dense[r * blocks : (r + 1) * blocks, :] for r in range(4)]
    turned = [pltpu.roll(v, part, 1) for v in comp]
    near0[0:blocks, :] = jnp.where(low, comp[0], turned[1])
    near0[blocks : 2 * blocks, :] = jnp.where(low, comp[2], turned[3])
    near1[0:blocks, :] = jnp.where(low, turned[0], comp[1])
    near1[blocks : 2 * blocks, :] = jnp.where(low, turned[2], comp[3])

    pl.semaphore_wait(barrier, slots.count - 1)

    def send(src, dst, ss, rs, s):
        copy = pltpu.make_async_remote_copy(
            src_ref=src, dst_ref=dst, send_sem=ss, recv_sem=rs, device_id=slots.device(s), device_id_type=MESH
        )
        copy.start()
        return copy

    def send_cells(source, landing, ss, rs):
        copies = []
        for s in range(nz, slots.count):
            here, there = slots.cell_number(s), slots.cell_number(slots.opposite(s))
            copies.append(send(source(here), landing(there), ss.at[here], rs.at[there], s))
        return copies

    def rows_of(ref, size):
        return lambda c: ref.at[c * size : (c + 1) * size]

    named = send_cells(lambda c: kin.at[0:8], rows_of(kin, 8), kn_s, kn_r)
    above = []
    for s in range(1, nz):
        there = slots.opposite(s) * (blocks + 1)
        above.append(
            send(tow.at[0 : blocks + 1], tow.at[there : there + blocks + 1], tow_s.at[s], tow_r.at[slots.opposite(s)], s)
        )
    first = send_cells(lambda c: near0.at[0:pitch], rows_of(near0, pitch), n0_s, n0_r)
    second = send_cells(lambda c: near1.at[0:pitch], rows_of(near1, pitch), n1_s, n1_r)

    bit = jnp.left_shift(1, lax.broadcasted_iota(jnp.int32, (8, width), 0))
    term = lax.broadcasted_iota(jnp.int32, (TERMS, width), 0)
    early = jnp.where(term < 3, -1.0, 0.0)
    late = jnp.where((term >= 3) & (term < 6), -1.0, 0.0)
    shifted = jnp.where(term == 12, 0.5, early)
    ones = jnp.where((term >= 9) & (term < 13), 1.0, 0.0)
    plain = (early, late, shifted, early, jnp.zeros((TERMS, width), f32), shifted)
    for copy in fetches[8:]:
        copy.wait()

    def expand(k, carry):
        for w in range(words):
            hit = excl[0, k, w : w + 1, :] & bit
            allowed[pl.ds(pl.multiple_of(k * width + w * 8, 8), 8), :] = jnp.where(hit == 0, edge, -1.0)
        at = pl.ds(pl.multiple_of(k * TERMS, TERMS), TERMS)
        left0[at, :] = ones
        left1[at, :] = ones
        for g in range(6):
            at_g = pl.ds(pl.multiple_of((g * pairs + k) * TERMS, TERMS), TERMS)
            right[at_g, :] = plain[g]
        return carry

    lax.fori_loop(0, pairs, expand, 0)
    for c in range(HALVES):
        plate_sum[c][...] = jnp.zeros(plate_sum[c].shape, f32)
    half = vel[...] + 0.5 * time_step * fold[...] * mass[...]
    moved = pos[...] + time_step * half
    for b in range(blocks):
        at = slice(b * width, (b + 1) * width)
        half_b[b] = half[:, at]
        moved_b[b] = moved[:, at]
        mass_b[b] = mass[:, at]
    for q in range(mig_block.shape[1]):
        at = slice(q * width, (q + 1) * width)
        going_m[0:3, at] = moved_b[mig_block[0, q]]
        going_m[3:4, at] = jnp.full((1, width), mig_dest[0, q], jnp.int32).astype(f32)
    going_v[...] = jnp.zeros(going_v.shape, f32)
    come_m[0] = going_m[...]
    leavers = send_cells(lambda s: going_m, lambda s: come_m.at[s], mm_s, mm_r)
    block_of = lax.broadcasted_iota(jnp.int32, pos.shape, 1) // width
    gone = block_of == mig_block[0, 0]
    for q in range(1, mig_block.shape[1]):
        gone = gone | (block_of == mig_block[0, q])
    pos_out[...] = jnp.where(gone, 0.0, moved)

    my_layer = lax.axis_index("gz")
    t_all = tower_v[...]
    p_all = plate_v[...]
    live = lax.broadcasted_iota(jnp.int32, (1, pairs), 1) < counts[0]
    t_layer = t_all // blocks
    t_turn = t_layer - my_layer
    t_turn = jnp.where(t_turn < 0, t_turn + nz, t_turn)
    t_block = t_all - t_layer * blocks
    t_flat[...] = t_turn * (blocks + 1) + t_block
    t_row = jnp.where(live, t_turn * blocks + t_block, -1)
    p_cell = p_all // blocks
    p_number = jnp.zeros((1, pairs), jnp.int32)
    for o in range(9):
        number = slots.cell_number(slots.cell_slot(o // 3 - 1, o % 3 - 1))
        p_number = jnp.where(p_cell == o, number, p_number)
    p_block = p_all - p_cell * blocks
    p_flat[...] = p_number * pitch + p_block
    p_row = jnp.where(live, p_number * blocks + p_block, -1)
    tables = []
    for src, dst in ((t_flat, tower), (p_flat, plate)):
        tables.append(pltpu.make_async_copy(src, dst, local_sem.at[14 + len(tables)]))
        tables[-1].start()
    t_pick = jnp.where(
        lax.broadcasted_iota(jnp.int32, (nz * blocks, pairs), 0) == t_row, 1.0, 0.0
    ).astype(bf16)
    p_pick = jnp.where(
        lax.broadcasted_iota(jnp.int32, (cells * blocks, pairs), 0) == p_row, 1.0, 0.0
    ).astype(bf16)
    same = lax.broadcasted_iota(jnp.int32, (pairs, pairs), 0) == lax.broadcasted_iota(jnp.int32, (pairs, pairs), 1)
    t_col = jnp.sum(jnp.where(same, (t_turn * blocks + t_block).astype(f32), 0.0), axis=1, keepdims=True)
    p_col = jnp.sum(jnp.where(same, (p_number * blocks + p_block).astype(f32), 0.0), axis=1, keepdims=True)

    for copy in tables:
        copy.wait()
    for copy in above:
        copy.wait()

    lane_f = lax.broadcasted_iota(jnp.int32, (pairs, width), 1).astype(f32)

    def of_block(column, rows):
        found = jnp.zeros((pairs, width), f32)
        for s, row in enumerate(rows):
            found = found + jnp.where(lane_f == column - float(s * blocks), row, 0.0)
        return jnp.sum(found, axis=1, keepdims=True)

    sig_t = of_block(t_col, [tow[s * (blocks + 1) + blocks, 0:1, :] for s in range(nz)])
    dep_t = of_block(t_col, [tow[s * (blocks + 1) + blocks, 1:2, :] for s in range(nz)])
    def collect_towers(i, carry):
        for u in range(0, 16, 2):
            two = [tow[tower[0, i * 16 + u + v]] for v in range(2)]
            towers[pl.ds(pl.multiple_of(i * 64 + u * 4, 8), 8), :] = jnp.concatenate(two, axis=0)
        return carry

    lax.fori_loop(0, pairs // 16, collect_towers, 0)
    for r, groups in ((0, (0, 2)), (2, (1,)), (1, (3, 5)), (3, (4,))):
        terms = ((3, 4, 5), (6, 8), (7,)) if r == 3 else ((9,), (10,), (11,))
        for value, places in zip(split3(towers[pl.ds(r, pairs, stride=4), :]), terms):
            for t in places:
                for g in groups:
                    right[pl.ds(g * pairs * TERMS + t, pairs, stride=TERMS), :] = value
    def narrow(i, carry):
        for u in range(UNROLL):
            k = i * UNROLL + u
            row = pl.ds(pl.multiple_of(k * TERMS, TERMS), TERMS)
            for g in range(6):
                at = pl.ds(pl.multiple_of((g * pairs + k) * TERMS, TERMS), TERMS)
                right_b[row, g * width : (g + 1) * width] = right[at, :].astype(bf16)
        return carry

    lax.fori_loop(0, pairs // UNROLL, narrow, 0)
    for copy in named:
        copy.wait()
    sig_p = of_block(p_col, [kin[8 * c : 8 * c + 1, :] for c in range(cells)])
    dep_p = of_block(p_col, [kin[8 * c + 1 : 8 * c + 2, :] for c in range(cells)])
    sig = 0.5 * (sig_t + sig_p)
    sig2 = sig * sig
    sig6 = sig2 * sig2 * sig2
    depth = dep_t * dep_p
    att_tab[...] = jnp.broadcast_to((0.5 * lx**6) / sig6, (pairs, width))
    rep_col = (12.0 * scale / lx**12) * depth * sig6 * sig6
    rep_row = jnp.sum(jnp.where(same, rep_col, 0.0), axis=0, keepdims=True)
    charge_lanes = lax.broadcasted_iota(jnp.int32, (pairs, width), 1) >= part
    charge_scale = jnp.where(charge_lanes, 1.0 / rep_col, 1.0)

    def collect_plates(c):
        def body(i, carry):
            for u in range(16):
                p = plate[0, i * 16 + u]
                plates[i * 16 + u] = near[c][p]
                plates[pairs + i * 16 + u] = near[c][p + blocks]
            return carry

        lax.fori_loop(0, pairs // 16, body, 0)
        for r, terms in ((0, ((0,), (1,), (2,))), (1, ((3, 6, 7), (4, 8), (5,)))):
            rows = plates[r * pairs : (r + 1) * pairs, :]
            for value, places in zip(split3(rows * charge_scale if r else rows), terms):
                for t in places:
                    left[c][pl.ds(t, pairs, stride=TERMS), :] = value

    for copy in first:
        copy.wait()
    collect_plates(0)

    lane = lax.broadcasted_iota(jnp.int32, (8, pairs), 1)

    def prepare(k, c, made):
        at = pl.ds(pl.multiple_of(k * TERMS, TERMS), TERMS)
        a = left[c][at, :].T
        for i in range(2):
            made[:, 3 * i * width : 3 * (i + 1) * width] = jnp.dot(
                a[i * part : (i + 1) * part].astype(bf16),
                right_b[at, 3 * i * width : 3 * (i + 1) * width],
                preferred_element_type=f32,
            )

    def arithmetic(k, c, made):
        att = att_tab[pl.ds(k, 1), :]
        here = lane == k
        sums = [None, None, None]
        for w in range(part // 8):
            at = slice(w * 8, (w + 1) * 8)
            dx = made[at, 0:width] - jnp.floor(made[at, 2 * width : 3 * width])
            dz = made[at, width : 2 * width]
            dy = made[at, 3 * width : 4 * width] - jnp.floor(made[at, 5 * width : 6 * width])
            h = (dx * dx + dz * dz) + (ratio * (dy * dy) + shift_h)
            q = lax.rsqrt(h)
            f = jnp.maximum(allowed[pl.ds(pl.multiple_of(k * width + (c * part + w * 8), 8), 8), :] - h, 0.0)
            s = pl.reciprocal(h, approx=True)
            s3 = s * s * s
            fq = f * q
            g = fq * fq
            e = s3 * (s3 - att) + made[at, 4 * width : 5 * width] * q
            force_c = e * g
            parts = (force_c * dx, force_c * dy, force_c * dz)
            sums = [v if u is None else u + v for u, v in zip(sums, parts)]
            for r in range(3):
                total = jnp.broadcast_to(jnp.sum(parts[r], axis=1, keepdims=True), (8, pairs))
                pltpu.store(plate_sum[c].at[r * part + w * 8 : r * part + (w + 1) * 8, :], total, mask=here)
        for r in range(3):
            at = pl.ds(pl.multiple_of((r * pairs + k) * 8, 8), 8)
            tower_sum[at, :] = sums[r] if c == 0 else tower_sum[at, :] + sums[r]

    def run(c):
        for u in range(UNROLL):
            prepare(u, c, made_a.at[u])

        def step(i, carry):
            k = i * (GROUPS * UNROLL)
            for g in range(GROUPS):
                now, later = (made_a, made_b) if g % 2 == 0 else (made_b, made_a)
                for u in range(UNROLL):
                    ahead = k + (g + 1) * UNROLL + u
                    prepare(ahead if g + 1 < GROUPS else lax.rem(ahead, pairs), c, later.at[u])
                    arithmetic(k + g * UNROLL + u, c, now.at[u])
            return carry

        lax.fori_loop(0, pairs // (GROUPS * UNROLL), step, 0)
    def scatter(c):
        total = jnp.zeros((cells * blocks, 4 * part), f32)
        for piece in split2(plate_sum[c][...] * rep_row):
            total = total + lax.dot_general(p_pick, piece, (((1,), (1,)), ((), ())), preferred_element_type=f32)
        for s in range(cells):
            mine = total[s * blocks : (s + 1) * blocks]
            out_p[c][s, 0:blocks, :] = mine[:, 0:width]
            last = mine[:, width:]
            out_p[c][s, blocks:, :] = last[0 : blocks // 2] + pltpu.roll(last[blocks // 2 :], part, 1)
        return send_cells(lambda s: out_p[c].at[s], lambda s: land_p[c].at[s], (r0_s, r1_s)[c], (r0_r, r1_r)[c])

    run(0)
    for copy in second:
        copy.wait()
    collect_plates(1)
    returns = scatter(0)
    run(1)
    returns += scatter(1)
    for r in range(3):
        on_slot = tower_sum[pl.ds(r * pairs * 8, pairs, stride=8), :]
        for j in range(1, 8):
            on_slot = on_slot + tower_sum[pl.ds(r * pairs * 8 + j, pairs, stride=8), :]
        total = jnp.zeros((nz * blocks, width), f32)
        for piece in split2(on_slot * rep_col):
            total = total + jnp.dot(t_pick, piece, preferred_element_type=f32)
        for s in range(nz):
            out_t[s, :, r * width : (r + 1) * width] = total[s * blocks : (s + 1) * blocks]
    for s in range(1, nz):
        there = slots.opposite(s)
        returns.append(send(out_t.at[s], land_t.at[there], rt_s.at[s], rt_r.at[there], s))
    for copy in returns:
        copy.wait()

    back = []
    for c in range(HALVES):
        total = out_p[c][0]
        for s in range(1, cells):
            total = total + land_p[c][s]
        back.append(total)
    on_tower = out_t[0]
    for s in range(1, nz):
        on_tower = on_tower + land_t[s]
    (a0, a1), (z0, z1) = [v[0:blocks] for v in back], [v[blocks:] for v in back]
    low_z = low[0 : blocks // 2]
    on_plate = (
        jnp.where(low, a0, pltpu.roll(a1, part, 1)),
        jnp.where(low, pltpu.roll(a0, part, 1), a1),
        jnp.concatenate(
            [jnp.where(low_z, z0, pltpu.roll(z1, part, 1)), jnp.where(low_z, pltpu.roll(z0, part, 1), z1)], axis=0
        ),
    )
    for r in range(3):
        force[r] = (on_tower[:, r * width : (r + 1) * width] - on_plate[r]) * lengths[r]
    for q in range(mig_block.shape[1]):
        at = slice(q * width, (q + 1) * width)
        block = mig_block[0, q]
        kick = 0.5 * time_step * mass_b[block]
        old = half_b[block]
        for r in range(3):
            going_v[r : r + 1, at] = old[r : r + 1] + kick * force[r, block][None, :]
    come_v[0] = going_v[...]
    last_hop = send_cells(lambda s: going_v, lambda s: come_v.at[s], mv_s, mv_r)
    for r in range(3):
        for b in range(blocks):
            force_out[r : r + 1, b * width : (b + 1) * width] = force[r, b : b + 1]
    half = vel[...] + 0.5 * time_step * fold[...] * mass[...]
    block_of = lax.broadcasted_iota(jnp.int32, pos.shape, 1) // width
    gone = block_of == mig_block[0, 0]
    for q in range(1, mig_block.shape[1]):
        gone = gone | (block_of == mig_block[0, q])
    vel_out[...] = jnp.where(gone, 0.0, half + 0.5 * time_step * force_out[...] * mass[...])
    for copy in leavers:
        copy.wait()
    wanted = []
    for i, (a, b) in enumerate(source_offsets):
        cell = slots.cell_number(slots.cell_slot(a, b))
        wanted.append((cell, come_m[cell, 3:4, :] == float((1 - a) * 3 + (1 - b))))
        for r in range(3):
            arrive[r, 0, i : i + 1, :] = jnp.where(wanted[i][1], come_m[cell, r : r + 1, :], 0.0)
    for copy in last_hop:
        copy.wait()
    for i, (cell, chosen) in enumerate(wanted):
        for r in range(3):
            arrive[3 + r, 0, i : i + 1, :] = jnp.where(chosen, come_v[cell, r : r + 1, :], 0.0)


def output_kernel(*refs):
    sem = refs[-1]
    copies = [pltpu.make_async_copy(refs[i], refs[4 + i], sem.at[i]) for i in range(4)]
    for copy in copies:
        copy.start()
    for copy in copies:
        copy.wait()


def local(
    slots, positions, velocities, forces_old, inv_mass, charges, block_species, sigma_table, epsilon_table,
    tower_index, plate_index, tile_counts, exclusions, mig_block, mig_dest,
):
    atoms = positions.shape[1]
    blocks = block_species.shape[0]
    width = atoms // blocks
    nz, cells = slots.nz, slots.cells
    pairs = tower_index.shape[1]
    leaving = mig_block.shape[1]
    kinds = sigma_table.shape[0]
    part = width // HALVES
    pitch = 2 * blocks
    hbm = pl.BlockSpec(memory_space=pltpu.HBM)
    vmem = pl.BlockSpec(memory_space=pltpu.VMEM)
    mass = inv_mass[None, :]
    f32, i32 = jnp.float32, jnp.int32

    def sems(n):
        return pltpu.SemaphoreType.DMA((n,))

    def v(*shape):
        return pltpu.VMEM(shape, f32)

    rows = jax.ShapeDtypeStruct((3, atoms), f32)
    arrive = jax.ShapeDtypeStruct((6, 1, len(source_offsets), leaving * width), f32)
    held = tuple(pltpu.VMEM(a.shape, f32) for a in (rows, rows, rows, arrive))
    made = pl.pallas_call(
        functools.partial(step_kernel, slots, blocks),
        out_shape=held,
        in_specs=[hbm] * 14,
        out_specs=(vmem,) * 4,
        scratch_shapes=[
            v(3, atoms), v(3, atoms), v(3, atoms), v(1, atoms), v(1, atoms), pltpu.VMEM((1, blocks), i32),
            pltpu.SMEM((kinds,), f32), pltpu.SMEM((kinds,), f32),
            pltpu.SMEM((1, pairs), i32), pltpu.SMEM((1, pairs), i32),
            pltpu.VMEM((1, pairs), i32), pltpu.VMEM((1, pairs), i32),
            pltpu.SMEM((1,), i32), pltpu.VMEM(exclusions.shape, i32),
            pltpu.SMEM((1, leaving), i32), pltpu.SMEM((1, leaving), i32),
            v(blocks, 3, width), v(blocks, 3, width), v(blocks, 1, width), v(4 * blocks, width), v(nz * (blocks + 1), 4, width),
            v(8 * cells, width), v(cells * pitch, width), v(cells * pitch, width),
            v(pairs * width, width), v(pairs, width), v(4 * pairs, width), v(2 * pairs, width),
            v(6 * pairs * TERMS, width), pltpu.VMEM((pairs * TERMS, 6 * width), jnp.bfloat16), v(pairs * TERMS, width), v(pairs * TERMS, width),
            v(UNROLL, part, 6 * width), v(UNROLL, part, 6 * width), v(3 * 8 * pairs, width), v(4 * part, pairs), v(4 * part, pairs),
            v(nz, blocks, 3 * width), v(cells, blocks + blocks // 2, width), v(cells, blocks + blocks // 2, width),
            v(nz, blocks, 3 * width), v(cells, blocks + blocks // 2, width), v(cells, blocks + blocks // 2, width),
            v(4, leaving * width), v(4, leaving * width), v(cells, 4, leaving * width), v(cells, 4, leaving * width),
            v(3, blocks, width),
            pltpu.VMEM((1, pairs), i32), pltpu.VMEM((1, pairs), i32), sems(16),
        ]
        + [sems(cells)] * 2 + [sems(nz)] * 2 + [sems(cells)] * 4 + [sems(nz)] * 2 + [sems(cells)] * 8,
        compiler_params=pltpu.CompilerParams(
            collective_id=0, has_side_effects=True, vmem_limit_bytes=60 * 1024 * 1024
        ),
        name="membrane_step",
    )(
        positions, velocities, forces_old, mass, charges[None, :], block_species[None, :], sigma_table,
        epsilon_table, tower_index, plate_index, tile_counts, exclusions, mig_block, mig_dest,
    )
    return pl.pallas_call(
        output_kernel,
        out_shape=(rows, rows, rows, arrive),
        in_specs=[vmem] * 4,
        out_specs=(hbm,) * 4,
        scratch_shapes=[sems(4)],
        compiler_params=pltpu.CompilerParams(vmem_limit_bytes=1024 * 1024),
        name="outputs",
    )(*made)


def solution(mesh):
    cells = ("gx", "gy", "gz")
    slots = Slots(mesh.shape["gx"], mesh.shape["gy"], mesh.shape["gz"])
    row = P(None, cells)
    flat = P(cells)
    pair = P(cells, None)
    in_specs = (
        row, row, row, flat, flat, flat, P(), P(), pair, pair, flat, P(cells, None, None, None), pair, pair,
    )
    out_specs = (row, row, row, P(None, cells, None, None))
    return jax.shard_map(
        functools.partial(local, slots), mesh=mesh, in_specs=in_specs, out_specs=out_specs, check_vma=False
    )
```

```python
import functools
import jax
import jax.numpy as jnp
from jax import lax
from jax.experimental import pallas as pl
from jax.experimental.pallas import tpu as pltpu
from jax.sharding import PartitionSpec as P

time_step = 0.2
soft_core = 0.09
cutoff_sq = 1.44
coulomb_k = 0.5
MESH = pl.DeviceIdType.MESH
UNROLL = 4
GROUPS = 4
HALVES = 2
TERMS = 16
source_offsets = ((-1, -1), (-1, 0), (-1, 1), (0, -1), (0, 1), (1, -1), (1, 0), (1, 1))


class Slots:
    def __init__(self, nx, ny, nz):
        self.nx, self.ny, self.nz = nx, ny, nz
        self.offsets = [(0, 0, 0)] + [(0, 0, k) for k in range(1, nz)]
        self.cell = {(0, 0): 0}
        for da in range(-1, 2):
            for db in range(-1, 2):
                key = (da % nx, db % ny)
                if key not in self.cell:
                    self.cell[key] = len(self.offsets)
                    self.offsets.append((key[0], key[1], 0))
        self.count = len(self.offsets)
        self.cells = 1 + self.count - nz

    def cell_slot(self, da, db):
        return self.cell[(da % self.nx, db % self.ny)]

    def cell_number(self, slot):
        return slot - self.nz + 1 if slot else 0

    def opposite(self, slot):
        dx, dy, dz = self.offsets[slot]
        if dz:
            return (self.nz - dz) % self.nz
        return self.cell_slot(-dx, -dy)

    def device(self, slot):
        dx, dy, dz = self.offsets[slot]
        return (
            lax.rem(lax.axis_index("gx") + dx, self.nx),
            lax.rem(lax.axis_index("gy") + dy, self.ny),
            lax.rem(lax.axis_index("gz") + dz, self.nz),
        )


def split3(value):
    high = value.astype(jnp.bfloat16).astype(jnp.float32)
    rest = value - high
    mid = rest.astype(jnp.bfloat16).astype(jnp.float32)
    return high, mid, rest - mid


def split2(value):
    high = value.astype(jnp.bfloat16)
    return high, (value - high.astype(jnp.float32)).astype(jnp.bfloat16)


def step_kernel(
    slots, blocks,
    pos_h, vel_h, fold_h, mass_h, charge_h, species_h, sigma_h, eps_h, tower_h, plate_h, counts_h, excl_h,
    mig_block_h, mig_dest_h,
    pos_out, vel_out, force_out, arrive,
    pos, vel, fold, mass, charge, species, sigma_s, eps_s, tower, plate, tower_v, plate_v, counts, excl,
    mig_block, mig_dest,
    half_b, moved_b, mass_b, dense, tow, kin, near0, near1, allowed, att_tab, towers, plates, right, right_b, left0, left1,
    made_a, made_b, tower_sum, plate_sum0, plate_sum1, out_t, out_p0, out_p1, land_t, land_p0, land_p1, going_m, going_v, come_m, come_v,
    force,
    t_flat, p_flat, local_sem,
    kn_s, kn_r, tow_s, tow_r, n0_s, n0_r, n1_s, n1_r, rt_s, rt_r, r0_s, r0_r, r1_s, r1_r, mm_s, mm_r, mv_s, mv_r,
):
    atoms = pos.shape[1]
    width = atoms // blocks
    pairs = tower.shape[1]
    words = excl.shape[2]
    part = width // HALVES
    pitch = 2 * blocks
    nx, ny, nz, cells = slots.nx, slots.ny, slots.nz, slots.cells
    lx, ly = float(nx), float(ny)
    lengths = (lx, ly, lx)
    f32 = jnp.float32
    bf16 = jnp.bfloat16
    near = (near0, near1)
    left = (left0, left1)
    plate_sum = (plate_sum0, plate_sum1)
    out_p = (out_p0, out_p1)
    land_p = (land_p0, land_p1)
    ratio = (ly / lx) ** 2
    shift_h = soft_core / (lx * lx)
    edge = (cutoff_sq + soft_core) / (lx * lx)
    scale = lx * lx / (cutoff_sq * cutoff_sq)

    barrier = pltpu.get_barrier_semaphore()
    for s in range(1, slots.count):
        pl.semaphore_signal(barrier, inc=1, device_id=slots.device(s), device_id_type=MESH)
    fetches = []
    for src, dst in (
        (pos_h, pos), (vel_h, vel), (fold_h, fold), (mass_h, mass), (charge_h, charge), (species_h, species),
        (sigma_h, sigma_s), (eps_h, eps_s), (excl_h, excl),
        (tower_h, tower_v), (plate_h, plate_v), (counts_h, counts), (mig_block_h, mig_block), (mig_dest_h, mig_dest),
    ):
        copy = pltpu.make_async_copy(src, dst, local_sem.at[len(fetches)])
        copy.start()
        fetches.append(copy)
    for copy in fetches[:8]:
        copy.wait()

    half = vel[...] + 0.5 * time_step * fold[...] * mass[...]
    moved = pos[...] + time_step * half
    row3 = lax.broadcasted_iota(jnp.int32, (3, atoms), 0)
    scaled = moved * jnp.where(row3 == 1, f32(1.0 / ly), f32(1.0 / lx))
    tower_charge = charge[...] * (coulomb_k * scale / lx)
    for b in range(blocks):
        at = slice(b * width, (b + 1) * width)
        tow[b, 0:3, :] = scaled[:, at]
        tow[b, 3:4, :] = tower_charge[:, at]
        for r in range(3):
            dense[r * blocks + b : r * blocks + b + 1, :] = scaled[r : r + 1, at]
        dense[3 * blocks + b : 3 * blocks + b + 1, :] = charge[:, at]
    which = species[...]
    sigma = jnp.zeros((1, blocks), f32)
    eps = jnp.zeros((1, blocks), f32)
    for k in range(sigma_s.shape[0]):
        sigma = jnp.where(which == k, sigma_s[k], sigma)
        eps = jnp.where(which == k, eps_s[k], eps)
    depth_row = jnp.sqrt(eps)
    tow[blocks] = jnp.zeros((4, width), f32)
    tow[blocks, 0:1, 0:blocks] = sigma
    tow[blocks, 1:2, 0:blocks] = depth_row
    kin[0:8, :] = jnp.zeros((8, width), f32)
    kin[0:1, 0:blocks] = sigma
    kin[1:2, 0:blocks] = depth_row
    low = lax.broadcasted_iota(jnp.int32, (blocks, width), 1) < part
    comp = [dense[r * blocks : (r + 1) * blocks, :] for r in range(4)]
    turned = [pltpu.roll(v, part, 1) for v in comp]
    near0[0:blocks, :] = jnp.where(low, comp[0], turned[1])
    near0[blocks : 2 * blocks, :] = jnp.where(low, comp[2], turned[3])
    near1[0:blocks, :] = jnp.where(low, turned[0], comp[1])
    near1[blocks : 2 * blocks, :] = jnp.where(low, turned[2], comp[3])

    pl.semaphore_wait(barrier, slots.count - 1)

    def send(src, dst, ss, rs, s):
        copy = pltpu.make_async_remote_copy(
            src_ref=src, dst_ref=dst, send_sem=ss, recv_sem=rs, device_id=slots.device(s), device_id_type=MESH
        )
        copy.start()
        return copy

    def send_cells(source, landing, ss, rs):
        copies = []
        for s in range(nz, slots.count):
            here, there = slots.cell_number(s), slots.cell_number(slots.opposite(s))
            copies.append(send(source(here), landing(there), ss.at[here], rs.at[there], s))
        return copies

    def rows_of(ref, size):
        return lambda c: ref.at[c * size : (c + 1) * size]

    named = send_cells(lambda c: kin.at[0:8], rows_of(kin, 8), kn_s, kn_r)
    above = []
    for s in range(1, nz):
        there = slots.opposite(s) * (blocks + 1)
        above.append(
            send(tow.at[0 : blocks + 1], tow.at[there : there + blocks + 1], tow_s.at[s], tow_r.at[slots.opposite(s)], s)
        )
    first = send_cells(lambda c: near0.at[0:pitch], rows_of(near0, pitch), n0_s, n0_r)
    second = send_cells(lambda c: near1.at[0:pitch], rows_of(near1, pitch), n1_s, n1_r)

    bit = jnp.left_shift(1, lax.broadcasted_iota(jnp.int32, (8, width), 0))
    term = lax.broadcasted_iota(jnp.int32, (TERMS, width), 0)
    early = jnp.where(term < 3, -1.0, 0.0)
    late = jnp.where((term >= 3) & (term < 6), -1.0, 0.0)
    shifted = jnp.where(term == 12, 0.5, early)
    ones = jnp.where((term >= 9) & (term < 13), 1.0, 0.0)
    plain = (early, late, shifted, early, jnp.zeros((TERMS, width), f32), shifted)
    for copy in fetches[8:]:
        copy.wait()

    def expand(k, carry):
        for w in range(words):
            hit = excl[0, k, w : w + 1, :] & bit
            allowed[pl.ds(pl.multiple_of(k * width + w * 8, 8), 8), :] = jnp.where(hit == 0, edge, -1.0)
        at = pl.ds(pl.multiple_of(k * TERMS, TERMS), TERMS)
        left0[at, :] = ones
        left1[at, :] = ones
        for g in range(6):
            at_g = pl.ds(pl.multiple_of((g * pairs + k) * TERMS, TERMS), TERMS)
            right[at_g, :] = plain[g]
        return carry

    lax.fori_loop(0, pairs, expand, 0)
    for c in range(HALVES):
        plate_sum[c][...] = jnp.zeros(plate_sum[c].shape, f32)
    half = vel[...] + 0.5 * time_step * fold[...] * mass[...]
    moved = pos[...] + time_step * half
    for b in range(blocks):
        at = slice(b * width, (b + 1) * width)
        half_b[b] = half[:, at]
        moved_b[b] = moved[:, at]
        mass_b[b] = mass[:, at]
    for q in range(mig_block.shape[1]):
        at = slice(q * width, (q + 1) * width)
        going_m[0:3, at] = moved_b[mig_block[0, q]]
        going_m[3:4, at] = jnp.full((1, width), mig_dest[0, q], jnp.int32).astype(f32)
    going_v[...] = jnp.zeros(going_v.shape, f32)
    come_m[0] = going_m[...]
    leavers = send_cells(lambda s: going_m, lambda s: come_m.at[s], mm_s, mm_r)
    block_of = lax.broadcasted_iota(jnp.int32, pos.shape, 1) // width
    gone = block_of == mig_block[0, 0]
    for q in range(1, mig_block.shape[1]):
        gone = gone | (block_of == mig_block[0, q])
    pos_out[...] = jnp.where(gone, 0.0, moved)

    my_layer = lax.axis_index("gz")
    t_all = tower_v[...]
    p_all = plate_v[...]
    live = lax.broadcasted_iota(jnp.int32, (1, pairs), 1) < counts[0]
    t_layer = t_all // blocks
    t_turn = t_layer - my_layer
    t_turn = jnp.where(t_turn < 0, t_turn + nz, t_turn)
    t_block = t_all - t_layer * blocks
    t_flat[...] = t_turn * (blocks + 1) + t_block
    t_row = jnp.where(live, t_turn * blocks + t_block, -1)
    p_cell = p_all // blocks
    p_number = jnp.zeros((1, pairs), jnp.int32)
    for o in range(9):
        number = slots.cell_number(slots.cell_slot(o // 3 - 1, o % 3 - 1))
        p_number = jnp.where(p_cell == o, number, p_number)
    p_block = p_all - p_cell * blocks
    p_flat[...] = p_number * pitch + p_block
    p_row = jnp.where(live, p_number * blocks + p_block, -1)
    tables = []
    for src, dst in ((t_flat, tower), (p_flat, plate)):
        tables.append(pltpu.make_async_copy(src, dst, local_sem.at[14 + len(tables)]))
        tables[-1].start()
    t_pick = jnp.where(
        lax.broadcasted_iota(jnp.int32, (nz * blocks, pairs), 0) == t_row, 1.0, 0.0
    ).astype(bf16)
    p_pick = jnp.where(
        lax.broadcasted_iota(jnp.int32, (cells * blocks, pairs), 0) == p_row, 1.0, 0.0
    ).astype(bf16)
    same = lax.broadcasted_iota(jnp.int32, (pairs, pairs), 0) == lax.broadcasted_iota(jnp.int32, (pairs, pairs), 1)
    t_col = jnp.sum(jnp.where(same, (t_turn * blocks + t_block).astype(f32), 0.0), axis=1, keepdims=True)
    p_col = jnp.sum(jnp.where(same, (p_number * blocks + p_block).astype(f32), 0.0), axis=1, keepdims=True)

    for copy in tables:
        copy.wait()
    for copy in above:
        copy.wait()

    lane_f = lax.broadcasted_iota(jnp.int32, (pairs, width), 1).astype(f32)

    def of_block(column, rows):
        found = jnp.zeros((pairs, width), f32)
        for s, row in enumerate(rows):
            found = found + jnp.where(lane_f == column - float(s * blocks), row, 0.0)
        return jnp.sum(found, axis=1, keepdims=True)

    sig_t = of_block(t_col, [tow[s * (blocks + 1) + blocks, 0:1, :] for s in range(nz)])
    dep_t = of_block(t_col, [tow[s * (blocks + 1) + blocks, 1:2, :] for s in range(nz)])
    def collect_towers(i, carry):
        for u in range(0, 16, 2):
            two = [tow[tower[0, i * 16 + u + v]] for v in range(2)]
            towers[pl.ds(pl.multiple_of(i * 64 + u * 4, 8), 8), :] = jnp.concatenate(two, axis=0)
        return carry

    lax.fori_loop(0, pairs // 16, collect_towers, 0)
    for r, groups in ((0, (0, 2)), (2, (1,)), (1, (3, 5)), (3, (4,))):
        terms = ((3, 4, 5), (6, 8), (7,)) if r == 3 else ((9,), (10,), (11,))
        for value, places in zip(split3(towers[pl.ds(r, pairs, stride=4), :]), terms):
            for t in places:
                for g in groups:
                    right[pl.ds(g * pairs * TERMS + t, pairs, stride=TERMS), :] = value
    def narrow(i, carry):
        for u in range(UNROLL):
            k = i * UNROLL + u
            row = pl.ds(pl.multiple_of(k * TERMS, TERMS), TERMS)
            for g in range(6):
                at = pl.ds(pl.multiple_of((g * pairs + k) * TERMS, TERMS), TERMS)
                right_b[row, g * width : (g + 1) * width] = right[at, :].astype(bf16)
        return carry

    lax.fori_loop(0, pairs // UNROLL, narrow, 0)
    for copy in named:
        copy.wait()
    sig_p = of_block(p_col, [kin[8 * c : 8 * c + 1, :] for c in range(cells)])
    dep_p = of_block(p_col, [kin[8 * c + 1 : 8 * c + 2, :] for c in range(cells)])
    sig = 0.5 * (sig_t + sig_p)
    sig2 = sig * sig
    sig6 = sig2 * sig2 * sig2
    depth = dep_t * dep_p
    att_tab[...] = jnp.broadcast_to((0.5 * lx**6) / sig6, (pairs, width))
    rep_col = (12.0 * scale / lx**12) * depth * sig6 * sig6
    rep_row = jnp.sum(jnp.where(same, rep_col, 0.0), axis=0, keepdims=True)
    charge_lanes = lax.broadcasted_iota(jnp.int32, (pairs, width), 1) >= part
    charge_scale = jnp.where(charge_lanes, 1.0 / rep_col, 1.0)

    def collect_plates(c):
        def body(i, carry):
            for u in range(16):
                p = plate[0, i * 16 + u]
                plates[i * 16 + u] = near[c][p]
                plates[pairs + i * 16 + u] = near[c][p + blocks]
            return carry

        lax.fori_loop(0, pairs // 16, body, 0)
        for r, terms in ((0, ((0,), (1,), (2,))), (1, ((3, 6, 7), (4, 8), (5,)))):
            rows = plates[r * pairs : (r + 1) * pairs, :]
            for value, places in zip(split3(rows * charge_scale if r else rows), terms):
                for t in places:
                    left[c][pl.ds(t, pairs, stride=TERMS), :] = value

    for copy in first:
        copy.wait()
    collect_plates(0)

    lane = lax.broadcasted_iota(jnp.int32, (8, pairs), 1)

    def prepare(k, c, made):
        at = pl.ds(pl.multiple_of(k * TERMS, TERMS), TERMS)
        a = left[c][at, :].T
        for i in range(2):
            made[:, 3 * i * width : 3 * (i + 1) * width] = jnp.dot(
                a[i * part : (i + 1) * part].astype(bf16),
                right_b[at, 3 * i * width : 3 * (i + 1) * width],
                preferred_element_type=f32,
            )

    def arithmetic(k, c, made):
        att = att_tab[pl.ds(k, 1), :]
        here = lane == k
        sums = [None, None, None]
        for w in range(part // 8):
            at = slice(w * 8, (w + 1) * 8)
            dx = made[at, 0:width] - jnp.floor(made[at, 2 * width : 3 * width])
            dz = made[at, width : 2 * width]
            dy = made[at, 3 * width : 4 * width] - jnp.floor(made[at, 5 * width : 6 * width])
            h = (dx * dx + dz * dz) + (ratio * (dy * dy) + shift_h)
            q = lax.rsqrt(h)
            f = jnp.maximum(allowed[pl.ds(pl.multiple_of(k * width + (c * part + w * 8), 8), 8), :] - h, 0.0)
            s = q * q
            s3 = s * s * s
            fq = f * q
            g = fq * fq
            e = s3 * (s3 - att) + made[at, 4 * width : 5 * width] * q
            force_c = e * g
            parts = (force_c * dx, force_c * dy, force_c * dz)
            sums = [v if u is None else u + v for u, v in zip(sums, parts)]
            for r in range(3):
                total = jnp.broadcast_to(jnp.sum(parts[r], axis=1, keepdims=True), (8, pairs))
                pltpu.store(plate_sum[c].at[r * part + w * 8 : r * part + (w + 1) * 8, :], total, mask=here)
        for r in range(3):
            at = pl.ds(pl.multiple_of((r * pairs + k) * 8, 8), 8)
            tower_sum[at, :] = sums[r] if c == 0 else tower_sum[at, :] + sums[r]

    def run(c):
        for u in range(UNROLL):
            prepare(u, c, made_a.at[u])

        def step(i, carry):
            k = i * (GROUPS * UNROLL)
            for g in range(GROUPS):
                now, later = (made_a, made_b) if g % 2 == 0 else (made_b, made_a)
                for u in range(UNROLL):
                    ahead = k + (g + 1) * UNROLL + u
                    prepare(ahead if g + 1 < GROUPS else lax.rem(ahead, pairs), c, later.at[u])
                    arithmetic(k + g * UNROLL + u, c, now.at[u])
            return carry

        lax.fori_loop(0, pairs // (GROUPS * UNROLL), step, 0)
    def scatter(c):
        total = jnp.zeros((cells * blocks, 4 * part), f32)
        for piece in split2(plate_sum[c][...] * rep_row):
            total = total + lax.dot_general(p_pick, piece, (((1,), (1,)), ((), ())), preferred_element_type=f32)
        for s in range(cells):
            mine = total[s * blocks : (s + 1) * blocks]
            out_p[c][s, 0:blocks, :] = mine[:, 0:width]
            last = mine[:, width:]
            out_p[c][s, blocks:, :] = last[0 : blocks // 2] + pltpu.roll(last[blocks // 2 :], part, 1)
        return send_cells(lambda s: out_p[c].at[s], lambda s: land_p[c].at[s], (r0_s, r1_s)[c], (r0_r, r1_r)[c])

    run(0)
    for copy in second:
        copy.wait()
    collect_plates(1)
    returns = scatter(0)
    run(1)
    returns += scatter(1)
    for r in range(3):
        on_slot = tower_sum[pl.ds(r * pairs * 8, pairs, stride=8), :]
        for j in range(1, 8):
            on_slot = on_slot + tower_sum[pl.ds(r * pairs * 8 + j, pairs, stride=8), :]
        total = jnp.zeros((nz * blocks, width), f32)
        for piece in split2(on_slot * rep_col):
            total = total + jnp.dot(t_pick, piece, preferred_element_type=f32)
        for s in range(nz):
            out_t[s, :, r * width : (r + 1) * width] = total[s * blocks : (s + 1) * blocks]
    for s in range(1, nz):
        there = slots.opposite(s)
        returns.append(send(out_t.at[s], land_t.at[there], rt_s.at[s], rt_r.at[there], s))
    for copy in returns[HALVES * (cells - 1) :]:
        copy.wait()
    on_tower = out_t[0]
    for s in range(1, nz):
        on_tower = on_tower + land_t[s]
    back = []
    for c in range(HALVES):
        for copy in returns[c * (cells - 1) : (c + 1) * (cells - 1)]:
            copy.wait()
        total = out_p[c][0]
        for s in range(1, cells):
            total = total + land_p[c][s]
        back.append(total)
    (a0, a1), (z0, z1) = [v[0:blocks] for v in back], [v[blocks:] for v in back]
    low_z = low[0 : blocks // 2]
    on_plate = (
        jnp.where(low, a0, pltpu.roll(a1, part, 1)),
        jnp.where(low, pltpu.roll(a0, part, 1), a1),
        jnp.concatenate(
            [jnp.where(low_z, z0, pltpu.roll(z1, part, 1)), jnp.where(low_z, pltpu.roll(z0, part, 1), z1)], axis=0
        ),
    )
    for r in range(3):
        force[r] = (on_tower[:, r * width : (r + 1) * width] - on_plate[r]) * lengths[r]
    for q in range(mig_block.shape[1]):
        at = slice(q * width, (q + 1) * width)
        block = mig_block[0, q]
        kick = 0.5 * time_step * mass_b[block]
        old = half_b[block]
        for r in range(3):
            going_v[r : r + 1, at] = old[r : r + 1] + kick * force[r, block][None, :]
    come_v[0] = going_v[...]
    last_hop = send_cells(lambda s: going_v, lambda s: come_v.at[s], mv_s, mv_r)
    for r in range(3):
        for b in range(blocks):
            force_out[r : r + 1, b * width : (b + 1) * width] = force[r, b : b + 1]
    half = vel[...] + 0.5 * time_step * fold[...] * mass[...]
    block_of = lax.broadcasted_iota(jnp.int32, pos.shape, 1) // width
    gone = block_of == mig_block[0, 0]
    for q in range(1, mig_block.shape[1]):
        gone = gone | (block_of == mig_block[0, q])
    vel_out[...] = jnp.where(gone, 0.0, half + 0.5 * time_step * force_out[...] * mass[...])
    for copy in leavers:
        copy.wait()
    wanted = []
    for i, (a, b) in enumerate(source_offsets):
        cell = slots.cell_number(slots.cell_slot(a, b))
        wanted.append((cell, come_m[cell, 3:4, :] == float((1 - a) * 3 + (1 - b))))
        for r in range(3):
            arrive[r, 0, i : i + 1, :] = jnp.where(wanted[i][1], come_m[cell, r : r + 1, :], 0.0)
    for copy in last_hop:
        copy.wait()
    for i, (cell, chosen) in enumerate(wanted):
        for r in range(3):
            arrive[3 + r, 0, i : i + 1, :] = jnp.where(chosen, come_v[cell, r : r + 1, :], 0.0)


def output_kernel(*refs):
    sem = refs[-1]
    copies = [pltpu.make_async_copy(refs[i], refs[4 + i], sem.at[i]) for i in range(4)]
    for copy in copies:
        copy.start()
    for copy in copies:
        copy.wait()


def local(
    slots, positions, velocities, forces_old, inv_mass, charges, block_species, sigma_table, epsilon_table,
    tower_index, plate_index, tile_counts, exclusions, mig_block, mig_dest,
):
    atoms = positions.shape[1]
    blocks = block_species.shape[0]
    width = atoms // blocks
    nz, cells = slots.nz, slots.cells
    pairs = tower_index.shape[1]
    leaving = mig_block.shape[1]
    kinds = sigma_table.shape[0]
    part = width // HALVES
    pitch = 2 * blocks
    hbm = pl.BlockSpec(memory_space=pltpu.HBM)
    vmem = pl.BlockSpec(memory_space=pltpu.VMEM)
    mass = inv_mass[None, :]
    f32, i32 = jnp.float32, jnp.int32

    def sems(n):
        return pltpu.SemaphoreType.DMA((n,))

    def v(*shape):
        return pltpu.VMEM(shape, f32)

    rows = jax.ShapeDtypeStruct((3, atoms), f32)
    arrive = jax.ShapeDtypeStruct((6, 1, len(source_offsets), leaving * width), f32)
    held = tuple(pltpu.VMEM(a.shape, f32) for a in (rows, rows, rows, arrive))
    made = pl.pallas_call(
        functools.partial(step_kernel, slots, blocks),
        out_shape=held,
        in_specs=[hbm] * 14,
        out_specs=(vmem,) * 4,
        scratch_shapes=[
            v(3, atoms), v(3, atoms), v(3, atoms), v(1, atoms), v(1, atoms), pltpu.VMEM((1, blocks), i32),
            pltpu.SMEM((kinds,), f32), pltpu.SMEM((kinds,), f32),
            pltpu.SMEM((1, pairs), i32), pltpu.SMEM((1, pairs), i32),
            pltpu.VMEM((1, pairs), i32), pltpu.VMEM((1, pairs), i32),
            pltpu.SMEM((1,), i32), pltpu.VMEM(exclusions.shape, i32),
            pltpu.SMEM((1, leaving), i32), pltpu.SMEM((1, leaving), i32),
            v(blocks, 3, width), v(blocks, 3, width), v(blocks, 1, width), v(4 * blocks, width), v(nz * (blocks + 1), 4, width),
            v(8 * cells, width), v(cells * pitch, width), v(cells * pitch, width),
            v(pairs * width, width), v(pairs, width), v(4 * pairs, width), v(2 * pairs, width),
            v(6 * pairs * TERMS, width), pltpu.VMEM((pairs * TERMS, 6 * width), jnp.bfloat16), v(pairs * TERMS, width), v(pairs * TERMS, width),
            v(UNROLL, part, 6 * width), v(UNROLL, part, 6 * width), v(3 * 8 * pairs, width), v(4 * part, pairs), v(4 * part, pairs),
            v(nz, blocks, 3 * width), v(cells, blocks + blocks // 2, width), v(cells, blocks + blocks // 2, width),
            v(nz, blocks, 3 * width), v(cells, blocks + blocks // 2, width), v(cells, blocks + blocks // 2, width),
            v(4, leaving * width), v(4, leaving * width), v(cells, 4, leaving * width), v(cells, 4, leaving * width),
            v(3, blocks, width),
            pltpu.VMEM((1, pairs), i32), pltpu.VMEM((1, pairs), i32), sems(16),
        ]
        + [sems(cells)] * 2 + [sems(nz)] * 2 + [sems(cells)] * 4 + [sems(nz)] * 2 + [sems(cells)] * 8,
        compiler_params=pltpu.CompilerParams(
            collective_id=0, has_side_effects=True, vmem_limit_bytes=60 * 1024 * 1024
        ),
        name="membrane_step",
    )(
        positions, velocities, forces_old, mass, charges[None, :], block_species[None, :], sigma_table,
        epsilon_table, tower_index, plate_index, tile_counts, exclusions, mig_block, mig_dest,
    )
    return pl.pallas_call(
        output_kernel,
        out_shape=(rows, rows, rows, arrive),
        in_specs=[vmem] * 4,
        out_specs=(hbm,) * 4,
        scratch_shapes=[sems(4)],
        compiler_params=pltpu.CompilerParams(vmem_limit_bytes=1024 * 1024),
        name="outputs",
    )(*made)


def solution(mesh):
    cells = ("gx", "gy", "gz")
    slots = Slots(mesh.shape["gx"], mesh.shape["gy"], mesh.shape["gz"])
    row = P(None, cells)
    flat = P(cells)
    pair = P(cells, None)
    in_specs = (
        row, row, row, flat, flat, flat, P(), P(), pair, pair, flat, P(cells, None, None, None), pair, pair,
    )
    out_specs = (row, row, row, P(None, cells, None, None))
    return jax.shard_map(
        functools.partial(local, slots), mesh=mesh, in_specs=in_specs, out_specs=out_specs, check_vma=False
    )
```

```python
import functools
import jax
import jax.numpy as jnp
from jax import lax
from jax.experimental import pallas as pl
from jax.experimental.pallas import tpu as pltpu
from jax.sharding import PartitionSpec as P

time_step = 0.2
soft_core = 0.09
cutoff_sq = 1.44
coulomb_k = 0.5
MESH = pl.DeviceIdType.MESH
UNROLL = 4
GROUPS = 4
HALVES = 2
TERMS = 16
source_offsets = ((-1, -1), (-1, 0), (-1, 1), (0, -1), (0, 1), (1, -1), (1, 0), (1, 1))


class Slots:
    def __init__(self, nx, ny, nz):
        self.nx, self.ny, self.nz = nx, ny, nz
        self.offsets = [(0, 0, 0)] + [(0, 0, k) for k in range(1, nz)]
        self.cell = {(0, 0): 0}
        for da in range(-1, 2):
            for db in range(-1, 2):
                key = (da % nx, db % ny)
                if key not in self.cell:
                    self.cell[key] = len(self.offsets)
                    self.offsets.append((key[0], key[1], 0))
        self.count = len(self.offsets)
        self.cells = 1 + self.count - nz

    def cell_slot(self, da, db):
        return self.cell[(da % self.nx, db % self.ny)]

    def cell_number(self, slot):
        return slot - self.nz + 1 if slot else 0

    def opposite(self, slot):
        dx, dy, dz = self.offsets[slot]
        if dz:
            return (self.nz - dz) % self.nz
        return self.cell_slot(-dx, -dy)

    def device(self, slot):
        dx, dy, dz = self.offsets[slot]
        return (
            lax.rem(lax.axis_index("gx") + dx, self.nx),
            lax.rem(lax.axis_index("gy") + dy, self.ny),
            lax.rem(lax.axis_index("gz") + dz, self.nz),
        )


def split3(value):
    high = value.astype(jnp.bfloat16).astype(jnp.float32)
    rest = value - high
    mid = rest.astype(jnp.bfloat16).astype(jnp.float32)
    return high, mid, rest - mid


def split2(value):
    high = value.astype(jnp.bfloat16)
    return high, (value - high.astype(jnp.float32)).astype(jnp.bfloat16)


def step_kernel(
    slots, blocks,
    pos_h, vel_h, fold_h, mass_h, charge_h, species_h, sigma_h, eps_h, tower_h, plate_h, counts_h, excl_h,
    mig_block_h, mig_dest_h,
    pos_out, vel_out, force_out, arrive,
    pos, vel, fold, mass, charge, species, sigma_s, eps_s, tower, plate, tower_v, plate_v, counts, excl,
    mig_block, mig_dest,
    half_b, moved_b, mass_b, dense, tow, kin, near0, near1, allowed, att_tab, towers, plates, right, right_b, left0, left1,
    made_a, made_b, tower_sum, plate_sum0, plate_sum1, out_t, out_p0, out_p1, land_t, land_p0, land_p1, going_m, going_v, come_m, come_v,
    force,
    t_flat, p_flat, local_sem,
    kn_s, kn_r, tow_s, tow_r, n0_s, n0_r, n1_s, n1_r, rt_s, rt_r, r0_s, r0_r, r1_s, r1_r, mm_s, mm_r, mv_s, mv_r,
):
    atoms = pos.shape[1]
    width = atoms // blocks
    pairs = tower.shape[1]
    words = excl.shape[2]
    part = width // HALVES
    pitch = 2 * blocks
    nx, ny, nz, cells = slots.nx, slots.ny, slots.nz, slots.cells
    lx, ly = float(nx), float(ny)
    lengths = (lx, ly, lx)
    f32 = jnp.float32
    bf16 = jnp.bfloat16
    near = (near0, near1)
    left = (left0, left1)
    plate_sum = (plate_sum0, plate_sum1)
    out_p = (out_p0, out_p1)
    land_p = (land_p0, land_p1)
    ratio = (ly / lx) ** 2
    shift_h = soft_core / (lx * lx)
    edge = (cutoff_sq + soft_core) / (lx * lx)
    scale = lx * lx / (cutoff_sq * cutoff_sq)

    barrier = pltpu.get_barrier_semaphore()
    for s in range(1, slots.count):
        pl.semaphore_signal(barrier, inc=1, device_id=slots.device(s), device_id_type=MESH)
    fetches = []
    for src, dst in (
        (pos_h, pos), (vel_h, vel), (fold_h, fold), (mass_h, mass), (charge_h, charge), (species_h, species),
        (sigma_h, sigma_s), (eps_h, eps_s), (excl_h, excl),
        (tower_h, tower_v), (plate_h, plate_v), (counts_h, counts), (mig_block_h, mig_block), (mig_dest_h, mig_dest),
    ):
        copy = pltpu.make_async_copy(src, dst, local_sem.at[len(fetches)])
        copy.start()
        fetches.append(copy)
    for copy in fetches[:8]:
        copy.wait()

    half = vel[...] + 0.5 * time_step * fold[...] * mass[...]
    moved = pos[...] + time_step * half
    row3 = lax.broadcasted_iota(jnp.int32, (3, atoms), 0)
    scaled = moved * jnp.where(row3 == 1, f32(1.0 / ly), f32(1.0 / lx))
    tower_charge = charge[...] * (coulomb_k * scale / lx)
    for b in range(blocks):
        at = slice(b * width, (b + 1) * width)
        tow[b, 0:3, :] = scaled[:, at]
        tow[b, 3:4, :] = tower_charge[:, at]
        for r in range(3):
            dense[r * blocks + b : r * blocks + b + 1, :] = scaled[r : r + 1, at]
        dense[3 * blocks + b : 3 * blocks + b + 1, :] = charge[:, at]
    which = species[...]
    sigma = jnp.zeros((1, blocks), f32)
    eps = jnp.zeros((1, blocks), f32)
    for k in range(sigma_s.shape[0]):
        sigma = jnp.where(which == k, sigma_s[k], sigma)
        eps = jnp.where(which == k, eps_s[k], eps)
    depth_row = jnp.sqrt(eps)
    tow[blocks] = jnp.zeros((4, width), f32)
    tow[blocks, 0:1, 0:blocks] = sigma
    tow[blocks, 1:2, 0:blocks] = depth_row
    kin[0:8, :] = jnp.zeros((8, width), f32)
    kin[0:1, 0:blocks] = sigma
    kin[1:2, 0:blocks] = depth_row
    low = lax.broadcasted_iota(jnp.int32, (blocks, width), 1) < part
    comp = [dense[r * blocks : (r + 1) * blocks, :] for r in range(4)]
    turned = [pltpu.roll(v, part, 1) for v in comp]
    near0[0:blocks, :] = jnp.where(low, comp[0], turned[1])
    near0[blocks : 2 * blocks, :] = jnp.where(low, comp[2], turned[3])
    near1[0:blocks, :] = jnp.where(low, turned[0], comp[1])
    near1[blocks : 2 * blocks, :] = jnp.where(low, turned[2], comp[3])

    pl.semaphore_wait(barrier, slots.count - 1)

    def send(src, dst, ss, rs, s):
        copy = pltpu.make_async_remote_copy(
            src_ref=src, dst_ref=dst, send_sem=ss, recv_sem=rs, device_id=slots.device(s), device_id_type=MESH
        )
        copy.start()
        return copy

    def send_cells(source, landing, ss, rs):
        copies = []
        for s in range(nz, slots.count):
            here, there = slots.cell_number(s), slots.cell_number(slots.opposite(s))
            copies.append(send(source(here), landing(there), ss.at[here], rs.at[there], s))
        return copies

    def rows_of(ref, size):
        return lambda c: ref.at[c * size : (c + 1) * size]

    named = send_cells(lambda c: kin.at[0:8], rows_of(kin, 8), kn_s, kn_r)
    above = []
    for s in range(1, nz):
        there = slots.opposite(s) * (blocks + 1)
        above.append(
            send(tow.at[0 : blocks + 1], tow.at[there : there + blocks + 1], tow_s.at[s], tow_r.at[slots.opposite(s)], s)
        )
    first = send_cells(lambda c: near0.at[0:pitch], rows_of(near0, pitch), n0_s, n0_r)
    second = send_cells(lambda c: near1.at[0:pitch], rows_of(near1, pitch), n1_s, n1_r)

    bit = jnp.left_shift(1, lax.broadcasted_iota(jnp.int32, (8, width), 0))
    term = lax.broadcasted_iota(jnp.int32, (TERMS, width), 0)
    early = jnp.where(term < 3, -1.0, 0.0)
    late = jnp.where((term >= 3) & (term < 6), -1.0, 0.0)
    shifted = jnp.where(term == 12, 0.5, early)
    ones = jnp.where((term >= 9) & (term < 13), 1.0, 0.0)
    plain = (early, late, shifted, early, jnp.zeros((TERMS, width), f32), shifted)
    for copy in fetches[8:]:
        copy.wait()

    def expand(k, carry):
        for w in range(words):
            hit = excl[0, k, w : w + 1, :] & bit
            allowed[pl.ds(pl.multiple_of(k * width + w * 8, 8), 8), :] = jnp.where(hit == 0, edge, -1.0)
        at = pl.ds(pl.multiple_of(k * TERMS, TERMS), TERMS)
        left0[at, :] = ones
        left1[at, :] = ones
        for g in range(6):
            at_g = pl.ds(pl.multiple_of((g * pairs + k) * TERMS, TERMS), TERMS)
            right[at_g, :] = plain[g]
        return carry

    lax.fori_loop(0, pairs, expand, 0)
    for c in range(HALVES):
        plate_sum[c][...] = jnp.zeros(plate_sum[c].shape, f32)
    half = vel[...] + 0.5 * time_step * fold[...] * mass[...]
    moved = pos[...] + time_step * half
    for b in range(blocks):
        at = slice(b * width, (b + 1) * width)
        half_b[b] = half[:, at]
        moved_b[b] = moved[:, at]
        mass_b[b] = mass[:, at]
    for q in range(mig_block.shape[1]):
        at = slice(q * width, (q + 1) * width)
        going_m[0:3, at] = moved_b[mig_block[0, q]]
        going_m[3:4, at] = jnp.full((1, width), mig_dest[0, q], jnp.int32).astype(f32)
    going_v[...] = jnp.zeros(going_v.shape, f32)
    come_m[0] = going_m[...]
    leavers = send_cells(lambda s: going_m, lambda s: come_m.at[s], mm_s, mm_r)
    block_of = lax.broadcasted_iota(jnp.int32, pos.shape, 1) // width
    gone = block_of == mig_block[0, 0]
    for q in range(1, mig_block.shape[1]):
        gone = gone | (block_of == mig_block[0, q])
    pos_out[...] = jnp.where(gone, 0.0, moved)

    my_layer = lax.axis_index("gz")
    t_all = tower_v[...]
    p_all = plate_v[...]
    live = lax.broadcasted_iota(jnp.int32, (1, pairs), 1) < counts[0]
    t_layer = t_all // blocks
    t_turn = t_layer - my_layer
    t_turn = jnp.where(t_turn < 0, t_turn + nz, t_turn)
    t_block = t_all - t_layer * blocks
    t_flat[...] = t_turn * (blocks + 1) + t_block
    t_row = jnp.where(live, t_turn * blocks + t_block, -1)
    p_cell = p_all // blocks
    p_number = jnp.zeros((1, pairs), jnp.int32)
    for o in range(9):
        number = slots.cell_number(slots.cell_slot(o // 3 - 1, o % 3 - 1))
        p_number = jnp.where(p_cell == o, number, p_number)
    p_block = p_all - p_cell * blocks
    p_flat[...] = p_number * pitch + p_block
    p_row = jnp.where(live, p_number * blocks + p_block, -1)
    tables = []
    for src, dst in ((t_flat, tower), (p_flat, plate)):
        tables.append(pltpu.make_async_copy(src, dst, local_sem.at[14 + len(tables)]))
        tables[-1].start()
    t_pick = jnp.where(
        lax.broadcasted_iota(jnp.int32, (nz * blocks, pairs), 0) == t_row, 1.0, 0.0
    ).astype(bf16)
    p_pick = jnp.where(
        lax.broadcasted_iota(jnp.int32, (cells * blocks, pairs), 0) == p_row, 1.0, 0.0
    ).astype(bf16)
    same = lax.broadcasted_iota(jnp.int32, (pairs, pairs), 0) == lax.broadcasted_iota(jnp.int32, (pairs, pairs), 1)
    t_col = jnp.sum(jnp.where(same, (t_turn * blocks + t_block).astype(f32), 0.0), axis=1, keepdims=True)
    p_col = jnp.sum(jnp.where(same, (p_number * blocks + p_block).astype(f32), 0.0), axis=1, keepdims=True)

    for copy in tables:
        copy.wait()
    for copy in above:
        copy.wait()

    lane_f = lax.broadcasted_iota(jnp.int32, (pairs, width), 1).astype(f32)

    def of_block(column, rows):
        found = jnp.zeros((pairs, width), f32)
        for s, row in enumerate(rows):
            found = found + jnp.where(lane_f == column - float(s * blocks), row, 0.0)
        return jnp.sum(found, axis=1, keepdims=True)

    sig_t = of_block(t_col, [tow[s * (blocks + 1) + blocks, 0:1, :] for s in range(nz)])
    dep_t = of_block(t_col, [tow[s * (blocks + 1) + blocks, 1:2, :] for s in range(nz)])
    def collect_towers(i, carry):
        for u in range(0, 16, 2):
            two = [tow[tower[0, i * 16 + u + v]] for v in range(2)]
            towers[pl.ds(pl.multiple_of(i * 64 + u * 4, 8), 8), :] = jnp.concatenate(two, axis=0)
        return carry

    lax.fori_loop(0, pairs // 16, collect_towers, 0)
    for r, groups in ((0, (0, 2)), (2, (1,)), (1, (3, 5)), (3, (4,))):
        terms = ((3, 4, 5), (6, 8), (7,)) if r == 3 else ((9,), (10,), (11,))
        for value, places in zip(split3(towers[pl.ds(r, pairs, stride=4), :]), terms):
            for t in places:
                for g in groups:
                    right[pl.ds(g * pairs * TERMS + t, pairs, stride=TERMS), :] = value
    def narrow(i, carry):
        for u in range(UNROLL):
            k = i * UNROLL + u
            row = pl.ds(pl.multiple_of(k * TERMS, TERMS), TERMS)
            for g in range(6):
                at = pl.ds(pl.multiple_of((g * pairs + k) * TERMS, TERMS), TERMS)
                right_b[row, g * width : (g + 1) * width] = right[at, :].astype(bf16)
        return carry

    lax.fori_loop(0, pairs // UNROLL, narrow, 0)
    for copy in named:
        copy.wait()
    sig_p = of_block(p_col, [kin[8 * c : 8 * c + 1, :] for c in range(cells)])
    dep_p = of_block(p_col, [kin[8 * c + 1 : 8 * c + 2, :] for c in range(cells)])
    sig = 0.5 * (sig_t + sig_p)
    sig2 = sig * sig
    sig6 = sig2 * sig2 * sig2
    depth = dep_t * dep_p
    att_tab[...] = jnp.broadcast_to((0.5 * lx**6) / sig6, (pairs, width))
    rep_col = (12.0 * scale / lx**12) * depth * sig6 * sig6
    rep_row = jnp.sum(jnp.where(same, rep_col, 0.0), axis=0, keepdims=True)
    charge_lanes = lax.broadcasted_iota(jnp.int32, (pairs, width), 1) >= part
    charge_scale = jnp.where(charge_lanes, 1.0 / rep_col, 1.0)

    def collect_plates(c):
        def body(i, carry):
            for u in range(16):
                p = plate[0, i * 16 + u]
                plates[i * 16 + u] = near[c][p]
                plates[pairs + i * 16 + u] = near[c][p + blocks]
            return carry

        lax.fori_loop(0, pairs // 16, body, 0)
        for r, terms in ((0, ((0,), (1,), (2,))), (1, ((3, 6, 7), (4, 8), (5,)))):
            rows = plates[r * pairs : (r + 1) * pairs, :]
            for value, places in zip(split3(rows * charge_scale if r else rows), terms):
                for t in places:
                    left[c][pl.ds(t, pairs, stride=TERMS), :] = value

    for copy in first:
        copy.wait()
    collect_plates(0)

    lane = lax.broadcasted_iota(jnp.int32, (8, pairs), 1)

    def prepare(k, c, made):
        at = pl.ds(pl.multiple_of(k * TERMS, TERMS), TERMS)
        a = left[c][at, :].T
        for i in range(2):
            made[:, 3 * i * width : (3 * i + 2) * width] = jnp.dot(
                a[i * part : (i + 1) * part].astype(bf16),
                right_b[at, 3 * i * width : (3 * i + 2) * width],
                preferred_element_type=f32,
            )

    def arithmetic(k, c, made):
        att = att_tab[pl.ds(k, 1), :]
        here = lane == k
        sums = [None, None, None]
        for w in range(part // 8):
            at = slice(w * 8, (w + 1) * 8)
            dx = made[at, 0:width] - jnp.floor(made[at, 0:width] + 0.5)
            dz = made[at, width : 2 * width]
            dy = made[at, 3 * width : 4 * width] - jnp.floor(made[at, 3 * width : 4 * width] + 0.5)
            h = (dx * dx + dz * dz) + (ratio * (dy * dy) + shift_h)
            q = lax.rsqrt(h)
            f = jnp.maximum(allowed[pl.ds(pl.multiple_of(k * width + (c * part + w * 8), 8), 8), :] - h, 0.0)
            s = q * q
            s3 = s * s * s
            fq = f * q
            g = fq * fq
            e = s3 * (s3 - att) + made[at, 4 * width : 5 * width] * q
            force_c = e * g
            parts = (force_c * dx, force_c * dy, force_c * dz)
            sums = [v if u is None else u + v for u, v in zip(sums, parts)]
            for r in range(3):
                total = jnp.broadcast_to(jnp.sum(parts[r], axis=1, keepdims=True), (8, pairs))
                pltpu.store(plate_sum[c].at[r * part + w * 8 : r * part + (w + 1) * 8, :], total, mask=here)
        for r in range(3):
            at = pl.ds(pl.multiple_of((r * pairs + k) * 8, 8), 8)
            tower_sum[at, :] = sums[r] if c == 0 else tower_sum[at, :] + sums[r]

    def run(c):
        for u in range(UNROLL):
            prepare(u, c, made_a.at[u])

        def step(i, carry):
            k = i * (GROUPS * UNROLL)
            for g in range(GROUPS):
                now, later = (made_a, made_b) if g % 2 == 0 else (made_b, made_a)
                for u in range(UNROLL):
                    ahead = k + (g + 1) * UNROLL + u
                    prepare(ahead if g + 1 < GROUPS else lax.rem(ahead, pairs), c, later.at[u])
                    arithmetic(k + g * UNROLL + u, c, now.at[u])
            return carry

        lax.fori_loop(0, pairs // (GROUPS * UNROLL), step, 0)
    def scatter(c):
        total = jnp.zeros((cells * blocks, 4 * part), f32)
        for piece in split2(plate_sum[c][...] * rep_row):
            total = total + lax.dot_general(p_pick, piece, (((1,), (1,)), ((), ())), preferred_element_type=f32)
        for s in range(cells):
            mine = total[s * blocks : (s + 1) * blocks]
            out_p[c][s, 0:blocks, :] = mine[:, 0:width]
            last = mine[:, width:]
            out_p[c][s, blocks:, :] = last[0 : blocks // 2] + pltpu.roll(last[blocks // 2 :], part, 1)
        return send_cells(lambda s: out_p[c].at[s], lambda s: land_p[c].at[s], (r0_s, r1_s)[c], (r0_r, r1_r)[c])

    run(0)
    for copy in second:
        copy.wait()
    collect_plates(1)
    returns = scatter(0)
    run(1)
    returns += scatter(1)
    for r in range(3):
        on_slot = tower_sum[pl.ds(r * pairs * 8, pairs, stride=8), :]
        for j in range(1, 8):
            on_slot = on_slot + tower_sum[pl.ds(r * pairs * 8 + j, pairs, stride=8), :]
        total = jnp.zeros((nz * blocks, width), f32)
        for piece in split2(on_slot * rep_col):
            total = total + jnp.dot(t_pick, piece, preferred_element_type=f32)
        for s in range(nz):
            out_t[s, :, r * width : (r + 1) * width] = total[s * blocks : (s + 1) * blocks]
    for s in range(1, nz):
        there = slots.opposite(s)
        returns.append(send(out_t.at[s], land_t.at[there], rt_s.at[s], rt_r.at[there], s))
    for copy in returns[HALVES * (cells - 1) :]:
        copy.wait()
    on_tower = out_t[0]
    for s in range(1, nz):
        on_tower = on_tower + land_t[s]
    back = []
    for c in range(HALVES):
        for copy in returns[c * (cells - 1) : (c + 1) * (cells - 1)]:
            copy.wait()
        total = out_p[c][0]
        for s in range(1, cells):
            total = total + land_p[c][s]
        back.append(total)
    (a0, a1), (z0, z1) = [v[0:blocks] for v in back], [v[blocks:] for v in back]
    low_z = low[0 : blocks // 2]
    on_plate = (
        jnp.where(low, a0, pltpu.roll(a1, part, 1)),
        jnp.where(low, pltpu.roll(a0, part, 1), a1),
        jnp.concatenate(
            [jnp.where(low_z, z0, pltpu.roll(z1, part, 1)), jnp.where(low_z, pltpu.roll(z0, part, 1), z1)], axis=0
        ),
    )
    for r in range(3):
        force[r] = (on_tower[:, r * width : (r + 1) * width] - on_plate[r]) * lengths[r]
    for q in range(mig_block.shape[1]):
        at = slice(q * width, (q + 1) * width)
        block = mig_block[0, q]
        kick = 0.5 * time_step * mass_b[block]
        old = half_b[block]
        for r in range(3):
            going_v[r : r + 1, at] = old[r : r + 1] + kick * force[r, block][None, :]
    come_v[0] = going_v[...]
    last_hop = send_cells(lambda s: going_v, lambda s: come_v.at[s], mv_s, mv_r)
    for r in range(3):
        for b in range(blocks):
            force_out[r : r + 1, b * width : (b + 1) * width] = force[r, b : b + 1]
    half = vel[...] + 0.5 * time_step * fold[...] * mass[...]
    block_of = lax.broadcasted_iota(jnp.int32, pos.shape, 1) // width
    gone = block_of == mig_block[0, 0]
    for q in range(1, mig_block.shape[1]):
        gone = gone | (block_of == mig_block[0, q])
    vel_out[...] = jnp.where(gone, 0.0, half + 0.5 * time_step * force_out[...] * mass[...])
    for copy in leavers:
        copy.wait()
    wanted = []
    for i, (a, b) in enumerate(source_offsets):
        cell = slots.cell_number(slots.cell_slot(a, b))
        wanted.append((cell, come_m[cell, 3:4, :] == float((1 - a) * 3 + (1 - b))))
        for r in range(3):
            arrive[r, 0, i : i + 1, :] = jnp.where(wanted[i][1], come_m[cell, r : r + 1, :], 0.0)
    for copy in last_hop:
        copy.wait()
    for i, (cell, chosen) in enumerate(wanted):
        for r in range(3):
            arrive[3 + r, 0, i : i + 1, :] = jnp.where(chosen, come_v[cell, r : r + 1, :], 0.0)


def output_kernel(*refs):
    sem = refs[-1]
    copies = [pltpu.make_async_copy(refs[i], refs[4 + i], sem.at[i]) for i in range(4)]
    for copy in copies:
        copy.start()
    for copy in copies:
        copy.wait()


def local(
    slots, positions, velocities, forces_old, inv_mass, charges, block_species, sigma_table, epsilon_table,
    tower_index, plate_index, tile_counts, exclusions, mig_block, mig_dest,
):
    atoms = positions.shape[1]
    blocks = block_species.shape[0]
    width = atoms // blocks
    nz, cells = slots.nz, slots.cells
    pairs = tower_index.shape[1]
    leaving = mig_block.shape[1]
    kinds = sigma_table.shape[0]
    part = width // HALVES
    pitch = 2 * blocks
    hbm = pl.BlockSpec(memory_space=pltpu.HBM)
    vmem = pl.BlockSpec(memory_space=pltpu.VMEM)
    mass = inv_mass[None, :]
    f32, i32 = jnp.float32, jnp.int32

    def sems(n):
        return pltpu.SemaphoreType.DMA((n,))

    def v(*shape):
        return pltpu.VMEM(shape, f32)

    rows = jax.ShapeDtypeStruct((3, atoms), f32)
    arrive = jax.ShapeDtypeStruct((6, 1, len(source_offsets), leaving * width), f32)
    held = tuple(pltpu.VMEM(a.shape, f32) for a in (rows, rows, rows, arrive))
    made = pl.pallas_call(
        functools.partial(step_kernel, slots, blocks),
        out_shape=held,
        in_specs=[hbm] * 14,
        out_specs=(vmem,) * 4,
        scratch_shapes=[
            v(3, atoms), v(3, atoms), v(3, atoms), v(1, atoms), v(1, atoms), pltpu.VMEM((1, blocks), i32),
            pltpu.SMEM((kinds,), f32), pltpu.SMEM((kinds,), f32),
            pltpu.SMEM((1, pairs), i32), pltpu.SMEM((1, pairs), i32),
            pltpu.VMEM((1, pairs), i32), pltpu.VMEM((1, pairs), i32),
            pltpu.SMEM((1,), i32), pltpu.VMEM(exclusions.shape, i32),
            pltpu.SMEM((1, leaving), i32), pltpu.SMEM((1, leaving), i32),
            v(blocks, 3, width), v(blocks, 3, width), v(blocks, 1, width), v(4 * blocks, width), v(nz * (blocks + 1), 4, width),
            v(8 * cells, width), v(cells * pitch, width), v(cells * pitch, width),
            v(pairs * width, width), v(pairs, width), v(4 * pairs, width), v(2 * pairs, width),
            v(6 * pairs * TERMS, width), pltpu.VMEM((pairs * TERMS, 6 * width), jnp.bfloat16), v(pairs * TERMS, width), v(pairs * TERMS, width),
            v(UNROLL, part, 6 * width), v(UNROLL, part, 6 * width), v(3 * 8 * pairs, width), v(4 * part, pairs), v(4 * part, pairs),
            v(nz, blocks, 3 * width), v(cells, blocks + blocks // 2, width), v(cells, blocks + blocks // 2, width),
            v(nz, blocks, 3 * width), v(cells, blocks + blocks // 2, width), v(cells, blocks + blocks // 2, width),
            v(4, leaving * width), v(4, leaving * width), v(cells, 4, leaving * width), v(cells, 4, leaving * width),
            v(3, blocks, width),
            pltpu.VMEM((1, pairs), i32), pltpu.VMEM((1, pairs), i32), sems(16),
        ]
        + [sems(cells)] * 2 + [sems(nz)] * 2 + [sems(cells)] * 4 + [sems(nz)] * 2 + [sems(cells)] * 8,
        compiler_params=pltpu.CompilerParams(
            collective_id=0, has_side_effects=True, vmem_limit_bytes=60 * 1024 * 1024
        ),
        name="membrane_step",
    )(
        positions, velocities, forces_old, mass, charges[None, :], block_species[None, :], sigma_table,
        epsilon_table, tower_index, plate_index, tile_counts, exclusions, mig_block, mig_dest,
    )
    return pl.pallas_call(
        output_kernel,
        out_shape=(rows, rows, rows, arrive),
        in_specs=[vmem] * 4,
        out_specs=(hbm,) * 4,
        scratch_shapes=[sems(4)],
        compiler_params=pltpu.CompilerParams(vmem_limit_bytes=1024 * 1024),
        name="outputs",
    )(*made)


def solution(mesh):
    cells = ("gx", "gy", "gz")
    slots = Slots(mesh.shape["gx"], mesh.shape["gy"], mesh.shape["gz"])
    row = P(None, cells)
    flat = P(cells)
    pair = P(cells, None)
    in_specs = (
        row, row, row, flat, flat, flat, P(), P(), pair, pair, flat, P(cells, None, None, None), pair, pair,
    )
    out_specs = (row, row, row, P(None, cells, None, None))
    return jax.shard_map(
        functools.partial(local, slots), mesh=mesh, in_specs=in_specs, out_specs=out_specs, check_vma=False
    )
```
